256 devices in a mesh: rows: 16 (over z, x_lo), cols: 16 (over y, x_hi, core).
Axes of the slice: x: 4 (x_hi: 2, x_lo: 2; x = x_hi * 2 + x_lo), y: 4, z: 8, core: 2. Of those that a mesh axis runs over, the one named last changes fastest.
Arguments:
- pixels: bfloat16 [256, 512, 180], P('rows', 'cols'), may hold values from -32 to 32
- shift_prenorm: float32 [180], replicated, may hold values from 0.5 to 4, as said below
- shift_inputs: bfloat16 [180, 540], replicated, may hold values from -0.4375 to 0.4375
- shift_table: float32 [6, 31, 31], replicated, may hold values from -4 to 4
- shift_output: bfloat16 [180, 180], replicated, may hold values from -0.4375 to 0.4375
- shift_postnorm: float32 [180], replicated, may hold values from 0.5 to 1.5
- shift_widen: bfloat16 [180, 360], replicated, may hold values from -0.4375 to 0.4375
- shift_narrow: bfloat16 [360, 180], replicated, may hold values from -0.3125 to 0.3125
- cross_prenorm: float32 [180], replicated, may hold values from 0.5 to 4, as said below
- cross_query: bfloat16 [180, 180], replicated, may hold values from -0.4375 to 0.4375
- cross_keyval: bfloat16 [180, 360], replicated, may hold values from -0.4375 to 0.4375
- cross_table: float32 [6, 39, 39], replicated, may hold values from -4 to 4
- cross_output: bfloat16 [180, 180], replicated, may hold values from -0.4375 to 0.4375
- cross_postnorm: float32 [180], replicated, may hold values from 0.5 to 1.5
- cross_widen: bfloat16 [180, 360], replicated, may hold values from -0.4375 to 0.4375
- cross_narrow: bfloat16 [360, 180], replicated, may hold values from -0.3125 to 0.3125
Outputs:
- refined: bfloat16 [256, 512, 180], P('rows', 'cols')
The draws below stay inside these ranges and needn't reach their ends.
Inputs may be any that keep to these rules, and one draw needn't show every extreme that they name: `shift_prenorm`: positive. `cross_prenorm`: positive.
All inputs are finite; a program needn't handle non-finite values.
Results may differ from the reference program's by a relative error of at most 0.017.
Values may be sent and summed in bfloat16 or wider, within the bound.
No kernel may reach another device: no remote copies, remote signals or barrier semaphores. Data moves between devices by JAX's collectives and lax.ppermute only.
A program may use at most 128 MiB of HBM per device.

```python
import math
import jax
import jax.numpy as jnp
from jax import lax

C = 180
HEADS = 6
MLP = 360
WIN = 16
HEAD_DIM = 30
SHIFT = 8
PAD = 4
OWIN = 24
RB = 31
OB = 39
NY = 256
NX = 512


def draw_pixels(key, part):
    key = jax.random.fold_in(key, 7)
    key_pixel, key_channel, key_base = jax.random.split(key, 3)
    low = math.log(0.3)
    high = math.log(3.0)
    pixel_scale = jnp.exp(jax.random.uniform(key_pixel, (NY, NX, 1), jnp.float32, low, high))
    channel_scale = jnp.exp(jax.random.uniform(key_channel, (1, 1, C), jnp.float32, low, high))
    base = jnp.clip(jax.random.normal(key_base, (NY, NX, C), jnp.float32), -3.0, 3.0)
    return (base * pixel_scale * channel_scale).astype(jnp.bfloat16)


def draw_shift_prenorm(key, part):
    key = jax.random.fold_in(key, 11)
    return jax.random.uniform(key, (C,), jnp.float32, 0.6, 1.4)


def draw_cross_prenorm(key, part):
    key = jax.random.fold_in(key, 12)
    return jax.random.uniform(key, (C,), jnp.float32, 0.6, 1.4)


def normal_values(key, dims, scale, bound, held_as=jnp.bfloat16):
    entries = jax.random.normal(key, dims, jnp.float32) * scale
    return jnp.minimum(jnp.maximum(entries, -bound), bound).astype(held_as)


def setup_inputs(seed: int = 0) -> dict:
    arg_keys = jax.random.split(jax.random.key(seed), 17)
    return {
        "pixels": draw_pixels(jax.random.fold_in(arg_keys[16], 71), 0),
        "shift_prenorm": draw_shift_prenorm(jax.random.fold_in(arg_keys[16], 71), 0),
        "shift_inputs": normal_values(arg_keys[2], (C, 3 * C), C ** -0.5, 0.4375),
        "shift_table": normal_values(arg_keys[3], (HEADS, RB, RB), 1.0, 4.0, jnp.float32),
        "shift_output": normal_values(arg_keys[4], (C, C), C ** -0.5, 0.4375),
        "shift_postnorm": jnp.clip(1.0 + 0.1 * jax.random.normal(arg_keys[5], (C,), jnp.float32), 0.5, 1.5),
        "shift_widen": normal_values(arg_keys[6], (C, MLP), C ** -0.5, 0.4375),
        "shift_narrow": normal_values(arg_keys[7], (MLP, C), MLP ** -0.5, 0.3125),
        "cross_prenorm": draw_cross_prenorm(jax.random.fold_in(arg_keys[16], 71), 0),
        "cross_query": normal_values(arg_keys[9], (C, C), C ** -0.5, 0.4375),
        "cross_keyval": normal_values(arg_keys[10], (C, 2 * C), C ** -0.5, 0.4375),
        "cross_table": normal_values(arg_keys[11], (HEADS, OB, OB), 1.0, 4.0, jnp.float32),
        "cross_output": normal_values(arg_keys[12], (C, C), C ** -0.5, 0.4375),
        "cross_postnorm": jnp.clip(1.0 + 0.1 * jax.random.normal(arg_keys[13], (C,), jnp.float32), 0.5, 1.5),
        "cross_widen": normal_values(arg_keys[14], (C, MLP), C ** -0.5, 0.4375),
        "cross_narrow": normal_values(arg_keys[15], (MLP, C), MLP ** -0.5, 0.3125),
    }


EPS = 1e-05
NEG = -1e+30

def layer_norm(values, gain):
    values = values.astype(jnp.float32)
    center = values - lax.optimization_barrier(jnp.mean(values, axis=-1, keepdims=True))
    spread = lax.optimization_barrier(jnp.mean(center * center, axis=-1, keepdims=True))
    return center * lax.rsqrt(spread + EPS) * gain.astype(jnp.float32)

def project(inputs, weight):
    shape = inputs.shape
    result = jnp.dot(inputs.reshape(-1, shape[-1]), weight, preferred_element_type=jnp.float32)
    return result.reshape(shape[:-1] + (weight.shape[1],))

def feed_forward(residual, gain, widen, narrow):
    normed = layer_norm(residual, gain).astype(jnp.bfloat16)
    hidden = jax.nn.gelu(project(normed, widen), approximate=False).astype(jnp.bfloat16)
    return (residual + project(hidden, narrow)).astype(jnp.bfloat16)

def to_windows(grid, window):
    rows_count, cols_count, depth = grid.shape
    grid = grid.reshape(rows_count // window, window, cols_count // window, window, depth)
    return grid.transpose(0, 2, 1, 3, 4).reshape(rows_count // window, cols_count // window, window * window, depth)

def from_windows(blocks, window):
    band_count, cols_count, _, depth = blocks.shape
    blocks = blocks.reshape(band_count, cols_count, window, window, depth)
    return blocks.transpose(0, 2, 1, 3, 4).reshape(band_count * window, cols_count * window, depth)

def split_heads(grid):
    blocks = to_windows(grid, WIN)
    return blocks.reshape(blocks.shape[:3] + (HEADS, HEAD_DIM))

def key_windows(strip):
    span = strip.shape[1]
    depth = strip.shape[2]
    count = (span - 2 * PAD) // WIN
    stride = WIN // PAD
    blocks = strip.reshape(OWIN, span // PAD, PAD, depth)
    parts = [blocks[:, step:step + stride * (count - 1) + 1:stride] for step in range(OWIN // PAD)]
    stacked = jnp.stack(parts, axis=2)
    return stacked.transpose(1, 0, 2, 3, 4).reshape(count, OWIN * OWIN, depth)

def expand_table(table, query_side, key_side, key_first):
    query_pos = jnp.arange(query_side, dtype=jnp.int32)[:, None]
    key_pos = jnp.arange(key_side, dtype=jnp.int32)[None, :]
    if key_first:
        offset = key_pos - query_pos + query_side - 1
    else:
        offset = query_pos - key_pos + query_side - 1
    full = table[:, offset[:, None, :, None], offset[None, :, None, :]]
    return full.reshape(table.shape[0], query_side * query_side, key_side * key_side).astype(jnp.float32)

def region_labels(glob_rows, glob_cols, total_rows, total_cols):

    def side(coord, total):
        kind = jnp.where(coord < SHIFT, 2, jnp.where(coord >= total - SHIFT, 1, 0))
        inside = (coord >= 0) & (coord < total)
        return (kind, inside)
    row_kind, row_inside = side(glob_rows, total_rows)
    col_kind, col_inside = side(glob_cols, total_cols)
    label = 3 * row_kind[:, None] + col_kind[None, :]
    return jnp.where(row_inside[:, None] & col_inside[None, :], label, -1).astype(jnp.int32)

def attend(queries, key_set, value_set, bias, allowed):
    count, tokens = (queries.shape[0], queries.shape[1])

    def one_head(pieces):
        head_query, head_key, head_value, head_bias = pieces
        scores = jnp.einsum('wqd,wkd->wqk', head_query.astype(jnp.float32), head_key.astype(jnp.float32)) + head_bias[None]
        if allowed is not None:
            scores = jnp.where(allowed, scores, NEG)
        peak = lax.optimization_barrier(jnp.max(scores, axis=-1, keepdims=True))
        expo = jnp.exp(scores - peak)
        shares = (expo / lax.optimization_barrier(jnp.sum(expo, axis=-1, keepdims=True))).astype(jnp.bfloat16)
        mixed = jnp.einsum('wqk,wkd->wqd', shares.astype(jnp.float32), head_value.astype(jnp.float32))
        return mixed.astype(jnp.bfloat16)
    mixed = lax.map(one_head, (jnp.moveaxis(queries, 2, 0), jnp.moveaxis(key_set, 2, 0), jnp.moveaxis(value_set, 2, 0), bias))
    return jnp.moveaxis(mixed, 0, 2).reshape(count, tokens, -1)

def window_attention(region, labels, inputs_weight, bias):
    mixed = project(region, inputs_weight)
    queries = split_heads((mixed[..., :C] * HEAD_DIM ** (-0.5)).astype(jnp.bfloat16))
    key_set = split_heads(mixed[..., C:2 * C].astype(jnp.bfloat16))
    value_set = split_heads(mixed[..., 2 * C:].astype(jnp.bfloat16))
    label_set = to_windows(labels[:, :, None], WIN)[..., 0]

    def one_band(pieces):
        band_query, band_key, band_value, band_label = pieces
        allowed = band_label[:, :, None] == band_label[:, None, :]
        return attend(band_query, band_key, band_value, bias, allowed)
    out = lax.map(one_band, (queries, key_set, value_set, label_set))
    return from_windows(out, WIN)

def cross_attention(queries, region, bias):
    query_bands = split_heads(queries)
    band_ids = jnp.arange(query_bands.shape[0], dtype=jnp.int32)

    def one_band(pieces):
        band_index, band_query = pieces
        strip = lax.dynamic_slice_in_dim(region, (band_index * WIN).astype(jnp.int32), OWIN, 0)
        pairs = key_windows(strip)
        key_set = pairs[..., :C].reshape(pairs.shape[:2] + (HEADS, HEAD_DIM))
        value_set = pairs[..., C:].reshape(pairs.shape[:2] + (HEADS, HEAD_DIM))
        return attend(band_query, key_set, value_set, bias, None)
    out = lax.map(one_band, (band_ids, query_bands))
    return from_windows(out, WIN)

def reference(pixels, shift_prenorm, shift_inputs, shift_table, shift_output, shift_postnorm, shift_widen, shift_narrow, cross_prenorm, cross_query, cross_keyval, cross_table, cross_output, cross_postnorm, cross_widen, cross_narrow):
    normed = layer_norm(pixels, shift_prenorm).astype(jnp.bfloat16)
    rolled = jnp.roll(normed, (-SHIFT, -SHIFT), (0, 1))
    glob_rows = (jnp.arange(NY, dtype=jnp.int32) + SHIFT) % NY
    glob_cols = (jnp.arange(NX, dtype=jnp.int32) + SHIFT) % NX
    labels = region_labels(glob_rows, glob_cols, NY, NX)
    shift_bias = expand_table(shift_table, WIN, WIN, False)
    mixed = window_attention(rolled, labels, shift_inputs, shift_bias)
    mixed = jnp.roll(mixed, (SHIFT, SHIFT), (0, 1))
    residual = pixels.astype(jnp.float32) + project(mixed, shift_output)
    block_out = feed_forward(residual, shift_postnorm, shift_widen, shift_narrow)
    cross_normed = layer_norm(block_out, cross_prenorm).astype(jnp.bfloat16)
    queries = (project(cross_normed, cross_query) * HEAD_DIM ** (-0.5)).astype(jnp.bfloat16)
    pairs = project(cross_normed, cross_keyval).astype(jnp.bfloat16)
    region = jnp.pad(pairs, ((PAD, PAD), (PAD, PAD), (0, 0)))
    cross_bias = expand_table(cross_table, WIN, OWIN, True)
    cross_mixed = cross_attention(queries, region, cross_bias)
    second = block_out.astype(jnp.float32) + project(cross_mixed, cross_output)
    return feed_forward(second, cross_postnorm, cross_widen, cross_narrow)
```

```python
import jax
import jax.numpy as jnp
from jax import lax
from jax.experimental import pallas as pl
from jax.experimental.pallas import tpu as pltpu
from jax.sharding import PartitionSpec as P

C = 180
HEADS = 6
HEAD_DIM = 30
WIN = 16
SHIFT = 8
PAD = 4
OWIN = 24
EPS = 1e-05
LOG2E = 1.4426950408889634
SCALE = HEAD_DIM ** (-0.5) * LOG2E
LOW = -1e30
FLAG = 180
ONE = 181
KEYS = 640
BF = jnp.bfloat16
F32 = jnp.float32


def mm(a, b, dims=((1,), (0,)), precision=None):
    return lax.dot_general(a, b, (dims, ((), ())), preferred_element_type=F32, precision=precision)


NT = ((1,), (1,))


def lanes(shape):
    return lax.broadcasted_iota(jnp.int32, shape, len(shape) - 1)


def rows_of(shape):
    return lax.broadcasted_iota(jnp.int32, shape, len(shape) - 2)


def tables_kernel(
    st_ref, ct_ref, wi_ref, wo_ref, ww_ref, wn_ref, cq_ref, ckv_ref, co_ref, cw_ref, cn_ref,
    b1_ref, b2_ref, w1_ref, o1_ref, ww1_ref, wn1_ref, w2_ref, o2_ref, ww2_ref, wn2_ref,
    e1_ref, e2_ref,
):
    r = rows_of((256, 768))
    c = lanes((256, 768))
    base = jnp.where((r == FLAG) & (c == 256 + FLAG), LOW, 0.0)
    base = jnp.where((r == ONE) & (c == FLAG), 1.0, base)
    base = jnp.where((r == ONE) & (c >= 512 + 180) & (c < 512 + 186), 1.0, base)
    w1_ref[...] = base.astype(BF)
    w2_ref[...] = jnp.where(r == ONE, base, 0.0).astype(BF)
    w1_ref[:C, :C] = wi_ref[:, :C]
    w1_ref[:C, 256 : 256 + C] = wi_ref[:, C : 2 * C]
    w1_ref[:C, 512 : 512 + C] = wi_ref[:, 2 * C :]
    w2_ref[:C, :C] = cq_ref[...]
    w2_ref[:C, 256 : 256 + C] = ckv_ref[:, :C]
    w2_ref[:C, 512 : 512 + C] = ckv_ref[:, C:]
    for dst, src in ((o1_ref, wo_ref), (ww1_ref, ww_ref), (wn1_ref, wn_ref), (o2_ref, co_ref), (ww2_ref, cw_ref), (wn2_ref, cn_ref)):
        dst[...] = jnp.zeros(dst.shape, BF)
        dst[: src.shape[0], : src.shape[1]] = src[...]
    hi = lax.Precision.HIGHEST
    lane = lanes((32, 512))
    pick = jnp.where(lane // 16 == rows_of((32, 512)), LOG2E, 0.0)
    y = mm(st_ref[...], pick, precision=hi)
    amount = 15 - lanes((192, 512)) % 16
    for bit in (8, 4, 2, 1):
        y = jnp.where((amount & bit) != 0, pltpu.roll(y, 192 - bit, 0), y)
    e1_ref[...] = y
    for h in range(HEADS):
        for qy in range(WIN):
            b1_ref[h, qy * 16 : qy * 16 + 16, :] = e1_ref[h * 32 : h * 32 + 16, (15 - qy) * 16 : (15 - qy) * 16 + 256]
    lane = lanes((40, 1024))
    row = rows_of((40, 1024))
    pick = jnp.where((lane >= row * 24) & (lane < row * 24 + 24), LOG2E, 0.0)
    y = mm(ct_ref[...], pick, precision=hi)
    lane1 = lanes((1, 1024)).astype(F32)
    kx = lane1 - 24.0 * jnp.floor((lane1 + 0.5) * (1.0 / 24.0))
    amount = jnp.broadcast_to(23 - kx.astype(jnp.int32), (240, 1024))
    for bit in (16, 8, 4, 2, 1):
        y = jnp.where((amount & bit) != 0, pltpu.roll(y, 240 - bit, 0), y)
    e2_ref[...] = y
    for h in range(HEADS):
        b2_ref[h, :, 512:640] = jnp.zeros((256, 128), F32)
        for qy in range(WIN):
            b2_ref[h, qy * 16 : qy * 16 + 16, :576] = e2_ref[h * 40 : h * 40 + 16, (15 - qy) * 24 : (15 - qy) * 24 + 576]


def norm(x, gain, real):
    x0 = x[:, :128]
    x1 = jnp.where(real, x[:, 128:], 0.0)
    mean = jnp.sum(x0 + x1, axis=-1, keepdims=True) * (1.0 / C)
    c0 = x0 - mean
    c1 = jnp.where(real, x1 - mean, 0.0)
    spread = jnp.sum(c0 * c0 + c1 * c1, axis=-1, keepdims=True) * (1.0 / C)
    inv = lax.rsqrt(spread + EPS)
    return c0 * inv * gain[:, :128], c1 * inv * gain[:, 128:]


def gelu(x):
    return 0.5 * x * (1.0 + lax.erf(x * 0.7071067811865476))


def mlp(res, gain, real, widen, narrow):
    n0, n1 = norm(res, gain, real)
    normed = jnp.concatenate([n0, n1], axis=1).astype(BF)
    hidden = gelu(mm(normed, widen)).astype(BF)
    return res + mm(hidden, narrow, NT)


def head_masks():
    lane = lanes((1, 256))
    q, v = [], []
    for h in range(HEADS):
        own = (lane >= 30 * h) & (lane < 30 * h + 30)
        q.append(jnp.where(own | (lane == FLAG), 1.0, 0.0).astype(BF))
        v.append(jnp.where(own | (lane == C + h), 1.0, 0.0).astype(BF))
    return q, v


def spread_sums(mixed, expand):
    m1 = mixed[:, 128:]
    lane = lanes(m1.shape)
    r1 = jnp.where((lane >= C - 128) & (lane < C + HEADS - 128), 1.0 / m1, 0.0)
    top = r1.astype(BF)
    rest = (r1 - top.astype(F32)).astype(BF)
    return mixed * mm(jnp.concatenate([top, rest], axis=1), expand)


def attend(queries, keys, qmask, bias_of, p_ref, vall_ref, expand):
    width = keys.shape[0]
    for h in range(HEADS):
        scores = mm(queries * qmask[h], keys, NT) + bias_of(h)
        peak = jnp.max(scores, axis=-1, keepdims=True)
        p_ref[:, h * width : (h + 1) * width] = jnp.exp2(scores - peak).astype(BF)
    return spread_sums(mm(p_ref[...], vall_ref[...]), expand)


def main_kernel(
    pos_ref, cen_ref, ra_ref, rb_ref, ca_ref, cb_ref, gain_ref,
    b1_ref, b2_ref, w1_ref, o1_ref, ww1_ref, wn1_ref, w2_ref, o2_ref, ww2_ref, wn2_ref,
    out_ref,
    x_ref, p1_ref, v1_ref, bo_ref, a3_ref, kv_ref, p2_ref, v2_ref,
):
    row, col, last_row, last_col = pos_ref[0], pos_ref[1], pos_ref[2], pos_ref[3]
    real = lanes((1, 128)) < C - 128
    lane1 = lanes((1, 128))
    one1 = jnp.where(lane1 == ONE - 128, 1.0, 0.0)
    qmask, vmask = head_masks()
    er = rows_of((256, 256))
    ec = lanes((256, 256))
    hd = jnp.where(er >= 128, er - 128, er) - (C - 128)
    expand = jnp.where((hd >= 0) & (hd < HEADS) & (ec >= hd * 30) & (ec < hd * 30 + 30), 1.0, 0.0).astype(BF)

    def put(window, y0, x0, piece, flag):
        ny, nx = piece.shape[0], piece.shape[1]
        x_ref[window, y0 : y0 + ny, x0 : x0 + nx, 128:] = jnp.broadcast_to(
            jnp.where(lane1 == FLAG - 128, flag, one1), (ny, nx, 128)
        )
        x_ref[window, y0 : y0 + ny, x0 : x0 + nx, :C] = piece.astype(F32)

    row_odd = lax.rem(row, 2) == 1
    col_odd = lax.rem(col, 2) == 1
    out_top = jnp.where(row == 0, 1.0, 0.0)
    out_bot = jnp.where(row == last_row, 1.0, 0.0)
    out_lef = jnp.where(col == 0, 1.0, 0.0)
    out_rig = jnp.where(col == last_col, 1.0, 0.0)
    top = jnp.where(row_odd, ra_ref[...], rb_ref[...])
    bot = jnp.where(row_odd, rb_ref[...], ra_ref[...])
    lef = jnp.where(col_odd, ca_ref[...], cb_ref[...])
    rig = jnp.where(col_odd, cb_ref[...], ca_ref[...])
    both = jnp.maximum
    put(0, 0, 0, lef[:8], both(out_top, out_lef))
    put(0, 0, 8, top[:, :8], out_top)
    put(0, 8, 0, lef[8:16], out_lef)
    put(0, 8, 8, cen_ref[:8, :8], 0.0)
    put(1, 0, 0, top[:, 8:24], out_top)
    put(1, 8, 0, cen_ref[:8, 8:24], 0.0)
    put(2, 0, 0, top[:, 24:], out_top)
    put(2, 0, 8, rig[:8], both(out_top, out_rig))
    put(2, 8, 0, cen_ref[:8, 24:], 0.0)
    put(2, 8, 8, rig[8:16], out_rig)
    put(3, 0, 0, lef[16:24], out_lef)
    put(3, 0, 8, cen_ref[8:, :8], 0.0)
    put(3, 8, 0, lef[24:], both(out_bot, out_lef))
    put(3, 8, 8, bot[:, :8], out_bot)
    put(4, 0, 0, cen_ref[8:, 8:24], 0.0)
    put(4, 8, 0, bot[:, 8:24], out_bot)
    put(5, 0, 0, cen_ref[8:, 24:], 0.0)
    put(5, 0, 8, rig[16:24], out_rig)
    put(5, 8, 0, bot[:, 24:], out_bot)
    put(5, 8, 8, rig[24:], both(out_bot, out_rig))

    gains = [gain_ref[i : i + 1, :] for i in range(4)]

    def shifted(j, carry):
        for i in range(2):
            x = x_ref[i * 3 + j].reshape(256, 256)
            n0, n1 = norm(x, gains[0], real)
            n1 = jnp.where(real, n1, x[:, 128:])
            normed = jnp.concatenate([n0, n1], axis=1).astype(BF)
            first = 64 * (1 - i)
            q = (mm(normed[first : first + 192], w1_ref[:, :256]) * SCALE).astype(BF)
            kv = mm(normed, w1_ref[:, 256:]).astype(BF)
            for h in range(HEADS):
                v1_ref[i, h * 256 : (h + 1) * 256, :] = kv[:, 256:] * vmask[h]
            mixed = attend(
                q, kv[:, :256], qmask, lambda h: b1_ref[h, first : first + 192, :], p1_ref.at[i], v1_ref.at[i], expand
            )
            res = x[first : first + 192] + mm(mixed.astype(BF), o1_ref[...])
            out = mlp(res, gains[1], real, ww1_ref[...], wn1_ref[...])
            bo_ref[i * 12 : i * 12 + 12, pl.ds(pl.multiple_of(j * 16, 16), 16), :] = (
                out.astype(BF).astype(F32).reshape(12, 16, 256)
            )
        return carry

    lax.fori_loop(0, 3, shifted, 0)

    n0, n1 = norm(bo_ref[...].reshape(24 * 48, 256), gains[2], real)
    a3_ref[:, :, :128] = n0.reshape(24, 48, 128)
    a3_ref[:, :, 128:] = (n1 + one1).reshape(24, 48, 128)
    base = jnp.where(lanes((1, 1, 256)) == ONE, 1.0, 0.0)

    @pl.when(row == 0)
    def _():
        a3_ref[:4] = jnp.broadcast_to(base, (4, 48, 256))

    @pl.when(row == last_row)
    def _():
        a3_ref[20:] = jnp.broadcast_to(base, (4, 48, 256))

    @pl.when(col == 0)
    def _():
        a3_ref[:, :8] = jnp.broadcast_to(base, (24, 8, 256))

    @pl.when(col == last_col)
    def _():
        a3_ref[:, 40:] = jnp.broadcast_to(base, (24, 8, 256))

    kv = mm(a3_ref[:, 4:44, :].reshape(960, 256).astype(BF), w2_ref[:, 256:])
    kv_ref[...] = kv.reshape(24, 40, 512)
    pad = jnp.where(lanes((64, 256)) == FLAG, LOW, 0.0).astype(BF)
    zero = jnp.zeros((64, 256), BF)

    for j in range(2):
        q = a3_ref[4:20, 8 + 16 * j : 24 + 16 * j, :].reshape(256, 256).astype(BF)
        q = (mm(q, w2_ref[:, :256]) * SCALE).astype(BF)
        keys = kv_ref[:, 16 * j : 16 * j + 24, :256].reshape(576, 256).astype(BF)
        keys = jnp.concatenate([keys, pad], axis=0)
        values = kv_ref[:, 16 * j : 16 * j + 24, 256:].reshape(576, 256).astype(BF)
        for h in range(HEADS):
            v2_ref[j, h * KEYS : h * KEYS + 576, :] = values * vmask[h]
            v2_ref[j, h * KEYS + 576 : (h + 1) * KEYS, :] = zero
        mixed = attend(q, keys, qmask, lambda h: b2_ref[h], p2_ref.at[j], v2_ref.at[j], expand)
        res = bo_ref[4:20, 8 + 16 * j : 24 + 16 * j, :].reshape(256, 256) + mm(mixed.astype(BF), o2_ref[...])
        out = mlp(res, gains[3], real, ww2_ref[...], wn2_ref[...])
        out_ref[:, 16 * j : 16 * j + 16, :] = out.reshape(16, 16, 256)[:, :, :C].astype(BF)


def swap(low, high, axis):
    count = lax.axis_size(axis)
    even = lax.axis_index(axis) % 2 == 0

    def pairs(first):
        found = []
        for i in range(first, count - 1, 2):
            found += [(i, i + 1), (i + 1, i)]
        return found

    a = lax.ppermute(jnp.where(even, high, low), axis, pairs(0))
    b = lax.ppermute(jnp.where(even, low, high), axis, pairs(1))
    return a, b


def per_device(
    pixels, shift_prenorm, shift_inputs, shift_table, shift_output, shift_postnorm, shift_widen, shift_narrow,
    cross_prenorm, cross_query, cross_keyval, cross_table, cross_output, cross_postnorm, cross_widen, cross_narrow,
):
    ra, rb = swap(pixels[:SHIFT], pixels[SHIFT:], "rows")
    odd = lax.axis_index("rows") % 2 == 1
    top = jnp.where(odd, ra, rb)
    bot = jnp.where(odd, rb, ra)
    column = lambda part: jnp.concatenate([top[:, part], pixels[:, part], bot[:, part]], axis=0)
    ca, cb = swap(column(slice(0, SHIFT)), column(slice(24, 32)), "cols")

    st = jnp.pad(jnp.swapaxes(shift_table[:, ::-1, :], 1, 2), ((0, 0), (0, 1), (0, 1))).reshape(192, 32)
    ct = jnp.pad(jnp.swapaxes(cross_table, 1, 2)[:, ::-1, :], ((0, 0), (0, 1), (0, 1))).reshape(240, 40)
    gains = jnp.pad(jnp.stack([shift_prenorm, shift_postnorm, cross_prenorm, cross_postnorm]), ((0, 4), (0, 76)))
    sds = jax.ShapeDtypeStruct
    made = pl.pallas_call(
        tables_kernel,
        out_shape=(
            sds((HEADS, 256, 256), F32), sds((HEADS, 256, KEYS), F32), sds((256, 768), BF), sds((256, 256), BF),
            sds((256, 384), BF), sds((256, 384), BF), sds((256, 768), BF), sds((256, 256), BF), sds((256, 384), BF),
            sds((256, 384), BF),
        ),
        scratch_shapes=[pltpu.VMEM((192, 512), F32), pltpu.VMEM((240, 1024), F32)],
        cost_estimate=pl.CostEstimate(flops=200_000_000, bytes_accessed=8_000_000, transcendentals=0),
        name="tables",
    )(
        st, ct, shift_inputs, shift_output, shift_widen, shift_narrow.T, cross_query, cross_keyval, cross_output,
        cross_widen, cross_narrow.T,
    )
    position = jnp.stack(
        [
            lax.axis_index("rows"), lax.axis_index("cols"),
            jnp.int32(lax.axis_size("rows") - 1), jnp.int32(lax.axis_size("cols") - 1),
        ]
    ).astype(jnp.int32)
    vmem = pl.BlockSpec(memory_space=pltpu.VMEM)
    return pl.pallas_call(
        main_kernel,
        out_shape=sds(pixels.shape, BF),
        in_specs=[pl.BlockSpec(memory_space=pltpu.SMEM)] + [vmem] * 16,
        out_specs=vmem,
        scratch_shapes=[
            pltpu.VMEM((6, 16, 16, 256), F32),
            pltpu.VMEM((2, 192, HEADS * 256), BF),
            pltpu.VMEM((2, HEADS * 256, 256), BF),
            pltpu.VMEM((24, 48, 256), F32),
            pltpu.VMEM((24, 48, 256), F32),
            pltpu.VMEM((24, 40, 512), F32),
            pltpu.VMEM((2, 256, HEADS * KEYS), BF),
            pltpu.VMEM((2, HEADS * KEYS, 256), BF),
        ],
        cost_estimate=pl.CostEstimate(flops=10_000_000_000, bytes_accessed=8_000_000, transcendentals=4_000_000),
        name="blocks",
    )(position, pixels, ra, rb, ca, cb, gains, *made)


def solution(mesh):
    return jax.shard_map(
        per_device,
        mesh=mesh,
        in_specs=(P("rows", "cols", None),) + (P(),) * 15,
        out_specs=P("rows", "cols", None),
        check_vma=False,
    )
```

```python
import jax
import jax.numpy as jnp
from jax import lax
from jax.experimental import pallas as pl
from jax.experimental.pallas import tpu as pltpu
from jax.sharding import PartitionSpec as P

C = 180
HEADS = 6
HEAD_DIM = 30
WIN = 16
SHIFT = 8
PAD = 4
OWIN = 24
EPS = 1e-05
LOG2E = 1.4426950408889634
SCALE = HEAD_DIM ** (-0.5) * LOG2E
LOW = -1e30
FLAG = 180
ONE = 181
KFLAG = 100
SUM = 96
KEYS = 640
BF = jnp.bfloat16
F32 = jnp.float32


def mm(a, b, dims=((1,), (0,)), precision=None):
    return lax.dot_general(a, b, (dims, ((), ())), preferred_element_type=F32, precision=precision)


NT = ((1,), (1,))


def lanes(shape):
    return lax.broadcasted_iota(jnp.int32, shape, len(shape) - 1)


def rows_of(shape):
    return lax.broadcasted_iota(jnp.int32, shape, len(shape) - 2)


def place(dst_ref, src, row, col):
    dst_ref[row : row + src.shape[0], col : col + src.shape[1]] = src


def exact_parts(x):
    first = x.astype(BF)
    rest = x - first.astype(F32)
    second = rest.astype(BF)
    return first, second, (rest - second.astype(F32)).astype(BF)


def shear(table_ref, flip, side, pick, amount, bits):
    top = HEADS * side
    y = None
    for part in exact_parts(table_ref[...] * LOG2E):
        turned = [mm(flip, part[h * side : (h + 1) * side], NT) for h in range(HEADS)]
        term = mm(jnp.concatenate(turned, axis=0).astype(BF), pick)
        y = term if y is None else y + term
    for bit in bits:
        y = jnp.where((amount & bit) != 0, pltpu.roll(y, top - bit, 0), y)
    return y


def tables_kernel(
    g0_ref, g1_ref, g2_ref, g3_ref,
    st_ref, ct_ref, wi_ref, wo_ref, ww_ref, wn_ref, cq_ref, ckv_ref, co_ref, cw_ref, cn_ref,
    gain_ref, b1_ref, b2_ref, w1_ref, o1_ref, ww1_ref, wn1_ref, w2_ref, o2_ref, ww2_ref, wn2_ref,
    t1_ref, t2_ref, e1_ref, e2_ref,
):
    r = rows_of((256, 768))
    c = lanes((256, 768))
    base = jnp.where((r == FLAG) & ((c == 256 + KFLAG) | (c == 384 + KFLAG)), LOW, 0.0)
    base = jnp.where((r == ONE) & ((c == KFLAG) | (c == 128 + KFLAG)), 1.0, base)
    base = jnp.where((r == ONE) & ((c == 512 + SUM) | (c == 640 + SUM)), 1.0, base)
    w1_ref[...] = base.astype(BF)
    w2_ref[...] = jnp.where(r == ONE, base, 0.0).astype(BF)
    for k in range(6):
        place(w1_ref, wi_ref[:, 90 * k : 90 * k + 90], 0, 128 * k)
    for k in range(2):
        place(w2_ref, cq_ref[:, 90 * k : 90 * k + 90], 0, 128 * k)
    for k in range(4):
        place(w2_ref, ckv_ref[:, 90 * k : 90 * k + 90], 0, 256 + 128 * k)
    for dst, src in ((o1_ref, wo_ref), (o2_ref, co_ref)):
        dst[...] = jnp.zeros(dst.shape, BF)
        place(dst, src[:90], 0, 0)
        place(dst, src[90:], 128, 0)
    for dst, src in ((ww1_ref, ww_ref), (wn1_ref, wn_ref), (ww2_ref, cw_ref), (wn2_ref, cn_ref)):
        dst[...] = jnp.zeros(dst.shape, BF)
        place(dst, src[...], 0, 0)
    gain_ref[...] = jnp.zeros(gain_ref.shape, F32)
    for i, src in enumerate((g0_ref, g1_ref, g2_ref, g3_ref)):
        gain_ref[i : i + 1, :C] = src[...]
    t1_ref[...] = jnp.zeros(t1_ref.shape, F32)
    t2_ref[...] = jnp.zeros(t2_ref.shape, F32)
    for h in range(HEADS):
        t1_ref[h * 32 : h * 32 + 31, :31] = st_ref[h]
        t2_ref[h * 40 : h * 40 + 39, :39] = ct_ref[h]
    flip = jnp.where(rows_of((32, 32)) == lanes((32, 32)), 1.0, 0.0).astype(BF)
    pick = jnp.where(lanes((32, 512)) // 16 == 30 - rows_of((32, 512)), 1.0, 0.0).astype(BF)
    amount = 15 - lanes((192, 512)) % 16
    e1_ref[...] = shear(t1_ref, flip, 32, pick, amount, (8, 4, 2, 1))
    for h in range(HEADS):
        for qy in range(WIN):
            b1_ref[h, qy * 16 : qy * 16 + 16, :] = e1_ref[h * 32 : h * 32 + 16, (15 - qy) * 16 : (15 - qy) * 16 + 256]
    flip = jnp.where(rows_of((40, 40)) == 38 - lanes((40, 40)), 1.0, 0.0).astype(BF)
    lane = lanes((40, 1024))
    row = rows_of((40, 1024))
    pick = jnp.where((lane >= row * 24) & (lane < row * 24 + 24), 1.0, 0.0).astype(BF)
    lane1 = lanes((1, 1024)).astype(F32)
    kx = lane1 - 24.0 * jnp.floor((lane1 + 0.5) * (1.0 / 24.0))
    amount = jnp.broadcast_to(23 - kx.astype(jnp.int32), (240, 1024))
    e2_ref[...] = shear(t2_ref, flip, 40, pick, amount, (16, 8, 4, 2, 1))
    for h in range(HEADS):
        b2_ref[h, :, 512:640] = jnp.zeros((256, 128), F32)
        for qy in range(WIN):
            b2_ref[h, qy * 16 : qy * 16 + 16, :576] = e2_ref[h * 40 : h * 40 + 16, (15 - qy) * 24 : (15 - qy) * 24 + 576]


def norm(x, gain, real):
    x0 = x[:, :128]
    x1 = jnp.where(real, x[:, 128:], 0.0)
    mean = jnp.sum(x0 + x1, axis=-1, keepdims=True) * (1.0 / C)
    c0 = x0 - mean
    c1 = jnp.where(real, x1 - mean, 0.0)
    spread = jnp.sum(c0 * c0 + c1 * c1, axis=-1, keepdims=True) * (1.0 / C)
    inv = lax.rsqrt(spread + EPS)
    return c0 * inv * gain[:, :128], c1 * inv * gain[:, 128:]


def gelu(x):
    return 0.5 * x * (1.0 + lax.erf(x * 0.7071067811865476))


def mlp(res, gain, real, widen, narrow):
    n0, n1 = norm(res, gain, real)
    normed = jnp.concatenate([n0, n1], axis=1).astype(BF)
    hidden = gelu(mm(normed, widen)).astype(BF)
    return res + mm(hidden, narrow, NT)


def attend(queries, keys, values, bias_of):
    lane = lanes((1, 128))
    halves = []
    for half in range(2):
        part = slice(128 * half, 128 * half + 128)
        qh, kh, vh = queries[:, part], keys[:, part], values[:, part]
        mixed = None
        for t in range(3):
            own = ((lane >= 30 * t) & (lane < 30 * t + 30)) | (lane == KFLAG)
            scores = mm(qh * jnp.where(own, 1.0, 0.0).astype(BF), kh, NT) + bias_of(half * 3 + t)
            peak = jnp.max(scores, axis=-1, keepdims=True)
            weights = jnp.exp2(scores - peak).astype(BF)
            out = mm(weights, vh)
            out = out * (1.0 / out[:, SUM : SUM + 1])
            mixed = out if mixed is None else jnp.where(lane >= 30 * t, out, mixed)
        halves.append(mixed)
    return jnp.concatenate(halves, axis=1).astype(BF)


def main_kernel(
    cen_ref, ra_ref, rb_ref, ca_ref, cb_ref, gain_ref,
    b1_ref, b2_ref, w1_ref, o1_ref, ww1_ref, wn1_ref, w2_ref, o2_ref, ww2_ref, wn2_ref,
    out_ref,
    x_ref, bo_ref, a3_ref, kv_ref,
):
    row, col = lax.axis_index("rows"), lax.axis_index("cols")
    last_row, last_col = lax.axis_size("rows") - 1, lax.axis_size("cols") - 1
    real = lanes((1, 128)) < C - 128
    lane1 = lanes((1, 128))
    one1 = jnp.where(lane1 == ONE - 128, 1.0, 0.0)

    def put(window, y0, x0, piece, flag):
        ny, nx = piece.shape[0], piece.shape[1]
        x_ref[window, y0 : y0 + ny, x0 : x0 + nx, 128:] = jnp.broadcast_to(
            jnp.where(lane1 == FLAG - 128, flag, one1), (ny, nx, 128)
        )
        x_ref[window, y0 : y0 + ny, x0 : x0 + nx, :C] = piece.astype(F32)

    row_odd = lax.rem(row, 2) == 1
    col_odd = lax.rem(col, 2) == 1
    out_top = jnp.where(row == 0, 1.0, 0.0)
    out_bot = jnp.where(row == last_row, 1.0, 0.0)
    out_lef = jnp.where(col == 0, 1.0, 0.0)
    out_rig = jnp.where(col == last_col, 1.0, 0.0)
    top = jnp.where(row_odd, ra_ref[...], rb_ref[...])
    bot = jnp.where(row_odd, rb_ref[...], ra_ref[...])
    lef = jnp.where(col_odd, ca_ref[...], cb_ref[...])
    rig = jnp.where(col_odd, cb_ref[...], ca_ref[...])
    both = jnp.maximum
    put(0, 0, 0, lef[:8], both(out_top, out_lef))
    put(0, 0, 8, top[:, :8], out_top)
    put(0, 8, 0, lef[8:16], out_lef)
    put(0, 8, 8, cen_ref[:8, :8], 0.0)
    put(1, 0, 0, top[:, 8:24], out_top)
    put(1, 8, 0, cen_ref[:8, 8:24], 0.0)
    put(2, 0, 0, top[:, 24:], out_top)
    put(2, 0, 8, rig[:8], both(out_top, out_rig))
    put(2, 8, 0, cen_ref[:8, 24:], 0.0)
    put(2, 8, 8, rig[8:16], out_rig)
    put(3, 0, 0, lef[16:24], out_lef)
    put(3, 0, 8, cen_ref[8:, :8], 0.0)
    put(3, 8, 0, lef[24:], both(out_bot, out_lef))
    put(3, 8, 8, bot[:, :8], out_bot)
    put(4, 0, 0, cen_ref[8:, 8:24], 0.0)
    put(4, 8, 0, bot[:, 8:24], out_bot)
    put(5, 0, 0, cen_ref[8:, 24:], 0.0)
    put(5, 0, 8, rig[16:24], out_rig)
    put(5, 8, 0, bot[:, 24:], out_bot)
    put(5, 8, 8, rig[24:], both(out_bot, out_rig))

    gains = [gain_ref[i : i + 1, :] for i in range(4)]

    def shifted(j, carry):
        for i in range(2):
            x = x_ref[i * 3 + j].reshape(256, 256)
            n0, n1 = norm(x, gains[0], real)
            n1 = jnp.where(real, n1, x[:, 128:])
            normed = jnp.concatenate([n0, n1], axis=1).astype(BF)
            first = 64 * (1 - i)
            q = (mm(normed[first : first + 192], w1_ref[:, :256]) * SCALE).astype(BF)
            kv = mm(normed, w1_ref[:, 256:]).astype(BF)
            mixed = attend(q, kv[:, :256], kv[:, 256:], lambda h: b1_ref[h, first : first + 192, :])
            res = x[first : first + 192] + mm(mixed, o1_ref[...])
            out = mlp(res, gains[1], real, ww1_ref[...], wn1_ref[...])
            bo_ref[i * 12 : i * 12 + 12, pl.ds(pl.multiple_of(j * 16, 16), 16), :] = (
                out.astype(BF).astype(F32).reshape(12, 16, 256)
            )
        return carry

    lax.fori_loop(0, 3, shifted, 0)

    n0, n1 = norm(bo_ref[...].reshape(24 * 48, 256), gains[2], real)
    a3_ref[:, :, :128] = n0.reshape(24, 48, 128)
    a3_ref[:, :, 128:] = (n1 + one1).reshape(24, 48, 128)
    base = jnp.where(lanes((1, 1, 256)) == ONE, 1.0, 0.0)

    @pl.when(row == 0)
    def _():
        a3_ref[:4] = jnp.broadcast_to(base, (4, 48, 256))

    @pl.when(row == last_row)
    def _():
        a3_ref[20:] = jnp.broadcast_to(base, (4, 48, 256))

    @pl.when(col == 0)
    def _():
        a3_ref[:, :8] = jnp.broadcast_to(base, (24, 8, 256))

    @pl.when(col == last_col)
    def _():
        a3_ref[:, 40:] = jnp.broadcast_to(base, (24, 8, 256))

    kv = mm(a3_ref[:, 4:44, :].reshape(960, 256).astype(BF), w2_ref[:, 256:])
    kv_ref[...] = kv.reshape(24, 40, 512)
    pad = jnp.where(lanes((64, 256)) % 128 == KFLAG, LOW, 0.0).astype(BF)
    zero = jnp.zeros((64, 256), BF)

    for j in range(2):
        q = a3_ref[4:20, 8 + 16 * j : 24 + 16 * j, :].reshape(256, 256).astype(BF)
        q = (mm(q, w2_ref[:, :256]) * SCALE).astype(BF)
        keys = kv_ref[:, 16 * j : 16 * j + 24, :256].reshape(576, 256).astype(BF)
        keys = jnp.concatenate([keys, pad], axis=0)
        values = kv_ref[:, 16 * j : 16 * j + 24, 256:].reshape(576, 256).astype(BF)
        values = jnp.concatenate([values, zero], axis=0)
        mixed = attend(q, keys, values, lambda h: b2_ref[h])
        res = bo_ref[4:20, 8 + 16 * j : 24 + 16 * j, :].reshape(256, 256) + mm(mixed, o2_ref[...])
        out = mlp(res, gains[3], real, ww2_ref[...], wn2_ref[...])
        out_ref[:, 16 * j : 16 * j + 16, :] = out.reshape(16, 16, 256)[:, :, :C].astype(BF)


def swap(low, high, axis):
    count = lax.axis_size(axis)
    even = lax.axis_index(axis) % 2 == 0

    def pairs(first):
        found = []
        for i in range(first, count - 1, 2):
            found += [(i, i + 1), (i + 1, i)]
        return found

    a = lax.ppermute(jnp.where(even, high, low), axis, pairs(0))
    b = lax.ppermute(jnp.where(even, low, high), axis, pairs(1))
    return a, b


def per_device(
    pixels, shift_prenorm, shift_inputs, shift_table, shift_output, shift_postnorm, shift_widen, shift_narrow,
    cross_prenorm, cross_query, cross_keyval, cross_table, cross_output, cross_postnorm, cross_widen, cross_narrow,
):
    ra, rb = swap(pixels[:SHIFT], pixels[SHIFT:], "rows")
    odd = lax.axis_index("rows") % 2 == 1
    top = jnp.where(odd, ra, rb)
    bot = jnp.where(odd, rb, ra)
    column = lambda part: jnp.concatenate([top[:, part], pixels[:, part], bot[:, part]], axis=0)
    ca, cb = swap(column(slice(0, SHIFT)), column(slice(24, 32)), "cols")

    sds = jax.ShapeDtypeStruct
    made = pl.pallas_call(
        tables_kernel,
        out_shape=(
            sds((8, 256), F32), sds((HEADS, 256, 256), F32), sds((HEADS, 256, KEYS), F32), sds((256, 768), BF), sds((256, 256), BF),
            sds((256, 384), BF), sds((256, 384), BF), sds((256, 768), BF), sds((256, 256), BF), sds((256, 384), BF),
            sds((256, 384), BF),
        ),
        scratch_shapes=[pltpu.VMEM((192, 32), F32), pltpu.VMEM((240, 40), F32), pltpu.VMEM((192, 512), F32), pltpu.VMEM((240, 1024), F32)],
        cost_estimate=pl.CostEstimate(flops=200_000_000, bytes_accessed=8_000_000, transcendentals=0),
        compiler_params=pltpu.CompilerParams(vmem_limit_bytes=16 * 2**20),
        name="tables",
    )(
        shift_prenorm.reshape(1, C), shift_postnorm.reshape(1, C), cross_prenorm.reshape(1, C), cross_postnorm.reshape(1, C),
        shift_table, cross_table, shift_inputs, shift_output, shift_widen, shift_narrow.T, cross_query, cross_keyval, cross_output,
        cross_widen, cross_narrow.T,
    )
    vmem = pl.BlockSpec(memory_space=pltpu.VMEM)
    return pl.pallas_call(
        main_kernel,
        out_shape=sds(pixels.shape, BF),
        in_specs=[vmem] * 16,
        out_specs=vmem,
        scratch_shapes=[
            pltpu.VMEM((6, 16, 16, 256), F32),
            pltpu.VMEM((24, 48, 256), F32),
            pltpu.VMEM((24, 48, 256), F32),
            pltpu.VMEM((24, 40, 512), F32),
        ],
        cost_estimate=pl.CostEstimate(flops=10_000_000_000, bytes_accessed=8_000_000, transcendentals=4_000_000),
        compiler_params=pltpu.CompilerParams(vmem_limit_bytes=32 * 2**20),
        name="blocks",
    )(pixels, ra, rb, ca, cb, *made)


def solution(mesh):
    return jax.shard_map(
        per_device,
        mesh=mesh,
        in_specs=(P("rows", "cols", None),) + (P(),) * 15,
        out_specs=P("rows", "cols", None),
        check_vma=False,
    )
```

```python
import jax
import jax.numpy as jnp
from jax import lax
from jax.experimental import pallas as pl
from jax.experimental.pallas import tpu as pltpu
from jax.sharding import PartitionSpec as P

C = 180
HEADS = 6
HEAD_DIM = 30
WIN = 16
SHIFT = 8
PAD = 4
OWIN = 24
EPS = 1e-05
LOG2E = 1.4426950408889634
SCALE = HEAD_DIM ** (-0.5) * LOG2E
LOW = -1e30
FLAG = 180
ONE = 181
KFLAG = 100
SUM = 96
KEYS = 640
BF = jnp.bfloat16
F32 = jnp.float32


def mm(a, b, dims=((1,), (0,)), precision=None):
    return lax.dot_general(a, b, (dims, ((), ())), preferred_element_type=F32, precision=precision)


NT = ((1,), (1,))


def lanes(shape):
    return lax.broadcasted_iota(jnp.int32, shape, len(shape) - 1)


def rows_of(shape):
    return lax.broadcasted_iota(jnp.int32, shape, len(shape) - 2)


def place(dst_ref, src, row, col):
    dst_ref[row : row + src.shape[0], col : col + src.shape[1]] = src


def exact_parts(x):
    first = x.astype(BF)
    rest = x - first.astype(F32)
    second = rest.astype(BF)
    return first, second, (rest - second.astype(F32)).astype(BF)


def shear(table_ref, flip, side, pick, amount, bits):
    top = HEADS * side
    y = None
    for part in exact_parts(table_ref[...] * LOG2E):
        turned = [mm(flip, part[h * side : (h + 1) * side], NT) for h in range(HEADS)]
        term = mm(jnp.concatenate(turned, axis=0).astype(BF), pick)
        y = term if y is None else y + term
    for bit in bits:
        y = jnp.where((amount & bit) != 0, pltpu.roll(y, top - bit, 0), y)
    return y


def tables_kernel(*refs):
    sources = refs[:16]
    (
        cen_ref, low_ref, high_ref, gain_ref, b1_ref, b2_ref, w1_ref, o1_ref, ww1_ref, wn1_ref, w2_ref, o2_ref, ww2_ref, wn2_ref,
        g0_ref, g1_ref, g2_ref, g3_ref, st_ref, ct_ref, wi_ref, wo_ref, ww_ref, wn_ref, cq_ref, ckv_ref, co_ref, cw_ref, cn_ref,
        sems, t1_ref, t2_ref, e1_ref, e2_ref,
    ) = refs[16:]
    targets = (
        cen_ref, st_ref, ct_ref, g0_ref, g1_ref, g2_ref, g3_ref, wi_ref, wo_ref, ww_ref, wn_ref, cq_ref, ckv_ref, co_ref,
        cw_ref, cn_ref,
    )
    copies = [pltpu.make_async_copy(a, b, sems.at[i]) for i, (a, b) in enumerate(zip(sources, targets))]
    for copy in copies:
        copy.start()

    def zeros(ref):
        ref[...] = jnp.zeros(ref.shape, ref.dtype)

    r = rows_of((256, 768))
    c = lanes((256, 768))
    base = jnp.where((r == FLAG) & ((c == 256 + KFLAG) | (c == 384 + KFLAG)), LOW, 0.0)
    base = jnp.where((r == ONE) & ((c == KFLAG) | (c == 128 + KFLAG)), 1.0, base)
    base = jnp.where((r == ONE) & ((c == 512 + SUM) | (c == 640 + SUM)), 1.0, base)
    w1_ref[...] = base.astype(BF)
    w2_ref[...] = jnp.where(r == ONE, base, 0.0).astype(BF)
    for ref in (o1_ref, ww1_ref, wn1_ref, o2_ref, ww2_ref, wn2_ref, gain_ref, t1_ref, t2_ref):
        zeros(ref)
    for h in range(HEADS):
        b2_ref[h, :, 512:640] = jnp.zeros((256, 128), F32)
    for copy in copies[:3]:
        copy.wait()
    low_ref[...] = cen_ref[:, :SHIFT]
    high_ref[...] = cen_ref[:, 24:]
    for h in range(HEADS):
        t1_ref[h * 32 : h * 32 + 31, :31] = st_ref[h]
        t2_ref[h * 40 : h * 40 + 39, :39] = ct_ref[h]
    flip = jnp.where(rows_of((32, 32)) == lanes((32, 32)), 1.0, 0.0).astype(BF)
    pick = jnp.where(lanes((32, 512)) // 16 == 30 - rows_of((32, 512)), 1.0, 0.0).astype(BF)
    amount = 15 - lanes((192, 512)) % 16
    e1_ref[...] = shear(t1_ref, flip, 32, pick, amount, (8, 4, 2, 1))
    for h in range(HEADS):
        for qy in range(WIN):
            b1_ref[h, qy * 16 : qy * 16 + 16, :] = e1_ref[h * 32 : h * 32 + 16, (15 - qy) * 16 : (15 - qy) * 16 + 256]
    flip = jnp.where(rows_of((40, 40)) == 38 - lanes((40, 40)), 1.0, 0.0).astype(BF)
    lane = lanes((40, 1024))
    row = rows_of((40, 1024))
    pick = jnp.where((lane >= row * 24) & (lane < row * 24 + 24), 1.0, 0.0).astype(BF)
    lane1 = lanes((1, 1024)).astype(F32)
    kx = lane1 - 24.0 * jnp.floor((lane1 + 0.5) * (1.0 / 24.0))
    amount = jnp.broadcast_to(23 - kx.astype(jnp.int32), (240, 1024))
    e2_ref[...] = shear(t2_ref, flip, 40, pick, amount, (16, 8, 4, 2, 1))
    for h in range(HEADS):
        for qy in range(WIN):
            b2_ref[h, qy * 16 : qy * 16 + 16, :576] = e2_ref[h * 40 : h * 40 + 16, (15 - qy) * 24 : (15 - qy) * 24 + 576]
    for copy in copies[3:]:
        copy.wait()
    for k in range(6):
        place(w1_ref, wi_ref[:, 90 * k : 90 * k + 90], 0, 128 * k)
    for k in range(2):
        place(w2_ref, cq_ref[:, 90 * k : 90 * k + 90], 0, 128 * k)
    for k in range(4):
        place(w2_ref, ckv_ref[:, 90 * k : 90 * k + 90], 0, 256 + 128 * k)
    for dst, src in ((o1_ref, wo_ref), (o2_ref, co_ref)):
        place(dst, src[:90], 0, 0)
        place(dst, src[90:], 128, 0)
    for dst, src in ((ww1_ref, ww_ref), (wn1_ref, wn_ref), (ww2_ref, cw_ref), (wn2_ref, cn_ref)):
        place(dst, src[...], 0, 0)
    for i, src in enumerate((g0_ref, g1_ref, g2_ref, g3_ref)):
        gain_ref[i : i + 1, :C] = src[...]


def norm(x, gain, real):
    x0 = x[:, :128]
    x1 = jnp.where(real, x[:, 128:], 0.0)
    mean = jnp.sum(x0 + x1, axis=-1, keepdims=True) * (1.0 / C)
    c0 = x0 - mean
    c1 = jnp.where(real, x1 - mean, 0.0)
    spread = jnp.sum(c0 * c0 + c1 * c1, axis=-1, keepdims=True) * (1.0 / C)
    inv = lax.rsqrt(spread + EPS)
    return c0 * inv * gain[:, :128], c1 * inv * gain[:, 128:]


def gelu(x):
    return 0.5 * x * (1.0 + lax.erf(x * 0.7071067811865476))


def mlp(res, gain, real, widen, narrow):
    n0, n1 = norm(res, gain, real)
    normed = jnp.concatenate([n0, n1], axis=1).astype(BF)
    hidden = gelu(mm(normed, widen)).astype(BF)
    return res + mm(hidden, narrow, NT)


def attend(jobs, s_refs):
    lane = lanes((1, 128))
    order = [(job, h) for h in range(HEADS) for job in range(len(jobs))]

    def start(n):
        job, h = order[n]
        half, t = divmod(h, 3)
        queries, keys, _, bias = jobs[job]
        own = ((lane >= 30 * t) & (lane < 30 * t + 30)) | (lane == KFLAG)
        scores = mm(queries(half) * jnp.where(own, 1.0, 0.0).astype(BF), keys(half), NT) + bias(h)
        s_refs[n % len(s_refs)][...] = scores
        return jnp.max(scores, axis=-1, keepdims=True)

    mixed = [[None, None] for _ in jobs]
    peak = start(0)
    for n, (job, h) in enumerate(order):
        ahead = start(n + 1) if n + 1 < len(order) else None
        half, t = divmod(h, 3)
        weights = jnp.exp2(s_refs[n % len(s_refs)][...] - peak).astype(BF)
        out = mm(weights, jobs[job][2](half))
        out = out * (1.0 / out[:, SUM : SUM + 1])
        mixed[job][half] = out if t == 0 else jnp.where(lane >= 30 * t, out, mixed[job][half])
        peak = ahead
    return [jnp.concatenate(pair, axis=1).astype(BF) for pair in mixed]


def shifted_windows(windows, x_ref, gain_ref, b1_ref, w1_ref, o1_ref, ww1_ref, wn1_ref, q_ref, kv_ref, s_refs):
    real = lanes((1, 128)) < C - 128
    jobs = []
    for slot, i in windows:
        x = x_ref[slot].reshape(256, 256)
        n0, n1 = norm(x, gain_ref[0:1, :], real)
        n1 = jnp.where(real, n1, x[:, 128:])
        normed = jnp.concatenate([n0, n1], axis=1).astype(BF)
        first = 64 * (1 - i)
        q_ref[slot] = (mm(normed[first : first + 192], w1_ref[:, :256]) * SCALE).astype(BF)
        kv_ref[slot] = mm(normed, w1_ref[:, 256:]).astype(BF)
        jobs.append(
            (
                lambda half, slot=slot: q_ref[slot, :, half * 128 : half * 128 + 128],
                lambda half, slot=slot: kv_ref[slot, :, half * 128 : half * 128 + 128],
                lambda half, slot=slot: kv_ref[slot, :, 256 + half * 128 : 384 + half * 128],
                lambda h, first=first: b1_ref[h, first : first + 192, :],
            )
        )
    outs = []
    for (slot, i), mixed in zip(windows, attend(jobs, s_refs)):
        first = 64 * (1 - i)
        res = x_ref[slot].reshape(256, 256)[first : first + 192] + mm(mixed, o1_ref[...])
        out = mlp(res, gain_ref[1:2, :], real, ww1_ref[...], wn1_ref[...])
        outs.append(out.astype(BF).astype(F32).reshape(12, 16, 256))
    return outs


def put(x_ref, slot, y0, x0, piece, flag):
    lane1 = lanes((1, 128))
    ny, nx = piece.shape[0], piece.shape[1]
    x_ref[slot, y0 : y0 + ny, x0 : x0 + nx, 128:] = jnp.broadcast_to(
        jnp.where(lane1 == FLAG - 128, flag, jnp.where(lane1 == ONE - 128, 1.0, 0.0)), (ny, nx, 128)
    )
    x_ref[slot, y0 : y0 + ny, x0 : x0 + nx, :C] = piece.astype(F32)


def edges():
    row, col = lax.axis_index("rows"), lax.axis_index("cols")
    return row, col, lax.axis_size("rows") - 1, lax.axis_size("cols") - 1


def flag_of(condition):
    return jnp.where(condition, 1.0, 0.0)


def middle_kernel(
    cen_ref, ra_ref, rb_ref, gain_ref, b1_ref, w1_ref, o1_ref, ww1_ref, wn1_ref, out_ref, x_ref, q_ref, kv_ref, s0_ref, s1_ref
):
    row, _, last_row, _ = edges()
    odd = lax.rem(row, 2) == 1
    top = jnp.where(odd, ra_ref[:, 8:24], rb_ref[:, 8:24])
    bot = jnp.where(odd, rb_ref[:, 8:24], ra_ref[:, 8:24])
    put(x_ref, 0, 0, 0, top, flag_of(row == 0))
    put(x_ref, 0, 8, 0, cen_ref[:8, 8:24], 0.0)
    put(x_ref, 1, 0, 0, cen_ref[8:, 8:24], 0.0)
    put(x_ref, 1, 8, 0, bot, flag_of(row == last_row))
    outs = shifted_windows(
        [(0, 0), (1, 1)], x_ref, gain_ref, b1_ref, w1_ref, o1_ref, ww1_ref, wn1_ref, q_ref, kv_ref, (s0_ref, s1_ref)
    )
    out_ref[:12] = outs[0]
    out_ref[12:] = outs[1]


def main_kernel(
    cen_ref, ra_ref, rb_ref, ca_ref, cb_ref, mid_ref, gain_ref,
    b1_ref, b2_ref, w1_ref, o1_ref, ww1_ref, wn1_ref, w2_ref, o2_ref, ww2_ref, wn2_ref,
    out_ref,
    x_ref, q_ref, kv_ref, s0_ref, s1_ref, bo_ref, a3_ref, kvs_ref, q2_ref, kv2_ref, s2_ref, s3_ref,
):
    row, col, last_row, last_col = edges()
    real = lanes((1, 128)) < C - 128
    one1 = jnp.where(lanes((1, 128)) == ONE - 128, 1.0, 0.0)
    row_odd = lax.rem(row, 2) == 1
    col_odd = lax.rem(col, 2) == 1
    out_top = flag_of(row == 0)
    out_bot = flag_of(row == last_row)
    out_lef = flag_of(col == 0)
    out_rig = flag_of(col == last_col)
    top = jnp.where(row_odd, ra_ref[...], rb_ref[...])
    bot = jnp.where(row_odd, rb_ref[...], ra_ref[...])
    lef = jnp.where(col_odd, ca_ref[...], cb_ref[...])
    rig = jnp.where(col_odd, cb_ref[...], ca_ref[...])
    both = jnp.maximum
    put(x_ref, 0, 0, 0, lef[:8], both(out_top, out_lef))
    put(x_ref, 0, 0, 8, top[:, :8], out_top)
    put(x_ref, 0, 8, 0, lef[8:16], out_lef)
    put(x_ref, 0, 8, 8, cen_ref[:8, :8], 0.0)
    put(x_ref, 1, 0, 0, lef[16:24], out_lef)
    put(x_ref, 1, 0, 8, cen_ref[8:, :8], 0.0)
    put(x_ref, 1, 8, 0, lef[24:], both(out_bot, out_lef))
    put(x_ref, 1, 8, 8, bot[:, :8], out_bot)
    put(x_ref, 2, 0, 0, top[:, 24:], out_top)
    put(x_ref, 2, 0, 8, rig[:8], both(out_top, out_rig))
    put(x_ref, 2, 8, 0, cen_ref[:8, 24:], 0.0)
    put(x_ref, 2, 8, 8, rig[8:16], out_rig)
    put(x_ref, 3, 0, 0, cen_ref[8:, 24:], 0.0)
    put(x_ref, 3, 0, 8, rig[16:24], out_rig)
    put(x_ref, 3, 8, 0, bot[:, 24:], out_bot)
    put(x_ref, 3, 8, 8, rig[24:], both(out_bot, out_rig))

    outs = shifted_windows(
        [(0, 0), (1, 1), (2, 0), (3, 1)],
        x_ref, gain_ref, b1_ref, w1_ref, o1_ref, ww1_ref, wn1_ref, q_ref, kv_ref, (s0_ref, s1_ref),
    )
    bo_ref[:12, :16] = outs[0]
    bo_ref[12:, :16] = outs[1]
    bo_ref[:, 16:32] = mid_ref[...]
    bo_ref[:12, 32:] = outs[2]
    bo_ref[12:, 32:] = outs[3]

    n0, n1 = norm(bo_ref[...].reshape(24 * 48, 256), gain_ref[2:3, :], real)
    a3_ref[:, :, :128] = n0.reshape(24, 48, 128)
    a3_ref[:, :, 128:] = (n1 + one1).reshape(24, 48, 128)
    base = jnp.where(lanes((1, 1, 256)) == ONE, 1.0, 0.0)

    @pl.when(row == 0)
    def _():
        a3_ref[:4] = jnp.broadcast_to(base, (4, 48, 256))

    @pl.when(row == last_row)
    def _():
        a3_ref[20:] = jnp.broadcast_to(base, (4, 48, 256))

    @pl.when(col == 0)
    def _():
        a3_ref[:, :8] = jnp.broadcast_to(base, (24, 8, 256))

    @pl.when(col == last_col)
    def _():
        a3_ref[:, 40:] = jnp.broadcast_to(base, (24, 8, 256))

    kvs_ref[...] = mm(a3_ref[:, 4:44, :].reshape(960, 256).astype(BF), w2_ref[:, 256:]).reshape(24, 40, 512)
    pad = jnp.where(lanes((64, 512)) % 128 == KFLAG, LOW, 0.0)
    pad = jnp.where(lanes((64, 512)) < 256, pad, 0.0).astype(BF)
    jobs = []
    for j in range(2):
        q = a3_ref[4:20, 8 + 16 * j : 24 + 16 * j, :].reshape(256, 256).astype(BF)
        q2_ref[j] = (mm(q, w2_ref[:, :256]) * SCALE).astype(BF)
        kv2_ref[j, :576, :] = kvs_ref[:, 16 * j : 16 * j + 24, :].reshape(576, 512).astype(BF)
        kv2_ref[j, 576:, :] = pad
        jobs.append(
            (
                lambda half, j=j: q2_ref[j, :, half * 128 : half * 128 + 128],
                lambda half, j=j: kv2_ref[j, :, half * 128 : half * 128 + 128],
                lambda half, j=j: kv2_ref[j, :, 256 + half * 128 : 384 + half * 128],
                lambda h: b2_ref[h],
            )
        )
    for j, mixed in enumerate(attend(jobs, (s2_ref, s3_ref))):
        res = bo_ref[4:20, 8 + 16 * j : 24 + 16 * j, :].reshape(256, 256) + mm(mixed, o2_ref[...])
        out = mlp(res, gain_ref[3:4, :], real, ww2_ref[...], wn2_ref[...])
        out_ref[:, 16 * j : 16 * j + 16, :] = out.reshape(16, 16, 256)[:, :, :C].astype(BF)


def swap(low, high, axis):
    count = lax.axis_size(axis)
    even = lax.axis_index(axis) % 2 == 0

    def pairs(first):
        found = []
        for i in range(first, count - 1, 2):
            found += [(i, i + 1), (i + 1, i)]
        return found

    a = lax.ppermute(jnp.where(even, high, low), axis, pairs(0))
    b = lax.ppermute(jnp.where(even, low, high), axis, pairs(1))
    return a, b


def per_device(
    pixels, shift_prenorm, shift_inputs, shift_table, shift_output, shift_postnorm, shift_widen, shift_narrow,
    cross_prenorm, cross_query, cross_keyval, cross_table, cross_output, cross_postnorm, cross_widen, cross_narrow,
):
    ra, rb = swap(pixels[:SHIFT], pixels[SHIFT:], "rows")
    odd = lax.axis_index("rows") % 2 == 1
    top = jnp.where(odd, ra, rb)
    bot = jnp.where(odd, rb, ra)
    sds = jax.ShapeDtypeStruct
    vmem = pl.BlockSpec(memory_space=pltpu.VMEM)
    hbm = pl.BlockSpec(memory_space=pltpu.HBM)
    operands = (
        pixels, shift_table, cross_table,
        shift_prenorm.reshape(1, C), shift_postnorm.reshape(1, C), cross_prenorm.reshape(1, C), cross_postnorm.reshape(1, C),
        shift_inputs, shift_output, shift_widen, shift_narrow.T, cross_query, cross_keyval, cross_output,
        cross_widen, cross_narrow.T,
    )
    strip = (pixels.shape[0], SHIFT, C)
    center, low, high, gains, *made = pl.pallas_call(
        tables_kernel,
        out_shape=(
            sds(pixels.shape, BF), sds(strip, BF), sds(strip, BF), sds((8, 256), F32),
            sds((HEADS, 256, 256), F32), sds((HEADS, 256, KEYS), F32), sds((256, 768), BF), sds((256, 256), BF),
            sds((256, 384), BF), sds((256, 384), BF), sds((256, 768), BF), sds((256, 256), BF), sds((256, 384), BF),
            sds((256, 384), BF),
        ),
        in_specs=[hbm] * 16,
        out_specs=[vmem] * 14,
        scratch_shapes=[pltpu.VMEM(x.shape, x.dtype) for x in (*operands[3:7], *operands[1:3], *operands[7:])]
        + [
            pltpu.SemaphoreType.DMA((16,)),
            pltpu.VMEM((192, 32), F32), pltpu.VMEM((240, 40), F32), pltpu.VMEM((192, 512), F32), pltpu.VMEM((240, 1024), F32),
        ],
        cost_estimate=pl.CostEstimate(flops=200_000_000, bytes_accessed=8_000_000, transcendentals=0),
        compiler_params=pltpu.CompilerParams(vmem_limit_bytes=20 * 2**20),
        name="tables",
    )(*[pltpu.with_memory_space_constraint(x, pltpu.HBM) for x in operands])
    b1, b2, w1, o1, ww1, wn1, w2, o2, ww2, wn2 = made

    strips = [
        jnp.concatenate([top[:, part], own, bot[:, part]], axis=0)
        for part, own in ((slice(0, SHIFT), low), (slice(24, 32), high))
    ]
    ca, cb = swap(strips[0], strips[1], "cols")
    middle = pl.pallas_call(
        middle_kernel,
        out_shape=sds((24, 16, 256), F32),
        in_specs=[vmem] * 9,
        out_specs=vmem,
        scratch_shapes=[
            pltpu.VMEM((2, 16, 16, 256), F32), pltpu.VMEM((2, 192, 256), BF), pltpu.VMEM((2, 256, 512), BF),
            pltpu.VMEM((192, 256), F32), pltpu.VMEM((192, 256), F32),
        ],
        cost_estimate=pl.CostEstimate(flops=2_000_000_000, bytes_accessed=8_000_000, transcendentals=1_000_000),
        compiler_params=pltpu.CompilerParams(vmem_limit_bytes=16 * 2**20),
        name="middle",
    )(center, ra, rb, gains, b1, w1, o1, ww1, wn1)
    return pl.pallas_call(
        main_kernel,
        out_shape=sds(pixels.shape, BF),
        in_specs=[vmem] * 17,
        out_specs=vmem,
        scratch_shapes=[
            pltpu.VMEM((4, 16, 16, 256), F32), pltpu.VMEM((4, 192, 256), BF), pltpu.VMEM((4, 256, 512), BF),
            pltpu.VMEM((192, 256), F32), pltpu.VMEM((192, 256), F32),
            pltpu.VMEM((24, 48, 256), F32), pltpu.VMEM((24, 48, 256), F32), pltpu.VMEM((24, 40, 512), F32),
            pltpu.VMEM((2, 256, 256), BF), pltpu.VMEM((2, KEYS, 512), BF),
            pltpu.VMEM((256, KEYS), F32), pltpu.VMEM((256, KEYS), F32),
        ],
        cost_estimate=pl.CostEstimate(flops=10_000_000_000, bytes_accessed=8_000_000, transcendentals=4_000_000),
        compiler_params=pltpu.CompilerParams(vmem_limit_bytes=32 * 2**20),
        name="blocks",
    )(center, ra, rb, ca, cb, middle, gains, b1, b2, w1, o1, ww1, wn1, w2, o2, ww2, wn2)


def solution(mesh):
    return jax.shard_map(
        per_device,
        mesh=mesh,
        in_specs=(P("rows", "cols", None),) + (P(),) * 15,
        out_specs=P("rows", "cols", None),
        check_vma=False,
    )
```

```python
import jax
import jax.numpy as jnp
from jax import lax
from jax.experimental import pallas as pl
from jax.experimental.pallas import tpu as pltpu
from jax.sharding import PartitionSpec as P

C = 180
HEADS = 6
HEAD_DIM = 30
WIN = 16
SHIFT = 8
PAD = 4
OWIN = 24
EPS = 1e-05
LOG2E = 1.4426950408889634
SCALE = HEAD_DIM ** (-0.5) * LOG2E
LOW = -1e30
FLAG = 180
ONE = 181
KFLAG = 100
KEYS = 640
AHEAD = 4
CROSS_AHEAD = 1
BF = jnp.bfloat16
F32 = jnp.float32


def mm(a, b, dims=((1,), (0,)), precision=None):
    return lax.dot_general(a, b, (dims, ((), ())), preferred_element_type=F32, precision=precision)


NT = ((1,), (1,))


def lanes(shape):
    return lax.broadcasted_iota(jnp.int32, shape, len(shape) - 1)


def rows_of(shape):
    return lax.broadcasted_iota(jnp.int32, shape, len(shape) - 2)


def place(dst_ref, src, row, col):
    dst_ref[row : row + src.shape[0], col : col + src.shape[1]] = src


def exact_parts(x):
    first = x.astype(BF)
    rest = x - first.astype(F32)
    second = rest.astype(BF)
    return first, second, (rest - second.astype(F32)).astype(BF)


def shear(table_ref, flip, side, pick, amount, bits):
    top = HEADS * side
    y = None
    for part in exact_parts(table_ref[...] * LOG2E):
        turned = [mm(flip, part[h * side : (h + 1) * side], NT) for h in range(HEADS)]
        term = mm(jnp.concatenate(turned, axis=0).astype(BF), pick)
        y = term if y is None else y + term
    for bit in bits:
        y = jnp.where((amount & bit) != 0, pltpu.roll(y, top - bit, 0), y)
    return y


def tables_kernel(*refs):
    sources = refs[:16]
    (
        cen_ref, low_ref, high_ref, gain_ref, b1_ref, b2_ref, w1_ref, o1_ref, ww1_ref, wn1_ref, w2_ref, o2_ref, ww2_ref, wn2_ref,
        g0_ref, g1_ref, g2_ref, g3_ref, st_ref, ct_ref, wi_ref, wo_ref, ww_ref, wn_ref, cq_ref, ckv_ref, co_ref, cw_ref, cn_ref,
        sems, t1_ref, t2_ref, e1_ref, e2_ref,
    ) = refs[16:]
    targets = (
        cen_ref, st_ref, ct_ref, g0_ref, g1_ref, g2_ref, g3_ref, wi_ref, wo_ref, ww_ref, wn_ref, cq_ref, ckv_ref, co_ref,
        cw_ref, cn_ref,
    )
    copies = [pltpu.make_async_copy(a, b, sems.at[i]) for i, (a, b) in enumerate(zip(sources, targets))]
    for copy in copies:
        copy.start()

    def zeros(ref):
        ref[...] = jnp.zeros(ref.shape, ref.dtype)

    r = rows_of((256, 768))
    c = lanes((256, 768))
    base = jnp.where((r == FLAG) & ((c == 256 + KFLAG) | (c == 384 + KFLAG)), LOW, 0.0)
    base = jnp.where((r == ONE) & ((c == KFLAG) | (c == 128 + KFLAG)), 1.0, base)
    w1_ref[...] = base.astype(BF)
    w2_ref[...] = jnp.where(r == ONE, base, 0.0).astype(BF)
    for ref in (o1_ref, ww1_ref, wn1_ref, o2_ref, ww2_ref, wn2_ref, gain_ref, t1_ref, t2_ref):
        zeros(ref)
    for h in range(HEADS):
        b2_ref[h, :, 512:640] = jnp.zeros((256, 128), F32)
    for copy in copies[:3]:
        copy.wait()
    low_ref[...] = cen_ref[:, :SHIFT]
    high_ref[...] = cen_ref[:, 24:]
    for h in range(HEADS):
        t1_ref[h * 32 : h * 32 + 31, :31] = st_ref[h]
        t2_ref[h * 40 : h * 40 + 39, :39] = ct_ref[h]
    flip = jnp.where(rows_of((32, 32)) == lanes((32, 32)), 1.0, 0.0).astype(BF)
    pick = jnp.where(lanes((32, 512)) // 16 == 30 - rows_of((32, 512)), 1.0, 0.0).astype(BF)
    amount = 15 - lanes((192, 512)) % 16
    e1_ref[...] = shear(t1_ref, flip, 32, pick, amount, (8, 4, 2, 1))
    for h in range(HEADS):
        for qy in range(WIN):
            b1_ref[h, qy * 16 : qy * 16 + 16, :] = e1_ref[h * 32 : h * 32 + 16, (15 - qy) * 16 : (15 - qy) * 16 + 256]
    flip = jnp.where(rows_of((40, 40)) == 38 - lanes((40, 40)), 1.0, 0.0).astype(BF)
    lane = lanes((40, 1024))
    row = rows_of((40, 1024))
    pick = jnp.where((lane >= row * 24) & (lane < row * 24 + 24), 1.0, 0.0).astype(BF)
    lane1 = lanes((1, 1024)).astype(F32)
    kx = lane1 - 24.0 * jnp.floor((lane1 + 0.5) * (1.0 / 24.0))
    amount = jnp.broadcast_to(23 - kx.astype(jnp.int32), (240, 1024))
    e2_ref[...] = shear(t2_ref, flip, 40, pick, amount, (16, 8, 4, 2, 1))
    for h in range(HEADS):
        for qy in range(WIN):
            b2_ref[h, qy * 16 : qy * 16 + 16, :576] = e2_ref[h * 40 : h * 40 + 16, (15 - qy) * 24 : (15 - qy) * 24 + 576]
    for copy in copies[3:]:
        copy.wait()
    for k in range(6):
        place(w1_ref, wi_ref[:, 90 * k : 90 * k + 90], 0, 128 * k)
    for k in range(2):
        place(w2_ref, cq_ref[:, 90 * k : 90 * k + 90], 0, 128 * k)
    for k in range(4):
        place(w2_ref, ckv_ref[:, 90 * k : 90 * k + 90], 0, 256 + 128 * k)
    for dst, src in ((o1_ref, wo_ref), (o2_ref, co_ref)):
        place(dst, src[:90], 0, 0)
        place(dst, src[90:], 128, 0)
    for dst, src in ((ww1_ref, ww_ref), (wn1_ref, wn_ref), (ww2_ref, cw_ref), (wn2_ref, cn_ref)):
        place(dst, src[...], 0, 0)
    for i, src in enumerate((g0_ref, g1_ref, g2_ref, g3_ref)):
        gain_ref[i : i + 1, :C] = src[...]


def norm(x, gain, real):
    x0 = x[:, :128]
    x1 = jnp.where(real, x[:, 128:], 0.0)
    mean = jnp.sum(x0 + x1, axis=-1, keepdims=True) * (1.0 / C)
    c0 = x0 - mean
    c1 = jnp.where(real, x1 - mean, 0.0)
    spread = jnp.sum(c0 * c0 + c1 * c1, axis=-1, keepdims=True) * (1.0 / C)
    inv = lax.rsqrt(spread + EPS)
    return c0 * inv * gain[:, :128], c1 * inv * gain[:, 128:]


def gelu(x):
    return 0.5 * x * (1.0 + lax.erf(x * 0.7071067811865476))


def mlp(res, gain, real, widen, narrow):
    n0, n1 = norm(res, gain, real)
    normed = jnp.concatenate([n0, n1], axis=1).astype(BF)
    hidden = gelu(mm(normed, widen)).astype(BF)
    return res + mm(hidden, narrow, NT)


def attend(jobs, s_refs):
    lane = lanes((1, 128))
    order = [(job, h) for h in range(HEADS) for job in range(len(jobs))]

    def start(n):
        job, h = order[n]
        half, t = divmod(h, 3)
        queries, keys, _, bias = jobs[job]
        own = ((lane >= 30 * t) & (lane < 30 * t + 30)) | (lane == KFLAG)
        scores = mm(queries(half) * jnp.where(own, 1.0, 0.0).astype(BF), keys(half), NT) + bias(h)
        s_refs[n % s_refs.shape[0]] = scores
        return jnp.max(scores, axis=-1, keepdims=True)

    mixed = [[None, None] for _ in jobs]
    depth = s_refs.shape[0] - 1
    peaks = [start(n) for n in range(depth)]
    for n, (job, h) in enumerate(order):
        if n + depth < len(order):
            peaks.append(start(n + depth))
        half, t = divmod(h, 3)
        weights = jnp.exp2(s_refs[n % (depth + 1)] - peaks[n]).astype(BF)
        out = mm(weights, jobs[job][2](half))
        out = out[:, :128] / out[:, 128:]
        mixed[job][half] = out if t == 0 else jnp.where(lane >= 30 * t, out, mixed[job][half])
    return [jnp.concatenate(pair, axis=1).astype(BF) for pair in mixed]


def shifted_windows(windows, x_ref, gain_ref, b1_ref, w1_ref, o1_ref, ww1_ref, wn1_ref, q_ref, kv_ref, s_refs):
    real = lanes((1, 128)) < C - 128
    count = len(windows)
    x = x_ref[...].reshape(count * 256, 256)
    n0, n1 = norm(x, gain_ref[0:1, :], real)
    n1 = jnp.where(real, n1, x[:, 128:])
    normed = jnp.concatenate([n0, n1], axis=1).astype(BF)
    wanted = [slice(slot * 256 + 64 * (1 - i), slot * 256 + 64 * (1 - i) + 192) for slot, i in windows]
    kv = mm(normed, w1_ref[:, 256:]).astype(BF).reshape(count, 256, 512)
    ones = jnp.ones((count, 256, 128), BF)
    kv_ref[:, :, :384] = kv[:, :, :384]
    kv_ref[:, :, 384:512] = ones
    kv_ref[:, :, 512:640] = kv[:, :, 384:]
    kv_ref[:, :, 640:] = ones
    q = mm(jnp.concatenate([normed[rows] for rows in wanted], axis=0), w1_ref[:, :256])
    q_ref[...] = (q * SCALE).astype(BF).reshape(count, 192, 256)
    jobs = []
    for slot, i in windows:
        first = 64 * (1 - i)
        jobs.append(
            (
                lambda half, slot=slot: q_ref[slot, :, half * 128 : half * 128 + 128],
                lambda half, slot=slot: kv_ref[slot, :, half * 128 : half * 128 + 128],
                lambda half, slot=slot: kv_ref[slot, :, 256 + half * 256 : 512 + half * 256],
                lambda h, first=first: b1_ref[h, first : first + 192, :],
            )
        )
    mixed = jnp.concatenate(attend(jobs, s_refs), axis=0)
    x = x_ref[...].reshape(count * 256, 256)
    res = jnp.concatenate([x[rows] for rows in wanted], axis=0) + mm(mixed, o1_ref[...])
    out = mlp(res, gain_ref[1:2, :], real, ww1_ref[...], wn1_ref[...]).astype(BF).astype(F32)
    return [out[192 * k : 192 * k + 192].reshape(12, 16, 256) for k in range(count)]


def put(x_ref, slot, y0, x0, piece, flag):
    lane1 = lanes((1, 128))
    ny, nx = piece.shape[0], piece.shape[1]
    x_ref[slot, y0 : y0 + ny, x0 : x0 + nx, 128:] = jnp.broadcast_to(
        jnp.where(lane1 == FLAG - 128, flag, jnp.where(lane1 == ONE - 128, 1.0, 0.0)), (ny, nx, 128)
    )
    x_ref[slot, y0 : y0 + ny, x0 : x0 + nx, :C] = piece.astype(F32)


def edges():
    row, col = lax.axis_index("rows"), lax.axis_index("cols")
    return row, col, lax.axis_size("rows") - 1, lax.axis_size("cols") - 1


def flag_of(condition):
    return jnp.where(condition, 1.0, 0.0)


def middle_kernel(
    cen_ref, ra_ref, rb_ref, gain_ref, b1_ref, w1_ref, o1_ref, ww1_ref, wn1_ref, out_ref, x_ref, q_ref, kv_ref, s_ref
):
    row, _, last_row, _ = edges()
    odd = lax.rem(row, 2) == 1
    top = jnp.where(odd, ra_ref[:, 8:24], rb_ref[:, 8:24])
    bot = jnp.where(odd, rb_ref[:, 8:24], ra_ref[:, 8:24])
    put(x_ref, 0, 0, 0, top, flag_of(row == 0))
    put(x_ref, 0, 8, 0, cen_ref[:8, 8:24], 0.0)
    put(x_ref, 1, 0, 0, cen_ref[8:, 8:24], 0.0)
    put(x_ref, 1, 8, 0, bot, flag_of(row == last_row))
    outs = shifted_windows(
        [(0, 0), (1, 1)], x_ref, gain_ref, b1_ref, w1_ref, o1_ref, ww1_ref, wn1_ref, q_ref, kv_ref, s_ref
    )
    out_ref[:12] = outs[0]
    out_ref[12:] = outs[1]


def main_kernel(
    cen_ref, ra_ref, rb_ref, ca_ref, cb_ref, mid_ref, gain_ref,
    b1_ref, b2_ref, w1_ref, o1_ref, ww1_ref, wn1_ref, w2_ref, o2_ref, ww2_ref, wn2_ref,
    out_ref,
    x_ref, q_ref, kv_ref, s_ref, bo_ref, a3_ref, kvs_ref, q2_ref, kv2_ref, s2_ref,
):
    row, col, last_row, last_col = edges()
    real = lanes((1, 128)) < C - 128
    one1 = jnp.where(lanes((1, 128)) == ONE - 128, 1.0, 0.0)
    row_odd = lax.rem(row, 2) == 1
    col_odd = lax.rem(col, 2) == 1
    out_top = flag_of(row == 0)
    out_bot = flag_of(row == last_row)
    out_lef = flag_of(col == 0)
    out_rig = flag_of(col == last_col)
    top = jnp.where(row_odd, ra_ref[...], rb_ref[...])
    bot = jnp.where(row_odd, rb_ref[...], ra_ref[...])
    lef = jnp.where(col_odd, ca_ref[...], cb_ref[...])
    rig = jnp.where(col_odd, cb_ref[...], ca_ref[...])
    both = jnp.maximum
    put(x_ref, 0, 0, 0, lef[:8], both(out_top, out_lef))
    put(x_ref, 0, 0, 8, top[:, :8], out_top)
    put(x_ref, 0, 8, 0, lef[8:16], out_lef)
    put(x_ref, 0, 8, 8, cen_ref[:8, :8], 0.0)
    put(x_ref, 1, 0, 0, lef[16:24], out_lef)
    put(x_ref, 1, 0, 8, cen_ref[8:, :8], 0.0)
    put(x_ref, 1, 8, 0, lef[24:], both(out_bot, out_lef))
    put(x_ref, 1, 8, 8, bot[:, :8], out_bot)
    put(x_ref, 2, 0, 0, top[:, 24:], out_top)
    put(x_ref, 2, 0, 8, rig[:8], both(out_top, out_rig))
    put(x_ref, 2, 8, 0, cen_ref[:8, 24:], 0.0)
    put(x_ref, 2, 8, 8, rig[8:16], out_rig)
    put(x_ref, 3, 0, 0, cen_ref[8:, 24:], 0.0)
    put(x_ref, 3, 0, 8, rig[16:24], out_rig)
    put(x_ref, 3, 8, 0, bot[:, 24:], out_bot)
    put(x_ref, 3, 8, 8, rig[24:], both(out_bot, out_rig))

    outs = shifted_windows(
        [(0, 0), (1, 1), (2, 0), (3, 1)],
        x_ref, gain_ref, b1_ref, w1_ref, o1_ref, ww1_ref, wn1_ref, q_ref, kv_ref, s_ref,
    )
    bo_ref[:12, :16] = outs[0]
    bo_ref[12:, :16] = outs[1]
    bo_ref[:, 16:32] = mid_ref[...]
    bo_ref[:12, 32:] = outs[2]
    bo_ref[12:, 32:] = outs[3]

    n0, n1 = norm(bo_ref[...].reshape(24 * 48, 256), gain_ref[2:3, :], real)
    a3_ref[:, :, :128] = n0.reshape(24, 48, 128)
    a3_ref[:, :, 128:] = (n1 + one1).reshape(24, 48, 128)
    base = jnp.where(lanes((1, 1, 256)) == ONE, 1.0, 0.0)

    @pl.when(row == 0)
    def _():
        a3_ref[:4] = jnp.broadcast_to(base, (4, 48, 256))

    @pl.when(row == last_row)
    def _():
        a3_ref[20:] = jnp.broadcast_to(base, (4, 48, 256))

    @pl.when(col == 0)
    def _():
        a3_ref[:, :8] = jnp.broadcast_to(base, (24, 8, 256))

    @pl.when(col == last_col)
    def _():
        a3_ref[:, 40:] = jnp.broadcast_to(base, (24, 8, 256))

    kvs_ref[...] = mm(a3_ref[:, 4:44, :].reshape(960, 256).astype(BF), w2_ref[:, 256:]).reshape(24, 40, 512)
    lane = lanes((64, 640))
    pad = jnp.where((lane == KFLAG) | (lane == 128 + KFLAG), LOW, 0.0).astype(BF)
    jobs = []
    for j in range(2):
        q = a3_ref[4:20, 8 + 16 * j : 24 + 16 * j, :].reshape(256, 256).astype(BF)
        q2_ref[j] = (mm(q, w2_ref[:, :256]) * SCALE).astype(BF)
        kv = kvs_ref[:, 16 * j : 16 * j + 24, :].reshape(576, 512).astype(BF)
        kv2_ref[j, :576, :384] = kv[:, :384]
        kv2_ref[j, :576, 512:640] = kv[:, 384:]
        kv2_ref[j, 576:, :640] = pad
        kv2_ref[j, :, 384:512] = jnp.ones((KEYS, 128), BF)
        kv2_ref[j, :, 640:] = jnp.ones((KEYS, 128), BF)
        jobs.append(
            (
                lambda half, j=j: q2_ref[j, :, half * 128 : half * 128 + 128],
                lambda half, j=j: kv2_ref[j, :, half * 128 : half * 128 + 128],
                lambda half, j=j: kv2_ref[j, :, 256 + half * 256 : 512 + half * 256],
                lambda h: b2_ref[h],
            )
        )
    mixed = jnp.concatenate(attend(jobs, s2_ref), axis=0)
    own = [bo_ref[4:20, 8 + 16 * j : 24 + 16 * j, :].reshape(256, 256) for j in range(2)]
    res = jnp.concatenate(own, axis=0) + mm(mixed, o2_ref[...])
    out = mlp(res, gain_ref[3:4, :], real, ww2_ref[...], wn2_ref[...])
    for j in range(2):
        part = out[256 * j : 256 * j + 256].reshape(16, 16, 256)
        out_ref[:, 16 * j : 16 * j + 16, :] = part[:, :, :C].astype(BF)


def swap(low, high, axis):
    count = lax.axis_size(axis)
    even = lax.axis_index(axis) % 2 == 0

    def pairs(first):
        found = []
        for i in range(first, count - 1, 2):
            found += [(i, i + 1), (i + 1, i)]
        return found

    a = lax.ppermute(jnp.where(even, high, low), axis, pairs(0))
    b = lax.ppermute(jnp.where(even, low, high), axis, pairs(1))
    return a, b


def per_device(
    pixels, shift_prenorm, shift_inputs, shift_table, shift_output, shift_postnorm, shift_widen, shift_narrow,
    cross_prenorm, cross_query, cross_keyval, cross_table, cross_output, cross_postnorm, cross_widen, cross_narrow,
):
    ra, rb = swap(pixels[:SHIFT], pixels[SHIFT:], "rows")
    odd = lax.axis_index("rows") % 2 == 1
    top = jnp.where(odd, ra, rb)
    bot = jnp.where(odd, rb, ra)
    sds = jax.ShapeDtypeStruct
    vmem = pl.BlockSpec(memory_space=pltpu.VMEM)
    hbm = pl.BlockSpec(memory_space=pltpu.HBM)
    operands = (
        pixels, shift_table, cross_table,
        shift_prenorm.reshape(1, C), shift_postnorm.reshape(1, C), cross_prenorm.reshape(1, C), cross_postnorm.reshape(1, C),
        shift_inputs, shift_output, shift_widen, shift_narrow.T, cross_query, cross_keyval, cross_output,
        cross_widen, cross_narrow.T,
    )
    strip = (pixels.shape[0], SHIFT, C)
    center, low, high, gains, *made = pl.pallas_call(
        tables_kernel,
        out_shape=(
            sds(pixels.shape, BF), sds(strip, BF), sds(strip, BF), sds((8, 256), F32),
            sds((HEADS, 256, 256), F32), sds((HEADS, 256, KEYS), F32), sds((256, 768), BF), sds((256, 256), BF),
            sds((256, 384), BF), sds((256, 384), BF), sds((256, 768), BF), sds((256, 256), BF), sds((256, 384), BF),
            sds((256, 384), BF),
        ),
        in_specs=[hbm] * 16,
        out_specs=[vmem] * 14,
        scratch_shapes=[pltpu.VMEM(x.shape, x.dtype) for x in (*operands[3:7], *operands[1:3], *operands[7:])]
        + [
            pltpu.SemaphoreType.DMA((16,)),
            pltpu.VMEM((192, 32), F32), pltpu.VMEM((240, 40), F32), pltpu.VMEM((192, 512), F32), pltpu.VMEM((240, 1024), F32),
        ],
        cost_estimate=pl.CostEstimate(flops=200_000_000, bytes_accessed=8_000_000, transcendentals=0),
        compiler_params=pltpu.CompilerParams(vmem_limit_bytes=20 * 2**20),
        name="tables",
    )(*[pltpu.with_memory_space_constraint(x, pltpu.HBM) for x in operands])
    b1, b2, w1, o1, ww1, wn1, w2, o2, ww2, wn2 = made

    strips = [
        jnp.concatenate([top[:, part], own, bot[:, part]], axis=0)
        for part, own in ((slice(0, SHIFT), low), (slice(24, 32), high))
    ]
    ca, cb = swap(strips[0], strips[1], "cols")
    middle = pl.pallas_call(
        middle_kernel,
        out_shape=sds((24, 16, 256), F32),
        in_specs=[vmem] * 9,
        out_specs=vmem,
        scratch_shapes=[
            pltpu.VMEM((2, 16, 16, 256), F32), pltpu.VMEM((2, 192, 256), BF), pltpu.VMEM((2, 256, 768), BF),
            pltpu.VMEM((AHEAD + 1, 192, 256), F32),
        ],
        cost_estimate=pl.CostEstimate(flops=2_000_000_000, bytes_accessed=8_000_000, transcendentals=1_000_000),
        compiler_params=pltpu.CompilerParams(vmem_limit_bytes=16 * 2**20),
        name="middle",
    )(center, ra, rb, gains, b1, w1, o1, ww1, wn1)
    return pl.pallas_call(
        main_kernel,
        out_shape=sds(pixels.shape, BF),
        in_specs=[vmem] * 17,
        out_specs=vmem,
        scratch_shapes=[
            pltpu.VMEM((4, 16, 16, 256), F32), pltpu.VMEM((4, 192, 256), BF), pltpu.VMEM((4, 256, 768), BF),
            pltpu.VMEM((AHEAD + 1, 192, 256), F32),
            pltpu.VMEM((24, 48, 256), F32), pltpu.VMEM((24, 48, 256), F32), pltpu.VMEM((24, 40, 512), F32),
            pltpu.VMEM((2, 256, 256), BF), pltpu.VMEM((2, KEYS, 768), BF),
            pltpu.VMEM((CROSS_AHEAD + 1, 256, KEYS), F32),
        ],
        cost_estimate=pl.CostEstimate(flops=10_000_000_000, bytes_accessed=8_000_000, transcendentals=4_000_000),
        compiler_params=pltpu.CompilerParams(vmem_limit_bytes=32 * 2**20),
        name="blocks",
    )(center, ra, rb, ca, cb, middle, gains, b1, b2, w1, o1, ww1, wn1, w2, o2, ww2, wn2)


def solution(mesh):
    return jax.shard_map(
        per_device,
        mesh=mesh,
        in_specs=(P("rows", "cols", None),) + (P(),) * 15,
        out_specs=P("rows", "cols", None),
        check_vma=False,
    )
```

```python
import jax
import jax.numpy as jnp
from jax import lax
from jax.experimental import pallas as pl
from jax.experimental.pallas import tpu as pltpu
from jax.sharding import PartitionSpec as P

C = 180
HEADS = 6
HEAD_DIM = 30
WIN = 16
SHIFT = 8
PAD = 4
OWIN = 24
EPS = 1e-05
LOG2E = 1.4426950408889634
SCALE = HEAD_DIM ** (-0.5) * LOG2E
HALF_ROOT = 0.7071067811865476
LOW = -1e30
FLAG = 180
ONE = 181
KFLAG = 100
KEYS = 512
REST = 64
AHEAD = 4
CROSS_AHEAD = 1
BF = jnp.bfloat16
F32 = jnp.float32


def mm(a, b, dims=((1,), (0,)), precision=None):
    return lax.dot_general(a, b, (dims, ((), ())), preferred_element_type=F32, precision=precision)


NT = ((1,), (1,))


def lanes(shape):
    return lax.broadcasted_iota(jnp.int32, shape, len(shape) - 1)


def rows_of(shape):
    return lax.broadcasted_iota(jnp.int32, shape, len(shape) - 2)


def place(dst_ref, src, row, col):
    dst_ref[row : row + src.shape[0], col : col + src.shape[1]] = src


def exact_parts(x):
    first = x.astype(BF)
    rest = x - first.astype(F32)
    second = rest.astype(BF)
    return first, second, (rest - second.astype(F32)).astype(BF)


def shear(table_ref, flip, side, pick, amount, bits):
    top = HEADS * side
    y = None
    for part in exact_parts(table_ref[...] * LOG2E):
        turned = [mm(flip, part[h * side : (h + 1) * side], NT) for h in range(HEADS)]
        term = mm(jnp.concatenate(turned, axis=0).astype(BF), pick)
        y = term if y is None else y + term
    for bit in bits:
        y = jnp.where((amount & bit) != 0, pltpu.roll(y, top - bit, 0), y)
    return y


def tables_kernel(*refs):
    sources = refs[:16]
    (
        cen_ref, low_ref, high_ref, gain_ref, b1_ref, b2_ref, br_ref, w1_ref, o1_ref, ww1_ref, wn1_ref, w2_ref, o2_ref, ww2_ref, wn2_ref,
        g0_ref, g1_ref, g2_ref, g3_ref, st_ref, ct_ref, wi_ref, wo_ref, ww_ref, wn_ref, cq_ref, ckv_ref, co_ref, cw_ref, cn_ref,
        sems, t1_ref, t2_ref, e1_ref, e2_ref,
    ) = refs[16:]
    targets = (
        cen_ref, st_ref, ct_ref, g0_ref, g1_ref, g2_ref, g3_ref, wi_ref, wo_ref, ww_ref, wn_ref, cq_ref, ckv_ref, co_ref,
        cw_ref, cn_ref,
    )
    copies = [pltpu.make_async_copy(a, b, sems.at[i]) for i, (a, b) in enumerate(zip(sources, targets))]
    for copy in copies:
        copy.start()

    def zeros(ref):
        ref[...] = jnp.zeros(ref.shape, ref.dtype)

    r = rows_of((256, 768))
    c = lanes((256, 768))
    base = jnp.where((r == FLAG) & ((c == 256 + KFLAG) | (c == 384 + KFLAG)), LOW, 0.0)
    base = jnp.where((r == ONE) & ((c == KFLAG) | (c == 128 + KFLAG)), 1.0, base)
    w1_ref[...] = base.astype(BF)
    w2_ref[...] = jnp.where(r == ONE, base, 0.0).astype(BF)
    for ref in (o1_ref, ww1_ref, wn1_ref, o2_ref, ww2_ref, wn2_ref, gain_ref, t1_ref, t2_ref):
        zeros(ref)
    br_ref[...] = jnp.full(br_ref.shape, LOW, F32)
    for copy in copies[:3]:
        copy.wait()
    low_ref[...] = cen_ref[:, :SHIFT]
    high_ref[...] = cen_ref[:, 24:]
    for h in range(HEADS):
        t1_ref[h * 32 : h * 32 + 31, :31] = st_ref[h]
        t2_ref[h * 40 : h * 40 + 39, :39] = ct_ref[h]
    flip = jnp.where(rows_of((32, 32)) == lanes((32, 32)), 1.0, 0.0).astype(BF)
    pick = jnp.where(lanes((32, 512)) // 16 == 30 - rows_of((32, 512)), 1.0, 0.0).astype(BF)
    amount = 15 - lanes((192, 512)) % 16
    e1_ref[...] = shear(t1_ref, flip, 32, pick, amount, (8, 4, 2, 1))
    for h in range(HEADS):
        for qy in range(WIN):
            b1_ref[h, qy * 16 : qy * 16 + 16, :] = e1_ref[h * 32 : h * 32 + 16, (15 - qy) * 16 : (15 - qy) * 16 + 256]
    flip = jnp.where(rows_of((40, 40)) == 38 - lanes((40, 40)), 1.0, 0.0).astype(BF)
    lane = lanes((40, 1024))
    row = rows_of((40, 1024))
    pick = jnp.where((lane >= row * 24) & (lane < row * 24 + 24), 1.0, 0.0).astype(BF)
    lane1 = lanes((1, 1024)).astype(F32)
    kx = lane1 - 24.0 * jnp.floor((lane1 + 0.5) * (1.0 / 24.0))
    amount = jnp.broadcast_to(23 - kx.astype(jnp.int32), (240, 1024))
    e2_ref[...] = shear(t2_ref, flip, 40, pick, amount, (16, 8, 4, 2, 1))
    for h in range(HEADS):
        for qy in range(WIN):
            bias = e2_ref[h * 40 : h * 40 + 16, (15 - qy) * 24 : (15 - qy) * 24 + 576]
            b2_ref[h, qy * 16 : qy * 16 + 16, :] = bias[:, :KEYS]
            br_ref[h // 3, qy * 16 : qy * 16 + 16, h % 3 * REST : h % 3 * REST + REST] = bias[:, KEYS:]
    for copy in copies[3:]:
        copy.wait()
    for k in range(6):
        place(w1_ref, wi_ref[:, 90 * k : 90 * k + 90], 0, 128 * k)
    for k in range(2):
        place(w2_ref, cq_ref[:, 90 * k : 90 * k + 90], 0, 128 * k)
    for k in range(4):
        place(w2_ref, ckv_ref[:, 90 * k : 90 * k + 90], 0, 256 + 128 * k)
    for dst, src in ((o1_ref, wo_ref), (o2_ref, co_ref)):
        place(dst, src[:90], 0, 0)
        place(dst, src[90:], 128, 0)
    for dst, src in ((ww1_ref, ww_ref), (wn1_ref, wn_ref), (ww2_ref, cw_ref), (wn2_ref, cn_ref)):
        place(dst, src[...], 0, 0)
    for i, src in enumerate((g0_ref, g1_ref, g2_ref, g3_ref)):
        gain_ref[i : i + 1, :C] = src[...] * (HALF_ROOT if i % 2 else 1.0)


def norm(x, gain, real):
    x0 = x[:, :128]
    x1 = jnp.where(real, x[:, 128:], 0.0)
    mean = jnp.sum(x0 + x1, axis=-1, keepdims=True) * (1.0 / C)
    c0 = x0 - mean
    c1 = jnp.where(real, x1 - mean, 0.0)
    spread = jnp.sum(c0 * c0 + c1 * c1, axis=-1, keepdims=True) * (1.0 / C)
    inv = lax.rsqrt(spread + EPS)
    return c0 * inv * gain[:, :128], c1 * inv * gain[:, 128:]


def mlp(res, gain, real, widen, narrow):
    n0, n1 = norm(res, gain, real)
    normed = jnp.concatenate([n0, n1], axis=1).astype(BF)
    y = mm(normed, widen)
    hidden = (y + y * lax.erf(y)).astype(BF)
    return res + mm(hidden, narrow, NT) * HALF_ROOT


def attend(jobs, s_refs):
    lane = lanes((1, 128))
    order = [(job, h) for h in range(HEADS) for job in range(len(jobs))]

    def start(n):
        job, h = order[n]
        half, t = divmod(h, 3)
        queries, keys, _, bias = jobs[job]
        own = ((lane >= 30 * t) & (lane < 30 * t + 30)) | (lane == KFLAG)
        scores = mm(queries(half) * jnp.where(own, 1.0, 0.0).astype(BF), keys(half), NT) + bias(h)
        s_refs[n % s_refs.shape[0]] = scores
        return jnp.max(scores, axis=-1, keepdims=True)

    mixed = [[None, None] for _ in jobs]
    depth = s_refs.shape[0] - 1
    peaks = [start(n) for n in range(depth)]
    for n, (job, h) in enumerate(order):
        if n + depth < len(order):
            peaks.append(start(n + depth))
        half, t = divmod(h, 3)
        weights = jnp.exp2(s_refs[n % (depth + 1)] - peaks[n]).astype(BF)
        out = mm(weights, jobs[job][2](half))
        out = out[:, :128] / out[:, 128:]
        mixed[job][half] = out if t == 0 else jnp.where(lane >= 30 * t, out, mixed[job][half])
    return [jnp.concatenate(pair, axis=1).astype(BF) for pair in mixed]


def cross_attend(count, q_ref, kv_ref, kr_ref, vr_ref, b2_ref, br_ref, s_ref, sr_ref):
    lane = lanes((1, 128))
    lane2 = lanes((1, 256)) % 128
    low = lane < REST
    order = [(j, h) for h in range(HEADS) for j in range(count)]
    depth = s_ref.shape[0] - 1

    def start(n):
        j, h = order[n]
        half, t = divmod(h, 3)
        part = slice(half * 128, half * 128 + 128)
        queries, keys = q_ref[j, :, part], kv_ref[j, :, part]
        if t == 0:
            sr_ref[j, half] = mm(queries, kr_ref[j, half], NT) + br_ref[half]
        own = (lane >= 30 * t) & (lane < 30 * t + 30)
        scores = mm(queries * jnp.where(own, 1.0, 0.0).astype(BF), keys, NT) + b2_ref[h]
        s_ref[n % (depth + 1)] = scores
        rest = sr_ref[j, half, :, t // 2 * 128 : t // 2 * 128 + 128]
        top = jnp.where(~low if t == 1 else low, rest, LOW)
        for k in range(4):
            top = jnp.maximum(top, scores[:, 128 * k : 128 * k + 128])
        return jnp.max(top, axis=-1, keepdims=True)

    peaks = [start(n) for n in range(depth)]
    total = {}
    mixed = [[None, None] for _ in range(count)]
    for n, (j, h) in enumerate(order):
        if n + depth < len(order):
            peaks.append(start(n + depth))
        half, t = divmod(h, 3)
        weights = jnp.exp2(s_ref[n % (depth + 1)] - peaks[n]).astype(BF)
        out = mm(weights, kv_ref[j, :, 256 + half * 256 : 512 + half * 256])
        total[j] = out if t == 0 else jnp.where(lane2 >= 30 * t, out, total[j])
        if t == 2:
            first = jnp.where(low, peaks[n - 2 * count], peaks[n - count])
            rest = [jnp.exp2(sr_ref[j, half, :, :128] - first), jnp.exp2(sr_ref[j, half, :, 128:] - peaks[n])]
            out = total[j] + mm(jnp.concatenate(rest, axis=1).astype(BF), vr_ref[j, half])
            mixed[j][half] = out[:, :128] / out[:, 128:]
    return [jnp.concatenate(pair, axis=1).astype(BF) for pair in mixed]


def shifted_windows(windows, x_ref, gain_ref, b1_ref, w1_ref, o1_ref, ww1_ref, wn1_ref, q_ref, kv_ref, s_refs):
    real = lanes((1, 128)) < C - 128
    count = len(windows)
    x = x_ref[...].reshape(count * 256, 256)
    n0, n1 = norm(x, gain_ref[0:1, :], real)
    n1 = jnp.where(real, n1, x[:, 128:])
    normed = jnp.concatenate([n0, n1], axis=1).astype(BF)
    wanted = [slice(slot * 256 + 64 * (1 - i), slot * 256 + 64 * (1 - i) + 192) for slot, i in windows]
    kv = mm(normed, w1_ref[:, 256:]).astype(BF).reshape(count, 256, 512)
    ones = jnp.ones((count, 256, 128), BF)
    kv_ref[:, :, :384] = kv[:, :, :384]
    kv_ref[:, :, 384:512] = ones
    kv_ref[:, :, 512:640] = kv[:, :, 384:]
    kv_ref[:, :, 640:] = ones
    q = mm(jnp.concatenate([normed[rows] for rows in wanted], axis=0), w1_ref[:, :256])
    q_ref[...] = (q * SCALE).astype(BF).reshape(count, 192, 256)
    jobs = []
    for slot, i in windows:
        first = 64 * (1 - i)
        jobs.append(
            (
                lambda half, slot=slot: q_ref[slot, :, half * 128 : half * 128 + 128],
                lambda half, slot=slot: kv_ref[slot, :, half * 128 : half * 128 + 128],
                lambda half, slot=slot: kv_ref[slot, :, 256 + half * 256 : 512 + half * 256],
                lambda h, first=first: b1_ref[h, first : first + 192, :],
            )
        )
    mixed = jnp.concatenate(attend(jobs, s_refs), axis=0)
    x = x_ref[...].reshape(count * 256, 256)
    res = jnp.concatenate([x[rows] for rows in wanted], axis=0) + mm(mixed, o1_ref[...])
    out = mlp(res, gain_ref[1:2, :], real, ww1_ref[...], wn1_ref[...]).astype(BF).astype(F32)
    return [out[192 * k : 192 * k + 192].reshape(12, 16, 256) for k in range(count)]


def put(x_ref, slot, y0, x0, piece, flag):
    lane1 = lanes((1, 128))
    ny, nx = piece.shape[0], piece.shape[1]
    x_ref[slot, y0 : y0 + ny, x0 : x0 + nx, 128:] = jnp.broadcast_to(
        jnp.where(lane1 == FLAG - 128, flag, jnp.where(lane1 == ONE - 128, 1.0, 0.0)), (ny, nx, 128)
    )
    x_ref[slot, y0 : y0 + ny, x0 : x0 + nx, :C] = piece.astype(F32)


def edges():
    row, col = lax.axis_index("rows"), lax.axis_index("cols")
    return row, col, lax.axis_size("rows") - 1, lax.axis_size("cols") - 1


def flag_of(condition):
    return jnp.where(condition, 1.0, 0.0)


def middle_kernel(
    cen_ref, ra_ref, rb_ref, gain_ref, b1_ref, w1_ref, o1_ref, ww1_ref, wn1_ref, out_ref, x_ref, q_ref, kv_ref, s_ref
):
    row, _, last_row, _ = edges()
    odd = lax.rem(row, 2) == 1
    top = jnp.where(odd, ra_ref[:, 8:24], rb_ref[:, 8:24])
    bot = jnp.where(odd, rb_ref[:, 8:24], ra_ref[:, 8:24])
    put(x_ref, 0, 0, 0, top, flag_of(row == 0))
    put(x_ref, 0, 8, 0, cen_ref[:8, 8:24], 0.0)
    put(x_ref, 1, 0, 0, cen_ref[8:, 8:24], 0.0)
    put(x_ref, 1, 8, 0, bot, flag_of(row == last_row))
    outs = shifted_windows(
        [(0, 0), (1, 1)], x_ref, gain_ref, b1_ref, w1_ref, o1_ref, ww1_ref, wn1_ref, q_ref, kv_ref, s_ref
    )
    out_ref[:12] = outs[0]
    out_ref[12:] = outs[1]


def main_kernel(
    cen_ref, ra_ref, rb_ref, ca_ref, cb_ref, mid_ref, gain_ref,
    b1_ref, b2_ref, br_ref, w1_ref, o1_ref, ww1_ref, wn1_ref, w2_ref, o2_ref, ww2_ref, wn2_ref,
    out_ref,
    x_ref, q_ref, kv_ref, s_ref, bo_ref, a3_ref, kvs_ref, q2_ref, kv2_ref, kr_ref, vr_ref, s2_ref, sr_ref,
):
    row, col, last_row, last_col = edges()
    real = lanes((1, 128)) < C - 128
    one1 = jnp.where(lanes((1, 128)) == ONE - 128, 1.0, 0.0)
    row_odd = lax.rem(row, 2) == 1
    col_odd = lax.rem(col, 2) == 1
    out_top = flag_of(row == 0)
    out_bot = flag_of(row == last_row)
    out_lef = flag_of(col == 0)
    out_rig = flag_of(col == last_col)
    top = jnp.where(row_odd, ra_ref[...], rb_ref[...])
    bot = jnp.where(row_odd, rb_ref[...], ra_ref[...])
    lef = jnp.where(col_odd, ca_ref[...], cb_ref[...])
    rig = jnp.where(col_odd, cb_ref[...], ca_ref[...])
    both = jnp.maximum
    put(x_ref, 0, 0, 0, lef[:8], both(out_top, out_lef))
    put(x_ref, 0, 0, 8, top[:, :8], out_top)
    put(x_ref, 0, 8, 0, lef[8:16], out_lef)
    put(x_ref, 0, 8, 8, cen_ref[:8, :8], 0.0)
    put(x_ref, 1, 0, 0, lef[16:24], out_lef)
    put(x_ref, 1, 0, 8, cen_ref[8:, :8], 0.0)
    put(x_ref, 1, 8, 0, lef[24:], both(out_bot, out_lef))
    put(x_ref, 1, 8, 8, bot[:, :8], out_bot)
    put(x_ref, 2, 0, 0, top[:, 24:], out_top)
    put(x_ref, 2, 0, 8, rig[:8], both(out_top, out_rig))
    put(x_ref, 2, 8, 0, cen_ref[:8, 24:], 0.0)
    put(x_ref, 2, 8, 8, rig[8:16], out_rig)
    put(x_ref, 3, 0, 0, cen_ref[8:, 24:], 0.0)
    put(x_ref, 3, 0, 8, rig[16:24], out_rig)
    put(x_ref, 3, 8, 0, bot[:, 24:], out_bot)
    put(x_ref, 3, 8, 8, rig[24:], both(out_bot, out_rig))

    outs = shifted_windows(
        [(0, 0), (1, 1), (2, 0), (3, 1)],
        x_ref, gain_ref, b1_ref, w1_ref, o1_ref, ww1_ref, wn1_ref, q_ref, kv_ref, s_ref,
    )
    bo_ref[:12, :16] = outs[0]
    bo_ref[12:, :16] = outs[1]
    bo_ref[:, 16:32] = mid_ref[...]
    bo_ref[:12, 32:] = outs[2]
    bo_ref[12:, 32:] = outs[3]

    n0, n1 = norm(bo_ref[...].reshape(24 * 48, 256), gain_ref[2:3, :], real)
    a3_ref[:, :, :128] = n0.reshape(24, 48, 128)
    a3_ref[:, :, 128:] = (n1 + one1).reshape(24, 48, 128)
    base = jnp.where(lanes((1, 1, 256)) == ONE, 1.0, 0.0)

    @pl.when(row == 0)
    def _():
        a3_ref[:4] = jnp.broadcast_to(base, (4, 48, 256))

    @pl.when(row == last_row)
    def _():
        a3_ref[20:] = jnp.broadcast_to(base, (4, 48, 256))

    @pl.when(col == 0)
    def _():
        a3_ref[:, :8] = jnp.broadcast_to(base, (24, 8, 256))

    @pl.when(col == last_col)
    def _():
        a3_ref[:, 40:] = jnp.broadcast_to(base, (24, 8, 256))

    kvs_ref[...] = mm(a3_ref[:, 4:44, :].reshape(960, 256).astype(BF), w2_ref[:, 256:]).reshape(24, 40, 512)
    lane = lanes((1, 128))
    masks = [jnp.where((lane >= 30 * t) & (lane < 30 * t + 30), 1.0, 0.0).astype(BF) for t in range(3)]
    kr_ref[:, :, 3 * REST :, :] = jnp.zeros((2, 2, 256 - 3 * REST, 128), BF)
    vr_ref[:, :, 3 * REST :, :] = jnp.zeros((2, 2, 256 - 3 * REST, 256), BF)
    for j in range(2):
        q = a3_ref[4:20, 8 + 16 * j : 24 + 16 * j, :].reshape(256, 256).astype(BF)
        q2_ref[j] = (mm(q, w2_ref[:, :256]) * SCALE).astype(BF)
        kv = kvs_ref[:, 16 * j : 16 * j + 24, :].reshape(576, 512).astype(BF)
        kv2_ref[j, :, :384] = kv[:KEYS, :384]
        kv2_ref[j, :, 512:640] = kv[:KEYS, 384:]
        kv2_ref[j, :, 384:512] = jnp.ones((KEYS, 128), BF)
        kv2_ref[j, :, 640:] = jnp.ones((KEYS, 128), BF)
        for half in range(2):
            for t in range(3):
                rows = slice(t * REST, t * REST + REST)
                kr_ref[j, half, rows, :] = kv[KEYS:, 128 * half : 128 * half + 128] * masks[t]
                vr_ref[j, half, rows, :128] = kv[KEYS:, 256 + 128 * half : 384 + 128 * half] * masks[t]
                vr_ref[j, half, rows, 128:] = jnp.broadcast_to(masks[t], (REST, 128))
    mixed = jnp.concatenate(cross_attend(2, q2_ref, kv2_ref, kr_ref, vr_ref, b2_ref, br_ref, s2_ref, sr_ref), axis=0)
    own = [bo_ref[4:20, 8 + 16 * j : 24 + 16 * j, :].reshape(256, 256) for j in range(2)]
    res = jnp.concatenate(own, axis=0) + mm(mixed, o2_ref[...])
    out = mlp(res, gain_ref[3:4, :], real, ww2_ref[...], wn2_ref[...])
    for j in range(2):
        part = out[256 * j : 256 * j + 256].reshape(16, 16, 256)
        out_ref[:, 16 * j : 16 * j + 16, :] = part[:, :, :C].astype(BF)


def swap(low, high, axis):
    count = lax.axis_size(axis)
    even = lax.axis_index(axis) % 2 == 0

    def pairs(first):
        found = []
        for i in range(first, count - 1, 2):
            found += [(i, i + 1), (i + 1, i)]
        return found

    a = lax.ppermute(jnp.where(even, high, low), axis, pairs(0))
    b = lax.ppermute(jnp.where(even, low, high), axis, pairs(1))
    return a, b


def per_device(
    pixels, shift_prenorm, shift_inputs, shift_table, shift_output, shift_postnorm, shift_widen, shift_narrow,
    cross_prenorm, cross_query, cross_keyval, cross_table, cross_output, cross_postnorm, cross_widen, cross_narrow,
):
    ra, rb = swap(pixels[:SHIFT], pixels[SHIFT:], "rows")
    odd = lax.axis_index("rows") % 2 == 1
    top = jnp.where(odd, ra, rb)
    bot = jnp.where(odd, rb, ra)
    sds = jax.ShapeDtypeStruct
    vmem = pl.BlockSpec(memory_space=pltpu.VMEM)
    hbm = pl.BlockSpec(memory_space=pltpu.HBM)
    operands = (
        pixels, shift_table, cross_table,
        shift_prenorm.reshape(1, C), shift_postnorm.reshape(1, C), cross_prenorm.reshape(1, C), cross_postnorm.reshape(1, C),
        shift_inputs, shift_output, shift_widen, shift_narrow.T, cross_query, cross_keyval, cross_output,
        cross_widen, cross_narrow.T,
    )
    strip = (pixels.shape[0], SHIFT, C)
    center, low, high, gains, *made = pl.pallas_call(
        tables_kernel,
        out_shape=(
            sds(pixels.shape, BF), sds(strip, BF), sds(strip, BF), sds((8, 256), F32),
            sds((HEADS, 256, 256), F32), sds((HEADS, 256, KEYS), F32), sds((2, 256, 256), F32), sds((256, 768), BF), sds((256, 256), BF),
            sds((256, 384), BF), sds((256, 384), BF), sds((256, 768), BF), sds((256, 256), BF), sds((256, 384), BF),
            sds((256, 384), BF),
        ),
        in_specs=[hbm] * 16,
        out_specs=[vmem] * 15,
        scratch_shapes=[pltpu.VMEM(x.shape, x.dtype) for x in (*operands[3:7], *operands[1:3], *operands[7:])]
        + [
            pltpu.SemaphoreType.DMA((16,)),
            pltpu.VMEM((192, 32), F32), pltpu.VMEM((240, 40), F32), pltpu.VMEM((192, 512), F32), pltpu.VMEM((240, 1024), F32),
        ],
        cost_estimate=pl.CostEstimate(flops=200_000_000, bytes_accessed=8_000_000, transcendentals=0),
        compiler_params=pltpu.CompilerParams(vmem_limit_bytes=20 * 2**20),
        name="tables",
    )(*[pltpu.with_memory_space_constraint(x, pltpu.HBM) for x in operands])
    b1, b2, br, w1, o1, ww1, wn1, w2, o2, ww2, wn2 = made

    strips = [
        jnp.concatenate([top[:, part], own, bot[:, part]], axis=0)
        for part, own in ((slice(0, SHIFT), low), (slice(24, 32), high))
    ]
    ca, cb = swap(strips[0], strips[1], "cols")
    middle = pl.pallas_call(
        middle_kernel,
        out_shape=sds((24, 16, 256), F32),
        in_specs=[vmem] * 9,
        out_specs=vmem,
        scratch_shapes=[
            pltpu.VMEM((2, 16, 16, 256), F32), pltpu.VMEM((2, 192, 256), BF), pltpu.VMEM((2, 256, 768), BF),
            pltpu.VMEM((AHEAD + 1, 192, 256), F32),
        ],
        cost_estimate=pl.CostEstimate(flops=2_000_000_000, bytes_accessed=8_000_000, transcendentals=1_000_000),
        compiler_params=pltpu.CompilerParams(vmem_limit_bytes=16 * 2**20),
        name="middle",
    )(center, ra, rb, gains, b1, w1, o1, ww1, wn1)
    return pl.pallas_call(
        main_kernel,
        out_shape=sds(pixels.shape, BF),
        in_specs=[vmem] * 18,
        out_specs=vmem,
        scratch_shapes=[
            pltpu.VMEM((4, 16, 16, 256), F32), pltpu.VMEM((4, 192, 256), BF), pltpu.VMEM((4, 256, 768), BF),
            pltpu.VMEM((AHEAD + 1, 192, 256), F32),
            pltpu.VMEM((24, 48, 256), F32), pltpu.VMEM((24, 48, 256), F32), pltpu.VMEM((24, 40, 512), F32),
            pltpu.VMEM((2, 256, 256), BF), pltpu.VMEM((2, KEYS, 768), BF),
            pltpu.VMEM((2, 2, 256, 128), BF), pltpu.VMEM((2, 2, 256, 256), BF),
            pltpu.VMEM((CROSS_AHEAD + 1, 256, KEYS), F32), pltpu.VMEM((2, 2, 256, 256), F32),
        ],
        cost_estimate=pl.CostEstimate(flops=10_000_000_000, bytes_accessed=8_000_000, transcendentals=4_000_000),
        compiler_params=pltpu.CompilerParams(vmem_limit_bytes=32 * 2**20),
        name="blocks",
    )(center, ra, rb, ca, cb, middle, gains, b1, b2, br, w1, o1, ww1, wn1, w2, o2, ww2, wn2)


def solution(mesh):
    return jax.shard_map(
        per_device,
        mesh=mesh,
        in_specs=(P("rows", "cols", None),) + (P(),) * 15,
        out_specs=P("rows", "cols", None),
        check_vma=False,
    )
```

```python
import jax
import jax.numpy as jnp
from jax import lax
from jax.experimental import pallas as pl
from jax.experimental.pallas import tpu as pltpu
from jax.sharding import PartitionSpec as P

C = 180
HEADS = 6
HEAD_DIM = 30
WIN = 16
SHIFT = 8
PAD = 4
OWIN = 24
EPS = 1e-05
LOG2E = 1.4426950408889634
SCALE = HEAD_DIM ** (-0.5) * LOG2E
HALF_ROOT = 0.7071067811865476
LOW = -1e30
FLAG = 180
ONE = 181
KFLAG = 100
KEYS = 512
REST = 64
AHEAD = 4
CROSS_AHEAD = 1
BF = jnp.bfloat16
F32 = jnp.float32


def mm(a, b, dims=((1,), (0,)), precision=None):
    return lax.dot_general(a, b, (dims, ((), ())), preferred_element_type=F32, precision=precision)


NT = ((1,), (1,))


def lanes(shape):
    return lax.broadcasted_iota(jnp.int32, shape, len(shape) - 1)


def rows_of(shape):
    return lax.broadcasted_iota(jnp.int32, shape, len(shape) - 2)


def place(dst_ref, src, row, col):
    dst_ref[row : row + src.shape[0], col : col + src.shape[1]] = src


def exact_parts(x):
    first = x.astype(BF)
    rest = x - first.astype(F32)
    second = rest.astype(BF)
    return first, second, (rest - second.astype(F32)).astype(BF)


def shear(table_ref, flip, side, pick, amount, bits):
    top = HEADS * side
    y = None
    for part in exact_parts(table_ref[...] * LOG2E):
        turned = [mm(flip, part[h * side : (h + 1) * side], NT) for h in range(HEADS)]
        term = mm(jnp.concatenate(turned, axis=0).astype(BF), pick)
        y = term if y is None else y + term
    for bit in bits:
        y = jnp.where((amount & bit) != 0, pltpu.roll(y, top - bit, 0), y)
    y = jnp.concatenate([y[h * side : h * side + 24] for h in range(HEADS)], axis=0)
    amount = jnp.broadcast_to(amount[:1], y.shape)
    for bit in (4, 2, 1):
        y = jnp.where((amount & bit) != 0, pltpu.roll(y, HEADS * 24 - bit, 0), y)
    return y


def widened(dst_ref, src_ref, first):
    for k in range(src_ref.shape[1] // 90):
        place(dst_ref, src_ref[:, 90 * k : 90 * k + 90], 0, 128 * (first + k))


def base_weights(flagged):
    r = rows_of((256, 768))
    c = lanes((256, 768))
    base = jnp.where((r == ONE) & ((c == KFLAG) | (c == 128 + KFLAG)), 1.0, 0.0)
    if flagged:
        base = jnp.where((r == FLAG) & ((c == 256 + KFLAG) | (c == 384 + KFLAG)), LOW, base)
    return base.astype(BF)


def zeros(ref):
    ref[...] = jnp.zeros(ref.shape, ref.dtype)


def tables_kernel(*refs):
    sources = refs[:16]
    (
        cen_ref, ct_ref, cq_ref, ckv_ref, co_ref, cw_ref, cn_ref,
        low_ref, high_ref, gain_ref, b1_ref, w1_ref, o1_ref, ww1_ref, wn1_ref,
        st_ref, g0_ref, g1_ref, g2_ref, g3_ref, wi_ref, wo_ref, ww_ref, wn_ref, sems, t1_ref, e1_ref,
    ) = refs[16:]
    targets = (
        cen_ref, st_ref, g0_ref, g1_ref, g2_ref, g3_ref, wi_ref, wo_ref, ww_ref, wn_ref,
        ct_ref, cq_ref, ckv_ref, co_ref, cw_ref, cn_ref,
    )
    copies = [pltpu.make_async_copy(a, b, sems.at[i]) for i, (a, b) in enumerate(zip(sources, targets))]
    for copy in copies:
        copy.start()
    w1_ref[...] = base_weights(True)
    for ref in (o1_ref, ww1_ref, wn1_ref, gain_ref, t1_ref):
        zeros(ref)
    flip = jnp.where(rows_of((32, 32)) == lanes((32, 32)), 1.0, 0.0).astype(BF)
    pick = jnp.where(lanes((32, 512)) // 16 == 30 - rows_of((32, 512)), 1.0, 0.0).astype(BF)
    amount = 15 - lanes((192, 512)) % 16
    for copy in copies[:2]:
        copy.wait()
    low_ref[...] = cen_ref[:, :SHIFT]
    high_ref[...] = cen_ref[:, 24:]
    for h in range(HEADS):
        t1_ref[h * 32 : h * 32 + 31, :31] = st_ref[h]
    e1_ref[...] = shear(t1_ref, flip, 32, pick, amount, (8,))
    for h in range(HEADS):
        for qy in range(WIN):
            b1_ref[h, qy * 16 : qy * 16 + 16, :] = e1_ref[h * 24 : h * 24 + 16, (15 - qy) * 16 : (15 - qy) * 16 + 256]
    for copy in copies[2:]:
        copy.wait()
    widened(w1_ref, wi_ref, 0)
    place(o1_ref, wo_ref[:90], 0, 0)
    place(o1_ref, wo_ref[90:], 128, 0)
    place(ww1_ref, ww_ref[...], 0, 0)
    place(wn1_ref, wn_ref[...], 0, 0)
    for i, src in enumerate((g0_ref, g1_ref, g2_ref, g3_ref)):
        gain_ref[i : i + 1, :C] = src[...] * (HALF_ROOT if i % 2 else 1.0)


def cross_tables(
    ct_ref, cq_ref, ckv_ref, co_ref, cw_ref, cn_ref, b2_ref, br_ref, w2_ref, o2_ref, ww2_ref, wn2_ref, t2_ref, e2_ref
):
    w2_ref[...] = base_weights(False)
    for ref in (o2_ref, ww2_ref, wn2_ref, t2_ref):
        zeros(ref)
    widened(w2_ref, cq_ref, 0)
    widened(w2_ref, ckv_ref, 2)
    place(o2_ref, co_ref[:90], 0, 0)
    place(o2_ref, co_ref[90:], 128, 0)
    place(ww2_ref, cw_ref[...], 0, 0)
    place(wn2_ref, cn_ref[...], 0, 0)
    for h in range(HEADS):
        t2_ref[h * 40 : h * 40 + 39, :39] = ct_ref[h]
    flip = jnp.where(rows_of((40, 40)) == 38 - lanes((40, 40)), 1.0, 0.0).astype(BF)
    lane = lanes((40, 1024))
    row = rows_of((40, 1024))
    pick = jnp.where((lane >= row * 24) & (lane < row * 24 + 24), 1.0, 0.0).astype(BF)
    lane1 = lanes((1, 1024)).astype(F32)
    kx = lane1 - 24.0 * jnp.floor((lane1 + 0.5) * (1.0 / 24.0))
    amount = jnp.broadcast_to(23 - kx.astype(jnp.int32), (240, 1024))
    e2_ref[...] = shear(t2_ref, flip, 40, pick, amount, (16, 8))
    for half in range(2):
        br_ref[half, :, 3 * REST :] = jnp.full((256, 256 - 3 * REST), LOW, F32)
    for h in range(HEADS):
        for qy in range(WIN):
            bias = e2_ref[h * 24 : h * 24 + 16, (15 - qy) * 24 : (15 - qy) * 24 + 576]
            b2_ref[h, qy * 16 : qy * 16 + 16, :] = bias[:, :KEYS]
            br_ref[h // 3, qy * 16 : qy * 16 + 16, h % 3 * REST : h % 3 * REST + REST] = bias[:, KEYS:]


def norm(x, gain, real):
    x0 = x[:, :128]
    x1 = jnp.where(real, x[:, 128:], 0.0)
    mean = jnp.sum(x0 + x1, axis=-1, keepdims=True) * (1.0 / C)
    c0 = x0 - mean
    c1 = jnp.where(real, x1 - mean, 0.0)
    spread = jnp.sum(c0 * c0 + c1 * c1, axis=-1, keepdims=True) * (1.0 / C)
    inv = lax.rsqrt(spread + EPS)
    return c0 * inv * gain[:, :128], c1 * inv * gain[:, 128:]


def mlp(res, gain, real, widen, narrow):
    n0, n1 = norm(res, gain, real)
    normed = jnp.concatenate([n0, n1], axis=1).astype(BF)
    y = mm(normed, widen)
    hidden = (y + y * lax.erf(y)).astype(BF)
    return res + mm(hidden, narrow, NT) * HALF_ROOT


def attend(jobs, s_refs):
    lane = lanes((1, 128))
    order = [(job, h) for h in range(HEADS) for job in range(len(jobs))]

    def start(n):
        job, h = order[n]
        half, t = divmod(h, 3)
        queries, keys, _, bias = jobs[job]
        own = ((lane >= 30 * t) & (lane < 30 * t + 30)) | (lane == KFLAG)
        scores = mm(queries(half) * jnp.where(own, 1.0, 0.0).astype(BF), keys(half), NT) + bias(h)
        s_refs[n % s_refs.shape[0]] = scores
        return jnp.max(scores, axis=-1, keepdims=True)

    mixed = [[None, None] for _ in jobs]
    depth = s_refs.shape[0] - 1
    peaks = [start(n) for n in range(depth)]
    for n, (job, h) in enumerate(order):
        if n + depth < len(order):
            peaks.append(start(n + depth))
        half, t = divmod(h, 3)
        weights = jnp.exp2(s_refs[n % (depth + 1)] - peaks[n]).astype(BF)
        out = mm(weights, jobs[job][2](half))
        out = out[:, :128] / out[:, 128:]
        mixed[job][half] = out if t == 0 else jnp.where(lane >= 30 * t, out, mixed[job][half])
    return [jnp.concatenate(pair, axis=1).astype(BF) for pair in mixed]


def cross_attend(count, q_ref, kv_ref, kr_ref, vr_ref, b2_ref, br_ref, s_ref, sr_ref):
    lane = lanes((1, 128))
    lane2 = lanes((1, 256)) % 128
    low = lane < REST
    order = [(j, h) for h in range(HEADS) for j in range(count)]
    depth = s_ref.shape[0] - 1

    def start(n):
        j, h = order[n]
        half, t = divmod(h, 3)
        part = slice(half * 128, half * 128 + 128)
        queries, keys = q_ref[j, :, part], kv_ref[j, :, part]
        if t == 0:
            sr_ref[j, half] = mm(queries, kr_ref[j, half], NT) + br_ref[half]
        own = (lane >= 30 * t) & (lane < 30 * t + 30)
        scores = mm(queries * jnp.where(own, 1.0, 0.0).astype(BF), keys, NT) + b2_ref[h]
        s_ref[n % (depth + 1)] = scores
        rest = sr_ref[j, half, :, t // 2 * 128 : t // 2 * 128 + 128]
        top = jnp.where(~low if t == 1 else low, rest, LOW)
        for k in range(4):
            top = jnp.maximum(top, scores[:, 128 * k : 128 * k + 128])
        return jnp.max(top, axis=-1, keepdims=True)

    peaks = [start(n) for n in range(depth)]
    total = {}
    mixed = [[None, None] for _ in range(count)]
    for n, (j, h) in enumerate(order):
        if n + depth < len(order):
            peaks.append(start(n + depth))
        half, t = divmod(h, 3)
        weights = jnp.exp2(s_ref[n % (depth + 1)] - peaks[n]).astype(BF)
        out = mm(weights, kv_ref[j, :, 256 + half * 256 : 512 + half * 256])
        total[j] = out if t == 0 else jnp.where(lane2 >= 30 * t, out, total[j])
        if t == 2:
            first = jnp.where(low, peaks[n - 2 * count], peaks[n - count])
            rest = [jnp.exp2(sr_ref[j, half, :, :128] - first), jnp.exp2(sr_ref[j, half, :, 128:] - peaks[n])]
            out = total[j] + mm(jnp.concatenate(rest, axis=1).astype(BF), vr_ref[j, half])
            mixed[j][half] = out[:, :128] / out[:, 128:]
    return [jnp.concatenate(pair, axis=1).astype(BF) for pair in mixed]


def shifted_windows(windows, x_ref, gain_ref, b1_ref, w1_ref, o1_ref, ww1_ref, wn1_ref, q_ref, kv_ref, s_refs):
    real = lanes((1, 128)) < C - 128
    count = len(windows)
    x = x_ref[...].reshape(count * 256, 256)
    n0, n1 = norm(x, gain_ref[0:1, :], real)
    n1 = jnp.where(real, n1, x[:, 128:])
    normed = jnp.concatenate([n0, n1], axis=1).astype(BF)
    wanted = [slice(slot * 256 + 64 * (1 - i), slot * 256 + 64 * (1 - i) + 192) for slot, i in windows]
    kv = mm(normed, w1_ref[:, 256:]).astype(BF).reshape(count, 256, 512)
    ones = jnp.ones((count, 256, 128), BF)
    kv_ref[:, :, :384] = kv[:, :, :384]
    kv_ref[:, :, 384:512] = ones
    kv_ref[:, :, 512:640] = kv[:, :, 384:]
    kv_ref[:, :, 640:] = ones
    q = mm(jnp.concatenate([normed[rows] for rows in wanted], axis=0), w1_ref[:, :256])
    q_ref[...] = (q * SCALE).astype(BF).reshape(count, 192, 256)
    jobs = []
    for slot, i in windows:
        first = 64 * (1 - i)
        jobs.append(
            (
                lambda half, slot=slot: q_ref[slot, :, half * 128 : half * 128 + 128],
                lambda half, slot=slot: kv_ref[slot, :, half * 128 : half * 128 + 128],
                lambda half, slot=slot: kv_ref[slot, :, 256 + half * 256 : 512 + half * 256],
                lambda h, first=first: b1_ref[h, first : first + 192, :],
            )
        )
    mixed = jnp.concatenate(attend(jobs, s_refs), axis=0)
    x = x_ref[...].reshape(count * 256, 256)
    res = jnp.concatenate([x[rows] for rows in wanted], axis=0) + mm(mixed, o1_ref[...])
    out = mlp(res, gain_ref[1:2, :], real, ww1_ref[...], wn1_ref[...]).astype(BF).astype(F32)
    return [out[192 * k : 192 * k + 192].reshape(12, 16, 256) for k in range(count)]


def put(x_ref, slot, y0, x0, piece, flag):
    lane1 = lanes((1, 128))
    ny, nx = piece.shape[0], piece.shape[1]
    x_ref[slot, y0 : y0 + ny, x0 : x0 + nx, 128:] = jnp.broadcast_to(
        jnp.where(lane1 == FLAG - 128, flag, jnp.where(lane1 == ONE - 128, 1.0, 0.0)), (ny, nx, 128)
    )
    x_ref[slot, y0 : y0 + ny, x0 : x0 + nx, :C] = piece.astype(F32)


def edges():
    row, col = lax.axis_index("rows"), lax.axis_index("cols")
    return row, col, lax.axis_size("rows") - 1, lax.axis_size("cols") - 1


def flag_of(condition):
    return jnp.where(condition, 1.0, 0.0)


def middle_kernel(
    cen_ref, ra_ref, rb_ref, gain_ref, b1_ref, w1_ref, o1_ref, ww1_ref, wn1_ref, ct_ref, cq_ref, ckv_ref, co_ref, cw_ref, cn_ref,
    out_ref, b2_ref, br_ref, w2_ref, o2_ref, ww2_ref, wn2_ref,
    x_ref, q_ref, kv_ref, s_ref, t2_ref, e2_ref,
):
    row, _, last_row, _ = edges()
    odd = lax.rem(row, 2) == 1
    top = jnp.where(odd, ra_ref[:, 8:24], rb_ref[:, 8:24])
    bot = jnp.where(odd, rb_ref[:, 8:24], ra_ref[:, 8:24])
    put(x_ref, 0, 0, 0, top, flag_of(row == 0))
    put(x_ref, 0, 8, 0, cen_ref[:8, 8:24], 0.0)
    put(x_ref, 1, 0, 0, cen_ref[8:, 8:24], 0.0)
    put(x_ref, 1, 8, 0, bot, flag_of(row == last_row))
    cross_tables(
        ct_ref, cq_ref, ckv_ref, co_ref, cw_ref, cn_ref, b2_ref, br_ref, w2_ref, o2_ref, ww2_ref, wn2_ref, t2_ref, e2_ref
    )
    outs = shifted_windows(
        [(0, 0), (1, 1)], x_ref, gain_ref, b1_ref, w1_ref, o1_ref, ww1_ref, wn1_ref, q_ref, kv_ref, s_ref
    )
    out_ref[:12] = outs[0]
    out_ref[12:] = outs[1]


def main_kernel(
    cen_ref, ra_ref, rb_ref, ca_ref, cb_ref, mid_ref, gain_ref,
    b1_ref, b2_ref, br_ref, w1_ref, o1_ref, ww1_ref, wn1_ref, w2_ref, o2_ref, ww2_ref, wn2_ref,
    out_ref,
    x_ref, q_ref, kv_ref, s_ref, bo_ref, a3_ref, kvs_ref, q2_ref, kv2_ref, kr_ref, vr_ref, s2_ref, sr_ref,
):
    row, col, last_row, last_col = edges()
    real = lanes((1, 128)) < C - 128
    one1 = jnp.where(lanes((1, 128)) == ONE - 128, 1.0, 0.0)
    row_odd = lax.rem(row, 2) == 1
    col_odd = lax.rem(col, 2) == 1
    out_top = flag_of(row == 0)
    out_bot = flag_of(row == last_row)
    out_lef = flag_of(col == 0)
    out_rig = flag_of(col == last_col)
    top = jnp.where(row_odd, ra_ref[...], rb_ref[...])
    bot = jnp.where(row_odd, rb_ref[...], ra_ref[...])
    lef = jnp.where(col_odd, ca_ref[...], cb_ref[...])
    rig = jnp.where(col_odd, cb_ref[...], ca_ref[...])
    both = jnp.maximum
    put(x_ref, 0, 0, 0, lef[:8], both(out_top, out_lef))
    put(x_ref, 0, 0, 8, top[:, :8], out_top)
    put(x_ref, 0, 8, 0, lef[8:16], out_lef)
    put(x_ref, 0, 8, 8, cen_ref[:8, :8], 0.0)
    put(x_ref, 1, 0, 0, lef[16:24], out_lef)
    put(x_ref, 1, 0, 8, cen_ref[8:, :8], 0.0)
    put(x_ref, 1, 8, 0, lef[24:], both(out_bot, out_lef))
    put(x_ref, 1, 8, 8, bot[:, :8], out_bot)
    put(x_ref, 2, 0, 0, top[:, 24:], out_top)
    put(x_ref, 2, 0, 8, rig[:8], both(out_top, out_rig))
    put(x_ref, 2, 8, 0, cen_ref[:8, 24:], 0.0)
    put(x_ref, 2, 8, 8, rig[8:16], out_rig)
    put(x_ref, 3, 0, 0, cen_ref[8:, 24:], 0.0)
    put(x_ref, 3, 0, 8, rig[16:24], out_rig)
    put(x_ref, 3, 8, 0, bot[:, 24:], out_bot)
    put(x_ref, 3, 8, 8, rig[24:], both(out_bot, out_rig))

    outs = shifted_windows(
        [(0, 0), (1, 1), (2, 0), (3, 1)],
        x_ref, gain_ref, b1_ref, w1_ref, o1_ref, ww1_ref, wn1_ref, q_ref, kv_ref, s_ref,
    )
    bo_ref[:12, :16] = outs[0]
    bo_ref[12:, :16] = outs[1]
    bo_ref[:, 16:32] = mid_ref[...]
    bo_ref[:12, 32:] = outs[2]
    bo_ref[12:, 32:] = outs[3]

    n0, n1 = norm(bo_ref[...].reshape(24 * 48, 256), gain_ref[2:3, :], real)
    a3_ref[:, :, :128] = n0.reshape(24, 48, 128)
    a3_ref[:, :, 128:] = (n1 + one1).reshape(24, 48, 128)
    base = jnp.where(lanes((1, 1, 256)) == ONE, 1.0, 0.0)

    @pl.when(row == 0)
    def _():
        a3_ref[:4] = jnp.broadcast_to(base, (4, 48, 256))

    @pl.when(row == last_row)
    def _():
        a3_ref[20:] = jnp.broadcast_to(base, (4, 48, 256))

    @pl.when(col == 0)
    def _():
        a3_ref[:, :8] = jnp.broadcast_to(base, (24, 8, 256))

    @pl.when(col == last_col)
    def _():
        a3_ref[:, 40:] = jnp.broadcast_to(base, (24, 8, 256))

    kvs_ref[...] = mm(a3_ref[:, 4:44, :].reshape(960, 256).astype(BF), w2_ref[:, 256:]).reshape(24, 40, 512)
    lane = lanes((1, 128))
    masks = [jnp.where((lane >= 30 * t) & (lane < 30 * t + 30), 1.0, 0.0).astype(BF) for t in range(3)]
    kr_ref[:, :, 3 * REST :, :] = jnp.zeros((2, 2, 256 - 3 * REST, 128), BF)
    vr_ref[:, :, 3 * REST :, :] = jnp.zeros((2, 2, 256 - 3 * REST, 256), BF)
    for j in range(2):
        q = a3_ref[4:20, 8 + 16 * j : 24 + 16 * j, :].reshape(256, 256).astype(BF)
        q2_ref[j] = (mm(q, w2_ref[:, :256]) * SCALE).astype(BF)
        kv = kvs_ref[:, 16 * j : 16 * j + 24, :].reshape(576, 512).astype(BF)
        kv2_ref[j, :, :384] = kv[:KEYS, :384]
        kv2_ref[j, :, 512:640] = kv[:KEYS, 384:]
        kv2_ref[j, :, 384:512] = jnp.ones((KEYS, 128), BF)
        kv2_ref[j, :, 640:] = jnp.ones((KEYS, 128), BF)
        for half in range(2):
            for t in range(3):
                rows = slice(t * REST, t * REST + REST)
                kr_ref[j, half, rows, :] = kv[KEYS:, 128 * half : 128 * half + 128] * masks[t]
                vr_ref[j, half, rows, :128] = kv[KEYS:, 256 + 128 * half : 384 + 128 * half] * masks[t]
                vr_ref[j, half, rows, 128:] = jnp.broadcast_to(masks[t], (REST, 128))
    mixed = jnp.concatenate(cross_attend(2, q2_ref, kv2_ref, kr_ref, vr_ref, b2_ref, br_ref, s2_ref, sr_ref), axis=0)
    own = [bo_ref[4:20, 8 + 16 * j : 24 + 16 * j, :].reshape(256, 256) for j in range(2)]
    res = jnp.concatenate(own, axis=0) + mm(mixed, o2_ref[...])
    out = mlp(res, gain_ref[3:4, :], real, ww2_ref[...], wn2_ref[...])
    for j in range(2):
        part = out[256 * j : 256 * j + 256].reshape(16, 16, 256)
        out_ref[:, 16 * j : 16 * j + 16, :] = part[:, :, :C].astype(BF)


def swap(low, high, axis):
    count = lax.axis_size(axis)
    even = lax.axis_index(axis) % 2 == 0

    def pairs(first):
        found = []
        for i in range(first, count - 1, 2):
            found += [(i, i + 1), (i + 1, i)]
        return found

    a = lax.ppermute(jnp.where(even, high, low), axis, pairs(0))
    b = lax.ppermute(jnp.where(even, low, high), axis, pairs(1))
    return a, b


def per_device(
    pixels, shift_prenorm, shift_inputs, shift_table, shift_output, shift_postnorm, shift_widen, shift_narrow,
    cross_prenorm, cross_query, cross_keyval, cross_table, cross_output, cross_postnorm, cross_widen, cross_narrow,
):
    ra, rb = swap(pixels[:SHIFT], pixels[SHIFT:], "rows")
    odd = lax.axis_index("rows") % 2 == 1
    top = jnp.where(odd, ra, rb)
    bot = jnp.where(odd, rb, ra)
    sds = jax.ShapeDtypeStruct
    vmem = pl.BlockSpec(memory_space=pltpu.VMEM)
    hbm = pl.BlockSpec(memory_space=pltpu.HBM)
    firsts = (
        pixels, shift_table,
        shift_prenorm.reshape(1, C), shift_postnorm.reshape(1, C), cross_prenorm.reshape(1, C), cross_postnorm.reshape(1, C),
        shift_inputs, shift_output, shift_widen, shift_narrow.T,
    )
    seconds = (cross_table, cross_query, cross_keyval, cross_output, cross_widen, cross_narrow.T)
    strip = (pixels.shape[0], SHIFT, C)
    like = lambda x: sds(x.shape, x.dtype)
    center, *rest = pl.pallas_call(
        tables_kernel,
        out_shape=(
            like(pixels), *map(like, seconds), sds(strip, BF), sds(strip, BF), sds((8, 256), F32), sds((HEADS, 256, 256), F32),
            sds((256, 768), BF), sds((256, 256), BF), sds((256, 384), BF), sds((256, 384), BF),
        ),
        in_specs=[hbm] * 16,
        out_specs=[vmem] * 15,
        scratch_shapes=[pltpu.VMEM(x.shape, x.dtype) for x in firsts[1:]]
        + [pltpu.SemaphoreType.DMA((16,)), pltpu.VMEM((192, 32), F32), pltpu.VMEM((144, 512), F32)],
        cost_estimate=pl.CostEstimate(flops=100_000_000, bytes_accessed=5_000_000, transcendentals=0),
        compiler_params=pltpu.CompilerParams(vmem_limit_bytes=16 * 2**20),
        name="tables",
    )(*[pltpu.with_memory_space_constraint(x, pltpu.HBM) for x in (*firsts, *seconds)])
    raw, (low, high, gains, b1, w1, o1, ww1, wn1) = rest[:6], rest[6:]

    strips = [
        jnp.concatenate([top[:, part], own, bot[:, part]], axis=0)
        for part, own in ((slice(0, SHIFT), low), (slice(24, 32), high))
    ]
    ca, cb = swap(strips[0], strips[1], "cols")
    middle, b2, br, w2, o2, ww2, wn2 = pl.pallas_call(
        middle_kernel,
        out_shape=(
            sds((24, 16, 256), F32), sds((HEADS, 256, KEYS), F32), sds((2, 256, 256), F32), sds((256, 768), BF),
            sds((256, 256), BF), sds((256, 384), BF), sds((256, 384), BF),
        ),
        in_specs=[vmem] * 15,
        out_specs=[vmem] * 7,
        scratch_shapes=[
            pltpu.VMEM((2, 16, 16, 256), F32), pltpu.VMEM((2, 192, 256), BF), pltpu.VMEM((2, 256, 768), BF),
            pltpu.VMEM((AHEAD + 1, 192, 256), F32), pltpu.VMEM((240, 40), F32), pltpu.VMEM((144, 1024), F32),
        ],
        cost_estimate=pl.CostEstimate(flops=2_000_000_000, bytes_accessed=8_000_000, transcendentals=1_000_000),
        compiler_params=pltpu.CompilerParams(vmem_limit_bytes=20 * 2**20),
        name="middle",
    )(center, ra, rb, gains, b1, w1, o1, ww1, wn1, *raw)
    return pl.pallas_call(
        main_kernel,
        out_shape=sds(pixels.shape, BF),
        in_specs=[vmem] * 18,
        out_specs=vmem,
        scratch_shapes=[
            pltpu.VMEM((4, 16, 16, 256), F32), pltpu.VMEM((4, 192, 256), BF), pltpu.VMEM((4, 256, 768), BF),
            pltpu.VMEM((AHEAD + 1, 192, 256), F32),
            pltpu.VMEM((24, 48, 256), F32), pltpu.VMEM((24, 48, 256), F32), pltpu.VMEM((24, 40, 512), F32),
            pltpu.VMEM((2, 256, 256), BF), pltpu.VMEM((2, KEYS, 768), BF),
            pltpu.VMEM((2, 2, 256, 128), BF), pltpu.VMEM((2, 2, 256, 256), BF),
            pltpu.VMEM((CROSS_AHEAD + 1, 256, KEYS), F32), pltpu.VMEM((2, 2, 256, 256), F32),
        ],
        cost_estimate=pl.CostEstimate(flops=10_000_000_000, bytes_accessed=8_000_000, transcendentals=4_000_000),
        compiler_params=pltpu.CompilerParams(vmem_limit_bytes=32 * 2**20),
        name="blocks",
    )(center, ra, rb, ca, cb, middle, gains, b1, b2, br, w1, o1, ww1, wn1, w2, o2, ww2, wn2)


def solution(mesh):
    return jax.shard_map(
        per_device,
        mesh=mesh,
        in_specs=(P("rows", "cols", None),) + (P(),) * 15,
        out_specs=P("rows", "cols", None),
        check_vma=False,
    )
```

```python
import jax
import jax.numpy as jnp
from jax import lax
from jax.experimental import pallas as pl
from jax.experimental.pallas import tpu as pltpu
from jax.sharding import PartitionSpec as P

C = 180
HEADS = 6
HEAD_DIM = 30
WIN = 16
SHIFT = 8
EPS = 1e-05
LOG2E = 1.4426950408889634
SCALE = HEAD_DIM ** (-0.5) * LOG2E
HALF_ROOT = 0.7071067811865476
LOW = -1e30
FLAG = 180
ONE = 181
KFLAG = 100
KEYS = 512
REST = 64
AHEAD = 4
CROSS_AHEAD = 1
BF = jnp.bfloat16
F32 = jnp.float32


def mm(a, b, dims=((1,), (0,)), precision=None):
    return lax.dot_general(a, b, (dims, ((), ())), preferred_element_type=F32, precision=precision)


NT = ((1,), (1,))


def lanes(shape):
    return lax.broadcasted_iota(jnp.int32, shape, len(shape) - 1)


def rows_of(shape):
    return lax.broadcasted_iota(jnp.int32, shape, len(shape) - 2)


def place(dst_ref, src, row, col):
    dst_ref[row : row + src.shape[0], col : col + src.shape[1]] = src


def exact_parts(x):
    first = x.astype(BF)
    rest = x - first.astype(F32)
    second = rest.astype(BF)
    return first, second, (rest - second.astype(F32)).astype(BF)


def shear(table_ref, flip, side, pick, amount, bits):
    top = HEADS * side
    y = None
    for part in exact_parts(table_ref[...] * LOG2E):
        turned = [mm(flip, part[h * side : (h + 1) * side], NT) for h in range(HEADS)]
        term = mm(jnp.concatenate(turned, axis=0).astype(BF), pick)
        y = term if y is None else y + term
    for bit in bits:
        y = jnp.where((amount & bit) != 0, pltpu.roll(y, top - bit, 0), y)
    y = jnp.concatenate([y[h * side : h * side + 24] for h in range(HEADS)], axis=0)
    amount = jnp.broadcast_to(amount[:1], y.shape)
    for bit in (4, 2, 1):
        y = jnp.where((amount & bit) != 0, pltpu.roll(y, HEADS * 24 - bit, 0), y)
    return y


def widened(dst_ref, src_ref, first):
    for k in range(src_ref.shape[1] // 90):
        place(dst_ref, src_ref[:, 90 * k : 90 * k + 90], 0, 128 * (first + k))


def base_weights(flagged):
    r = rows_of((256, 768))
    c = lanes((256, 768))
    base = jnp.where((r == ONE) & ((c == KFLAG) | (c == 128 + KFLAG)), 1.0, 0.0)
    if flagged:
        base = jnp.where((r == FLAG) & ((c == 256 + KFLAG) | (c == 384 + KFLAG)), LOW, base)
    return base.astype(BF)


def zeros(ref):
    ref[...] = jnp.zeros(ref.shape, ref.dtype)


def tables_kernel(*refs):
    sources = refs[:16]
    (
        cen_ref, ct_ref, cq_ref, ckv_ref, co_ref, cw_ref, cn_ref,
        low_ref, high_ref, gain_ref, b1_ref, w1_ref, o1_ref, ww1_ref, wn1_ref,
        st_ref, g0_ref, g1_ref, g2_ref, g3_ref, wi_ref, wo_ref, ww_ref, wn_ref, sems, t1_ref, e1_ref,
    ) = refs[16:]
    targets = (
        cen_ref, st_ref, g0_ref, g1_ref, g2_ref, g3_ref, wi_ref, wo_ref, ww_ref, wn_ref,
        ct_ref, cq_ref, ckv_ref, co_ref, cw_ref, cn_ref,
    )
    copies = [pltpu.make_async_copy(a, b, sems.at[i]) for i, (a, b) in enumerate(zip(sources, targets))]
    for copy in copies:
        copy.start()
    w1_ref[...] = base_weights(True)
    for ref in (o1_ref, ww1_ref, wn1_ref, gain_ref, t1_ref):
        zeros(ref)
    flip = jnp.where(rows_of((32, 32)) == lanes((32, 32)), 1.0, 0.0).astype(BF)
    pick = jnp.where(lanes((32, 512)) // 16 == 30 - rows_of((32, 512)), 1.0, 0.0).astype(BF)
    amount = 15 - lanes((192, 512)) % 16
    for copy in copies[:2]:
        copy.wait()
    low_ref[...] = cen_ref[:, :SHIFT]
    high_ref[...] = cen_ref[:, 24:]
    for h in range(HEADS):
        t1_ref[h * 32 : h * 32 + 31, :31] = st_ref[h]
    e1_ref[...] = shear(t1_ref, flip, 32, pick, amount, (8,))
    for h in range(HEADS):
        for qy in range(WIN):
            b1_ref[h, qy * 16 : qy * 16 + 16, :] = e1_ref[h * 24 : h * 24 + 16, (15 - qy) * 16 : (15 - qy) * 16 + 256]
    for copy in copies[2:]:
        copy.wait()
    widened(w1_ref, wi_ref, 0)
    place(o1_ref, wo_ref[:90], 0, 0)
    place(o1_ref, wo_ref[90:], 128, 0)
    place(ww1_ref, ww_ref[...], 0, 0)
    place(wn1_ref, wn_ref[...], 0, 0)
    for i, src in enumerate((g0_ref, g1_ref, g2_ref, g3_ref)):
        gain_ref[i : i + 1, :C] = src[...] * (HALF_ROOT if i % 2 else 1.0)


def cross_tables(
    ct_ref, cq_ref, ckv_ref, co_ref, cw_ref, cn_ref, b2_ref, br_ref, w2_ref, o2_ref, ww2_ref, wn2_ref, t2_ref, e2_ref
):
    w2_ref[...] = base_weights(False)
    for ref in (o2_ref, ww2_ref, wn2_ref, t2_ref):
        zeros(ref)
    widened(w2_ref, cq_ref, 0)
    widened(w2_ref, ckv_ref, 2)
    place(o2_ref, co_ref[:90], 0, 0)
    place(o2_ref, co_ref[90:], 128, 0)
    place(ww2_ref, cw_ref[...], 0, 0)
    place(wn2_ref, cn_ref[...], 0, 0)
    for h in range(HEADS):
        t2_ref[h * 40 : h * 40 + 39, :39] = ct_ref[h]
    flip = jnp.where(rows_of((40, 40)) == 38 - lanes((40, 40)), 1.0, 0.0).astype(BF)
    lane = lanes((40, 1024))
    row = rows_of((40, 1024))
    pick = jnp.where((lane >= row * 24) & (lane < row * 24 + 24), 1.0, 0.0).astype(BF)
    lane1 = lanes((1, 1024)).astype(F32)
    kx = lane1 - 24.0 * jnp.floor((lane1 + 0.5) * (1.0 / 24.0))
    amount = jnp.broadcast_to(23 - kx.astype(jnp.int32), (240, 1024))
    e2_ref[...] = shear(t2_ref, flip, 40, pick, amount, (16, 8))
    for half in range(2):
        br_ref[half, :, 3 * REST :] = jnp.full((256, 256 - 3 * REST), LOW, F32)
    for h in range(HEADS):
        for qy in range(WIN):
            bias = e2_ref[h * 24 : h * 24 + 16, (15 - qy) * 24 : (15 - qy) * 24 + 576]
            b2_ref[h, qy * 16 : qy * 16 + 16, :] = bias[:, :KEYS]
            br_ref[h // 3, qy * 16 : qy * 16 + 16, h % 3 * REST : h % 3 * REST + REST] = bias[:, KEYS:]


def norm(x, gain, real, inside=None):
    x0 = x[:, :128]
    x1 = jnp.where(real, x[:, 128:], 0.0)
    mean = jnp.sum(x0 + x1, axis=-1, keepdims=True) * (1.0 / C)
    c0 = x0 - mean
    c1 = jnp.where(real, x1 - mean, 0.0)
    spread = jnp.sum(c0 * c0 + c1 * c1, axis=-1, keepdims=True) * (1.0 / C)
    inv = lax.rsqrt(spread + EPS)
    if inside is not None:
        inv = inv * inside
    return c0 * inv * gain[:, :128], c1 * inv * gain[:, 128:]


def mlp(res, gain, real, widen, narrow):
    n0, n1 = norm(res, gain, real)
    normed = jnp.concatenate([n0, n1], axis=1).astype(BF)
    y = mm(normed, widen)
    hidden = (y + y * lax.erf(y)).astype(BF)
    return res + mm(hidden, narrow, NT) * HALF_ROOT


def attend(jobs, s_refs):
    lane = lanes((1, 128))
    order = [(job, h) for h in range(HEADS) for job in range(len(jobs))]

    def start(n):
        job, h = order[n]
        half, t = divmod(h, 3)
        queries, keys, _, bias = jobs[job]
        own = ((lane >= 30 * t) & (lane < 30 * t + 30)) | (lane == KFLAG)
        scores = mm(queries(half) * jnp.where(own, 1.0, 0.0).astype(BF), keys(half), NT) + bias(h)
        s_refs[n % s_refs.shape[0]] = scores
        return jnp.max(scores, axis=-1, keepdims=True)

    mixed = [[None, None] for _ in jobs]
    depth = s_refs.shape[0] - 1
    peaks = [start(n) for n in range(depth)]
    for n, (job, h) in enumerate(order):
        if n + depth < len(order):
            peaks.append(start(n + depth))
        half, t = divmod(h, 3)
        weights = jnp.exp2(s_refs[n % (depth + 1)] - peaks[n]).astype(BF)
        out = mm(weights, jobs[job][2](half))
        out = out[:, :128] / out[:, 128:]
        mixed[job][half] = out if t == 0 else jnp.where(lane >= 30 * t, out, mixed[job][half])
    return [jnp.concatenate(pair, axis=1).astype(BF) for pair in mixed]


def cross_attend(count, q_ref, kv_ref, kr_ref, vr_ref, b2_ref, br_ref, s_ref, sr_ref):
    lane = lanes((1, 128))
    lane2 = lanes((1, 256)) % 128
    low = lane < REST
    order = [(j, h) for h in range(HEADS) for j in range(count)]
    depth = s_ref.shape[0] - 1

    def start(n):
        j, h = order[n]
        half, t = divmod(h, 3)
        part = slice(half * 128, half * 128 + 128)
        queries, keys = q_ref[j, :, part], kv_ref[j, :, part]
        if t == 0:
            sr_ref[j, half] = mm(queries, kr_ref[j, half], NT) + br_ref[half]
        own = (lane >= 30 * t) & (lane < 30 * t + 30)
        scores = mm(queries * jnp.where(own, 1.0, 0.0).astype(BF), keys, NT) + b2_ref[h]
        s_ref[n % (depth + 1)] = scores
        rest = sr_ref[j, half, :, t // 2 * 128 : t // 2 * 128 + 128]
        top = jnp.where(~low if t == 1 else low, rest, LOW)
        for k in range(4):
            top = jnp.maximum(top, scores[:, 128 * k : 128 * k + 128])
        return jnp.max(top, axis=-1, keepdims=True)

    peaks = [start(n) for n in range(depth)]
    total = {}
    mixed = [[None, None] for _ in range(count)]
    for n, (j, h) in enumerate(order):
        if n + depth < len(order):
            peaks.append(start(n + depth))
        half, t = divmod(h, 3)
        weights = jnp.exp2(s_ref[n % (depth + 1)] - peaks[n]).astype(BF)
        out = mm(weights, kv_ref[j, :, 256 + half * 256 : 512 + half * 256])
        total[j] = out if t == 0 else jnp.where(lane2 >= 30 * t, out, total[j])
        if t == 2:
            first = jnp.where(low, peaks[n - 2 * count], peaks[n - count])
            rest = [jnp.exp2(sr_ref[j, half, :, :128] - first), jnp.exp2(sr_ref[j, half, :, 128:] - peaks[n])]
            out = total[j] + mm(jnp.concatenate(rest, axis=1).astype(BF), vr_ref[j, half])
            mixed[j][half] = out[:, :128] / out[:, 128:]
    return [jnp.concatenate(pair, axis=1).astype(BF) for pair in mixed]


def wanted(values, i, side):
    values = values.reshape(16, 16, 256)[4 * (1 - i) : 4 * (1 - i) + 12]
    if side is None:
        return values.reshape(192, 256)
    inner, outer = (values[:, 8:], values[:, :8]) if side == 0 else (values[:, :8], values[:, 8:])
    outer = outer.reshape(6, 2, 8, 256)
    even, odd = outer[:, 0].reshape(48, 256), outer[:, 1].reshape(48, 256)
    place_in = rows_of((48, 256)) % 8
    keep = place_in >= 4 if side == 0 else place_in < 4
    merged = jnp.where(keep, even, pltpu.roll(odd, 44 if side == 0 else 4, 0))
    return jnp.concatenate([inner.reshape(96, 256), merged], axis=0)


def spread(values, side):
    if side is None:
        return values.reshape(12, 16, 256)
    inner, even = values[:96].reshape(12, 8, 256), values[96:]
    odd = pltpu.roll(even, 4 if side == 0 else 44, 0)
    outer = jnp.concatenate([even.reshape(6, 1, 8, 256), odd.reshape(6, 1, 8, 256)], axis=1).reshape(12, 8, 256)
    return jnp.concatenate([outer, inner] if side == 0 else [inner, outer], axis=1)


def shifted_windows(windows, x_ref, gain_ref, b1_ref, w1_ref, o1_ref, ww1_ref, wn1_ref, q_ref, kv_ref, s_refs):
    real = lanes((1, 128)) < C - 128
    jobs = []
    count = len(windows)
    x = x_ref[...].reshape(count * 256, 256)
    n0, n1 = norm(x, gain_ref[0:1, :], real)
    n1 = jnp.where(real, n1, x[:, 128:])
    normed = jnp.concatenate([n0, n1], axis=1)
    kv = mm(normed.astype(BF), w1_ref[:, 256:]).astype(BF).reshape(count, 256, 512)
    ones = jnp.ones((count, 256, 128), BF)
    kv_ref[:, :, :384] = kv[:, :, :384]
    kv_ref[:, :, 384:512] = ones
    kv_ref[:, :, 512:640] = kv[:, :, 384:]
    kv_ref[:, :, 640:] = ones
    pixels_of = lambda all_rows, w: wanted(all_rows[256 * w[0] : 256 * w[0] + 256], w[1], w[2])
    q = mm(jnp.concatenate([pixels_of(normed, w) for w in windows], axis=0).astype(BF), w1_ref[:, :256])
    size = q.shape[0] // count
    q_ref[...] = (q * SCALE).astype(BF).reshape(count, size, 256)
    for slot, i, side in windows:
        jobs.append(
            (
                lambda half, slot=slot: q_ref[slot, :, half * 128 : half * 128 + 128],
                lambda half, slot=slot: kv_ref[slot, :, half * 128 : half * 128 + 128],
                lambda half, slot=slot: kv_ref[slot, :, 256 + half * 256 : 512 + half * 256],
                lambda h, i=i, side=side: wanted(b1_ref[h], i, side),
            )
        )
    mixed = jnp.concatenate(attend(jobs, s_refs), axis=0)
    x = x_ref[...].reshape(count * 256, 256)
    res = jnp.concatenate([pixels_of(x, w) for w in windows], axis=0) + mm(mixed, o1_ref[...])
    out = mlp(res, gain_ref[1:2, :], real, ww1_ref[...], wn1_ref[...]).astype(BF).astype(F32)
    return [spread(out[size * k : size * k + size], w[2]) for k, w in enumerate(windows)]


def put(x_ref, slot, y0, x0, piece, flag):
    lane1 = lanes((1, 128))
    ny, nx = piece.shape[0], piece.shape[1]
    x_ref[slot, y0 : y0 + ny, x0 : x0 + nx, 128:] = jnp.broadcast_to(
        jnp.where(lane1 == FLAG - 128, flag, jnp.where(lane1 == ONE - 128, 1.0, 0.0)), (ny, nx, 128)
    )
    x_ref[slot, y0 : y0 + ny, x0 : x0 + nx, :C] = piece.astype(F32)


def edges():
    row, col = lax.axis_index("rows"), lax.axis_index("cols")
    return row, col, lax.axis_size("rows") - 1, lax.axis_size("cols") - 1


def flag_of(condition):
    return jnp.where(condition, 1.0, 0.0)


def middle_kernel(
    cen_ref, ra_ref, rb_ref, gain_ref, b1_ref, w1_ref, o1_ref, ww1_ref, wn1_ref, ct_ref, cq_ref, ckv_ref, co_ref, cw_ref, cn_ref,
    out_ref, strip_ref, b2_ref, br_ref, w2_ref, o2_ref, ww2_ref, wn2_ref,
    x_ref, q_ref, kv_ref, s_ref, t2_ref, e2_ref,
):
    row, col, last_row, _ = edges()
    odd = lax.rem(row, 2) == 1
    top = jnp.where(odd, ra_ref[...], rb_ref[...])
    bot = jnp.where(odd, rb_ref[...], ra_ref[...])
    low = lax.rem(col, 2) == 1
    strip_ref[:8] = jnp.where(low, top[:, :8], top[:, 24:])
    strip_ref[8:24] = jnp.where(low, cen_ref[:, :8], cen_ref[:, 24:])
    strip_ref[24:] = jnp.where(low, bot[:, :8], bot[:, 24:])
    top, bot = top[:, 8:24], bot[:, 8:24]
    put(x_ref, 0, 0, 0, top, flag_of(row == 0))
    put(x_ref, 0, 8, 0, cen_ref[:8, 8:24], 0.0)
    put(x_ref, 1, 0, 0, cen_ref[8:, 8:24], 0.0)
    put(x_ref, 1, 8, 0, bot, flag_of(row == last_row))
    cross_tables(
        ct_ref, cq_ref, ckv_ref, co_ref, cw_ref, cn_ref, b2_ref, br_ref, w2_ref, o2_ref, ww2_ref, wn2_ref, t2_ref, e2_ref
    )
    outs = shifted_windows(
        [(0, 0, None), (1, 1, None)], x_ref, gain_ref, b1_ref, w1_ref, o1_ref, ww1_ref, wn1_ref, q_ref, kv_ref, s_ref
    )
    out_ref[:12] = outs[0]
    out_ref[12:] = outs[1]


def main_kernel(
    cen_ref, ra_ref, rb_ref, ca_ref, cb_ref, mid_ref, gain_ref,
    b1_ref, b2_ref, br_ref, w1_ref, o1_ref, ww1_ref, wn1_ref, w2_ref, o2_ref, ww2_ref, wn2_ref,
    out_ref,
    x_ref, q_ref, kv_ref, s_ref, bo_ref, a3_ref, kvs_ref, q2_ref, kv2_ref, kr_ref, vr_ref, s2_ref, sr_ref,
):
    row, col, last_row, last_col = edges()
    real = lanes((1, 128)) < C - 128
    one1 = jnp.where(lanes((1, 128)) == ONE - 128, 1.0, 0.0)
    row_odd = lax.rem(row, 2) == 1
    col_odd = lax.rem(col, 2) == 1
    out_top = flag_of(row == 0)
    out_bot = flag_of(row == last_row)
    out_lef = flag_of(col == 0)
    out_rig = flag_of(col == last_col)
    top = jnp.where(row_odd, ra_ref[...], rb_ref[...])
    bot = jnp.where(row_odd, rb_ref[...], ra_ref[...])
    lef = jnp.where(col_odd, ca_ref[...], cb_ref[...])
    rig = jnp.where(col_odd, cb_ref[...], ca_ref[...])
    both = jnp.maximum
    put(x_ref, 0, 0, 0, lef[:8], both(out_top, out_lef))
    put(x_ref, 0, 0, 8, top[:, :8], out_top)
    put(x_ref, 0, 8, 0, lef[8:16], out_lef)
    put(x_ref, 0, 8, 8, cen_ref[:8, :8], 0.0)
    put(x_ref, 1, 0, 0, lef[16:24], out_lef)
    put(x_ref, 1, 0, 8, cen_ref[8:, :8], 0.0)
    put(x_ref, 1, 8, 0, lef[24:], both(out_bot, out_lef))
    put(x_ref, 1, 8, 8, bot[:, :8], out_bot)
    put(x_ref, 2, 0, 0, top[:, 24:], out_top)
    put(x_ref, 2, 0, 8, rig[:8], both(out_top, out_rig))
    put(x_ref, 2, 8, 0, cen_ref[:8, 24:], 0.0)
    put(x_ref, 2, 8, 8, rig[8:16], out_rig)
    put(x_ref, 3, 0, 0, cen_ref[8:, 24:], 0.0)
    put(x_ref, 3, 0, 8, rig[16:24], out_rig)
    put(x_ref, 3, 8, 0, bot[:, 24:], out_bot)
    put(x_ref, 3, 8, 8, rig[24:], both(out_bot, out_rig))

    outs = shifted_windows(
        [(0, 0, 0), (1, 1, 0), (2, 0, 1), (3, 1, 1)],
        x_ref, gain_ref, b1_ref, w1_ref, o1_ref, ww1_ref, wn1_ref, q_ref, kv_ref, s_ref,
    )
    bo_ref[:12, :16] = outs[0]
    bo_ref[12:, :16] = outs[1]
    bo_ref[:, 16:32] = mid_ref[...]
    bo_ref[:12, 32:] = outs[2]
    bo_ref[12:, 32:] = outs[3]

    rows_in = jnp.concatenate(
        [jnp.full((4, 1, 1), 1.0 - out_top), jnp.ones((16, 1, 1), F32), jnp.full((4, 1, 1), 1.0 - out_bot)], axis=0
    )
    cols_in = jnp.concatenate(
        [jnp.full((1, 8, 1), 1.0 - out_lef), jnp.ones((1, 32, 1), F32), jnp.full((1, 8, 1), 1.0 - out_rig)], axis=1
    )
    inside = (rows_in * cols_in).reshape(24 * 48, 1)
    n0, n1 = norm(bo_ref[...].reshape(24 * 48, 256), gain_ref[2:3, :], real, inside)
    a3_ref[:, :, :128] = n0.reshape(24, 48, 128)
    a3_ref[:, :, 128:] = (n1 + one1).reshape(24, 48, 128)

    kvs_ref[...] = mm(a3_ref[:, 4:44, :].reshape(960, 256).astype(BF), w2_ref[:, 256:]).reshape(24, 40, 512)
    lane = lanes((1, 128))
    masks = [jnp.where((lane >= 30 * t) & (lane < 30 * t + 30), 1.0, 0.0).astype(BF) for t in range(3)]
    kr_ref[:, :, 3 * REST :, :] = jnp.zeros((2, 2, 256 - 3 * REST, 128), BF)
    vr_ref[:, :, 3 * REST :, :] = jnp.zeros((2, 2, 256 - 3 * REST, 256), BF)
    for j in range(2):
        q = a3_ref[4:20, 8 + 16 * j : 24 + 16 * j, :].reshape(256, 256).astype(BF)
        q2_ref[j] = (mm(q, w2_ref[:, :256]) * SCALE).astype(BF)
        kv = kvs_ref[:, 16 * j : 16 * j + 24, :].reshape(576, 512).astype(BF)
        kv2_ref[j, :, :384] = kv[:KEYS, :384]
        kv2_ref[j, :, 512:640] = kv[:KEYS, 384:]
        kv2_ref[j, :, 384:512] = jnp.ones((KEYS, 128), BF)
        kv2_ref[j, :, 640:] = jnp.ones((KEYS, 128), BF)
        for half in range(2):
            for t in range(3):
                rows = slice(t * REST, t * REST + REST)
                kr_ref[j, half, rows, :] = kv[KEYS:, 128 * half : 128 * half + 128] * masks[t]
                vr_ref[j, half, rows, :128] = kv[KEYS:, 256 + 128 * half : 384 + 128 * half] * masks[t]
                vr_ref[j, half, rows, 128:] = jnp.broadcast_to(masks[t], (REST, 128))
    mixed = jnp.concatenate(cross_attend(2, q2_ref, kv2_ref, kr_ref, vr_ref, b2_ref, br_ref, s2_ref, sr_ref), axis=0)
    own = [bo_ref[4:20, 8 + 16 * j : 24 + 16 * j, :].reshape(256, 256) for j in range(2)]
    res = jnp.concatenate(own, axis=0) + mm(mixed, o2_ref[...])
    out = mlp(res, gain_ref[3:4, :], real, ww2_ref[...], wn2_ref[...])
    for j in range(2):
        part = out[256 * j : 256 * j + 256].reshape(16, 16, 256)
        out_ref[:, 16 * j : 16 * j + 16, :] = part[:, :, :C].astype(BF)


def pairs(axis, first):
    found = []
    for i in range(first, lax.axis_size(axis) - 1, 2):
        found += [(i, i + 1), (i + 1, i)]
    return found


def per_device(
    pixels, shift_prenorm, shift_inputs, shift_table, shift_output, shift_postnorm, shift_widen, shift_narrow,
    cross_prenorm, cross_query, cross_keyval, cross_table, cross_output, cross_postnorm, cross_widen, cross_narrow,
):
    odd = lax.axis_index("rows") % 2 == 1
    ra = lax.ppermute(jnp.where(odd, pixels[:SHIFT], pixels[SHIFT:]), "rows", pairs("rows", 0))
    rb = lax.ppermute(jnp.where(odd, pixels[SHIFT:], pixels[:SHIFT]), "rows", pairs("rows", 1))
    top = jnp.where(odd, ra, rb)
    bot = jnp.where(odd, rb, ra)
    sds = jax.ShapeDtypeStruct
    vmem = pl.BlockSpec(memory_space=pltpu.VMEM)
    hbm = pl.BlockSpec(memory_space=pltpu.HBM)
    firsts = (
        pixels, shift_table,
        shift_prenorm.reshape(1, C), shift_postnorm.reshape(1, C), cross_prenorm.reshape(1, C), cross_postnorm.reshape(1, C),
        shift_inputs, shift_output, shift_widen, shift_narrow.T,
    )
    seconds = (cross_table, cross_query, cross_keyval, cross_output, cross_widen, cross_narrow.T)
    strip = (pixels.shape[0], SHIFT, C)
    like = lambda x: sds(x.shape, x.dtype)
    center, *rest = pl.pallas_call(
        tables_kernel,
        out_shape=(
            like(pixels), *map(like, seconds), sds(strip, BF), sds(strip, BF), sds((8, 256), F32), sds((HEADS, 256, 256), F32),
            sds((256, 768), BF), sds((256, 256), BF), sds((256, 384), BF), sds((256, 384), BF),
        ),
        in_specs=[hbm] * 16,
        out_specs=[vmem] * 15,
        scratch_shapes=[pltpu.VMEM(x.shape, x.dtype) for x in firsts[1:]]
        + [pltpu.SemaphoreType.DMA((16,)), pltpu.VMEM((192, 32), F32), pltpu.VMEM((144, 512), F32)],
        cost_estimate=pl.CostEstimate(flops=100_000_000, bytes_accessed=5_000_000, transcendentals=0),
        compiler_params=pltpu.CompilerParams(vmem_limit_bytes=16 * 2**20),
        name="tables",
    )(*[pltpu.with_memory_space_constraint(x, pltpu.HBM) for x in (*firsts, *seconds)])
    raw, (low, high, gains, b1, w1, o1, ww1, wn1) = rest[:6], rest[6:]

    column_odd = lax.axis_index("cols") % 2 == 1
    pick = lambda rows: jnp.where(column_odd, rows[:, 24:], rows[:, :SHIFT])
    strip = jnp.concatenate([pick(top), jnp.where(column_odd, high, low), pick(bot)], axis=0)
    cb = lax.ppermute(strip, "cols", pairs("cols", 1))
    middle, strip, b2, br, w2, o2, ww2, wn2 = pl.pallas_call(
        middle_kernel,
        out_shape=(
            sds((24, 16, 256), F32), like(strip), sds((HEADS, 256, KEYS), F32), sds((2, 256, 256), F32), sds((256, 768), BF),
            sds((256, 256), BF), sds((256, 384), BF), sds((256, 384), BF),
        ),
        in_specs=[vmem] * 15,
        out_specs=[vmem] * 8,
        scratch_shapes=[
            pltpu.VMEM((2, 16, 16, 256), F32), pltpu.VMEM((2, 192, 256), BF), pltpu.VMEM((2, 256, 768), BF),
            pltpu.VMEM((AHEAD + 1, 192, 256), F32), pltpu.VMEM((240, 40), F32), pltpu.VMEM((144, 1024), F32),
        ],
        cost_estimate=pl.CostEstimate(flops=2_000_000_000, bytes_accessed=8_000_000, transcendentals=1_000_000),
        compiler_params=pltpu.CompilerParams(vmem_limit_bytes=20 * 2**20),
        name="middle",
    )(center, ra, rb, gains, b1, w1, o1, ww1, wn1, *raw)
    ca = lax.ppermute(strip, "cols", pairs("cols", 0))
    return pl.pallas_call(
        main_kernel,
        out_shape=sds(pixels.shape, BF),
        in_specs=[vmem] * 18,
        out_specs=vmem,
        scratch_shapes=[
            pltpu.VMEM((4, 16, 16, 256), F32), pltpu.VMEM((4, 144, 256), BF), pltpu.VMEM((4, 256, 768), BF),
            pltpu.VMEM((AHEAD + 1, 144, 256), F32),
            pltpu.VMEM((24, 48, 256), F32), pltpu.VMEM((24, 48, 256), F32), pltpu.VMEM((24, 40, 512), F32),
            pltpu.VMEM((2, 256, 256), BF), pltpu.VMEM((2, KEYS, 768), BF),
            pltpu.VMEM((2, 2, 256, 128), BF), pltpu.VMEM((2, 2, 256, 256), BF),
            pltpu.VMEM((CROSS_AHEAD + 1, 256, KEYS), F32), pltpu.VMEM((2, 2, 256, 256), F32),
        ],
        cost_estimate=pl.CostEstimate(flops=10_000_000_000, bytes_accessed=8_000_000, transcendentals=4_000_000),
        compiler_params=pltpu.CompilerParams(vmem_limit_bytes=32 * 2**20),
        name="blocks",
    )(center, ra, rb, ca, cb, middle, gains, b1, b2, br, w1, o1, ww1, wn1, w2, o2, ww2, wn2)


def solution(mesh):
    return jax.shard_map(
        per_device,
        mesh=mesh,
        in_specs=(P("rows", "cols", None),) + (P(),) * 15,
        out_specs=P("rows", "cols", None),
        check_vma=False,
    )
```

```python
import jax
import jax.numpy as jnp
from jax import lax
from jax.experimental import pallas as pl
from jax.experimental.pallas import tpu as pltpu
from jax.sharding import PartitionSpec as P

C = 180
HEADS = 6
HEAD_DIM = 30
WIN = 16
SHIFT = 8
EPS = 1e-05
LOG2E = 1.4426950408889634
SCALE = HEAD_DIM ** (-0.5) * LOG2E
HALF_ROOT = 0.7071067811865476
LOW = -1e30
FLAG = 180
ONE = 181
KFLAG = 100
KEYS = 512
REST = 64
AHEAD = 4
CROSS_AHEAD = 1
BF = jnp.bfloat16
F32 = jnp.float32


def mm(a, b, dims=((1,), (0,)), precision=None):
    return lax.dot_general(a, b, (dims, ((), ())), preferred_element_type=F32, precision=precision)


NT = ((1,), (1,))


def lanes(shape):
    return lax.broadcasted_iota(jnp.int32, shape, len(shape) - 1)


def rows_of(shape):
    return lax.broadcasted_iota(jnp.int32, shape, len(shape) - 2)


def place(dst_ref, src, row, col):
    dst_ref[row : row + src.shape[0], col : col + src.shape[1]] = src


def exact_parts(x):
    first = x.astype(BF)
    rest = x - first.astype(F32)
    second = rest.astype(BF)
    return first, second, (rest - second.astype(F32)).astype(BF)


def shear(table_ref, flip, side, pick, amount, bits):
    top = HEADS * side
    y = None
    for part in exact_parts(table_ref[...] * LOG2E):
        turned = [mm(flip, part[h * side : (h + 1) * side], NT) for h in range(HEADS)]
        term = mm(jnp.concatenate(turned, axis=0).astype(BF), pick)
        y = term if y is None else y + term
    for bit in bits:
        y = jnp.where((amount & bit) != 0, pltpu.roll(y, top - bit, 0), y)
    y = jnp.concatenate([y[h * side : h * side + 24] for h in range(HEADS)], axis=0)
    amount = jnp.broadcast_to(amount[:1], y.shape)
    for bit in (4, 2, 1):
        y = jnp.where((amount & bit) != 0, pltpu.roll(y, HEADS * 24 - bit, 0), y)
    return y


def widened(dst_ref, src_ref, first):
    for k in range(src_ref.shape[1] // 90):
        place(dst_ref, src_ref[:, 90 * k : 90 * k + 90], 0, 128 * (first + k))


def base_weights(flagged):
    r = rows_of((256, 768))
    c = lanes((256, 768))
    base = jnp.where((r == ONE) & ((c == KFLAG) | (c == 128 + KFLAG)), 1.0, 0.0)
    if flagged:
        base = jnp.where((r == FLAG) & ((c == 256 + KFLAG) | (c == 384 + KFLAG)), LOW, base)
    return base.astype(BF)


def zeros(ref):
    ref[...] = jnp.zeros(ref.shape, ref.dtype)


def tables_kernel(*refs):
    sources = refs[:16]
    (
        cen_ref, ct_ref, cq_ref, ckv_ref, co_ref, cw_ref, cn_ref,
        low_ref, high_ref, gain_ref, b1_ref, w1_ref, o1_ref, ww1_ref, wn1_ref,
        st_ref, g0_ref, g1_ref, g2_ref, g3_ref, wi_ref, wo_ref, ww_ref, wn_ref, sems, t1_ref, e1_ref,
    ) = refs[16:]
    targets = (
        cen_ref, st_ref, g0_ref, g1_ref, g2_ref, g3_ref, wi_ref, wo_ref, ww_ref, wn_ref,
        ct_ref, cq_ref, ckv_ref, co_ref, cw_ref, cn_ref,
    )
    copies = [pltpu.make_async_copy(a, b, sems.at[i]) for i, (a, b) in enumerate(zip(sources, targets))]
    for copy in (copies[1], copies[0], *copies[2:]):
        copy.start()
    w1_ref[...] = base_weights(True)
    for ref in (o1_ref, ww1_ref, wn1_ref, gain_ref, t1_ref):
        zeros(ref)
    flip = jnp.where(rows_of((32, 32)) == lanes((32, 32)), 1.0, 0.0).astype(BF)
    pick = jnp.where(lanes((32, 512)) // 16 == 30 - rows_of((32, 512)), 1.0, 0.0).astype(BF)
    amount = 15 - lanes((192, 512)) % 16
    copies[1].wait()
    for h in range(HEADS):
        t1_ref[h * 32 : h * 32 + 31, :31] = st_ref[h]
    e1_ref[...] = shear(t1_ref, flip, 32, pick, amount, (8,))
    for h in range(HEADS):
        for qy in range(WIN):
            b1_ref[h, qy * 16 : qy * 16 + 16, :] = e1_ref[h * 24 : h * 24 + 16, (15 - qy) * 16 : (15 - qy) * 16 + 256]
    for copy in (copies[0], *copies[2:]):
        copy.wait()
    low_ref[...] = cen_ref[:, :SHIFT]
    high_ref[...] = cen_ref[:, 24:]
    widened(w1_ref, wi_ref, 0)
    place(o1_ref, wo_ref[:90], 0, 0)
    place(o1_ref, wo_ref[90:], 128, 0)
    place(ww1_ref, ww_ref[...], 0, 0)
    place(wn1_ref, wn_ref[...], 0, 0)
    for i, src in enumerate((g0_ref, g1_ref, g2_ref, g3_ref)):
        gain_ref[i : i + 1, :C] = src[...] * (HALF_ROOT if i % 2 else 1.0)


def cross_tables(
    ct_ref, cq_ref, ckv_ref, co_ref, cw_ref, cn_ref, b2_ref, br_ref, w2_ref, o2_ref, ww2_ref, wn2_ref, t2_ref, e2_ref
):
    w2_ref[...] = base_weights(False)
    for ref in (o2_ref, ww2_ref, wn2_ref, t2_ref):
        zeros(ref)
    widened(w2_ref, cq_ref, 0)
    widened(w2_ref, ckv_ref, 2)
    place(o2_ref, co_ref[:90], 0, 0)
    place(o2_ref, co_ref[90:], 128, 0)
    place(ww2_ref, cw_ref[...], 0, 0)
    place(wn2_ref, cn_ref[...], 0, 0)
    for h in range(HEADS):
        t2_ref[h * 40 : h * 40 + 39, :39] = ct_ref[h]
    flip = jnp.where(rows_of((40, 40)) == 38 - lanes((40, 40)), 1.0, 0.0).astype(BF)
    lane = lanes((40, 1024))
    row = rows_of((40, 1024))
    pick = jnp.where((lane >= row * 24) & (lane < row * 24 + 24), 1.0, 0.0).astype(BF)
    lane1 = lanes((1, 1024)).astype(F32)
    kx = lane1 - 24.0 * jnp.floor((lane1 + 0.5) * (1.0 / 24.0))
    amount = jnp.broadcast_to(23 - kx.astype(jnp.int32), (240, 1024))
    e2_ref[...] = shear(t2_ref, flip, 40, pick, amount, (16, 8))
    for half in range(2):
        br_ref[half, :, 3 * REST :] = jnp.full((256, 256 - 3 * REST), LOW, F32)
    for h in range(HEADS):
        for qy in range(WIN):
            bias = e2_ref[h * 24 : h * 24 + 16, (15 - qy) * 24 : (15 - qy) * 24 + 576]
            b2_ref[h, qy * 16 : qy * 16 + 16, :] = bias[:, :KEYS]
            br_ref[h // 3, qy * 16 : qy * 16 + 16, h % 3 * REST : h % 3 * REST + REST] = bias[:, KEYS:]


def norm(x, gain, real, inside=None):
    x0 = x[:, :128]
    x1 = jnp.where(real, x[:, 128:], 0.0)
    mean = jnp.sum(x0 + x1, axis=-1, keepdims=True) * (1.0 / C)
    c0 = x0 - mean
    c1 = jnp.where(real, x1 - mean, 0.0)
    spread = jnp.sum(c0 * c0 + c1 * c1, axis=-1, keepdims=True) * (1.0 / C)
    inv = lax.rsqrt(spread + EPS)
    if inside is not None:
        inv = inv * inside
    return c0 * inv * gain[:, :128], c1 * inv * gain[:, 128:]


def mlp(res, gain, real, widen, narrow):
    n0, n1 = norm(res, gain, real)
    normed = jnp.concatenate([n0, n1], axis=1).astype(BF)
    y = mm(normed, widen)
    hidden = (y + y * lax.erf(y)).astype(BF)
    return res + mm(hidden, narrow, NT) * HALF_ROOT


def attend(jobs, s_refs):
    lane = lanes((1, 128))
    order = [(job, h) for h in range(HEADS) for job in range(len(jobs))]

    def start(n):
        job, h = order[n]
        half, t = divmod(h, 3)
        queries, keys, _, bias = jobs[job]
        own = ((lane >= 30 * t) & (lane < 30 * t + 30)) | (lane == KFLAG)
        scores = mm(queries(half) * jnp.where(own, 1.0, 0.0).astype(BF), keys(half), NT) + bias(h)
        s_refs[n % s_refs.shape[0]] = scores
        return jnp.max(scores, axis=-1, keepdims=True)

    mixed = [[None, None] for _ in jobs]
    depth = s_refs.shape[0] - 1
    peaks = [start(n) for n in range(depth)]
    for n, (job, h) in enumerate(order):
        if n + depth < len(order):
            peaks.append(start(n + depth))
        half, t = divmod(h, 3)
        weights = jnp.exp2(s_refs[n % (depth + 1)] - peaks[n]).astype(BF)
        out = mm(weights, jobs[job][2](half))
        out = out[:, :128] / out[:, 128:]
        mixed[job][half] = out if t == 0 else jnp.where(lane >= 30 * t, out, mixed[job][half])
    return [jnp.concatenate(pair, axis=1).astype(BF) for pair in mixed]


def cross_attend(count, q_ref, kv_ref, kr_ref, vr_ref, b2_ref, br_ref, s_ref, sr_ref):
    lane = lanes((1, 128))
    lane2 = lanes((1, 256)) % 128
    low = lane < REST
    order = [(j, h) for h in range(HEADS) for j in range(count)]
    depth = s_ref.shape[0] - 1

    def start(n):
        j, h = order[n]
        half, t = divmod(h, 3)
        part = slice(half * 128, half * 128 + 128)
        queries, keys = q_ref[j, :, part], kv_ref[j, :, part]
        if t == 0:
            sr_ref[j, half] = mm(queries, kr_ref[j, half], NT) + br_ref[half]
        own = (lane >= 30 * t) & (lane < 30 * t + 30)
        scores = mm(queries * jnp.where(own, 1.0, 0.0).astype(BF), keys, NT) + b2_ref[h]
        s_ref[n % (depth + 1)] = scores
        rest = sr_ref[j, half, :, t // 2 * 128 : t // 2 * 128 + 128]
        top = jnp.where(~low if t == 1 else low, rest, LOW)
        for k in range(4):
            top = jnp.maximum(top, scores[:, 128 * k : 128 * k + 128])
        return jnp.max(top, axis=-1, keepdims=True)

    peaks = [start(n) for n in range(depth)]
    total = {}
    mixed = [[None, None] for _ in range(count)]
    for n, (j, h) in enumerate(order):
        if n + depth < len(order):
            peaks.append(start(n + depth))
        half, t = divmod(h, 3)
        weights = jnp.exp2(s_ref[n % (depth + 1)] - peaks[n]).astype(BF)
        out = mm(weights, kv_ref[j, :, 256 + half * 256 : 512 + half * 256])
        total[j] = out if t == 0 else jnp.where(lane2 >= 30 * t, out, total[j])
        if t == 2:
            first = jnp.where(low, peaks[n - 2 * count], peaks[n - count])
            rest = [jnp.exp2(sr_ref[j, half, :, :128] - first), jnp.exp2(sr_ref[j, half, :, 128:] - peaks[n])]
            out = total[j] + mm(jnp.concatenate(rest, axis=1).astype(BF), vr_ref[j, half])
            mixed[j][half] = out[:, :128] / out[:, 128:]
    return [jnp.concatenate(pair, axis=1).astype(BF) for pair in mixed]


def wanted(values, i, side):
    values = values.reshape(16, 16, 256)[4 * (1 - i) : 4 * (1 - i) + 12]
    if side is None:
        return values.reshape(192, 256)
    inner, outer = (values[:, 8:], values[:, :8]) if side == 0 else (values[:, :8], values[:, 8:])
    outer = outer.reshape(6, 2, 8, 256)
    even, odd = outer[:, 0].reshape(48, 256), outer[:, 1].reshape(48, 256)
    place_in = rows_of((48, 256)) % 8
    keep = place_in >= 4 if side == 0 else place_in < 4
    merged = jnp.where(keep, even, pltpu.roll(odd, 44 if side == 0 else 4, 0))
    return jnp.concatenate([inner.reshape(96, 256), merged], axis=0)


def spread(values, side):
    if side is None:
        return values.reshape(12, 16, 256)
    inner, even = values[:96].reshape(12, 8, 256), values[96:]
    odd = pltpu.roll(even, 4 if side == 0 else 44, 0)
    outer = jnp.concatenate([even.reshape(6, 1, 8, 256), odd.reshape(6, 1, 8, 256)], axis=1).reshape(12, 8, 256)
    return jnp.concatenate([outer, inner] if side == 0 else [inner, outer], axis=1)


def shifted_windows(windows, x_ref, gain_ref, b1_ref, w1_ref, o1_ref, ww1_ref, wn1_ref, q_ref, kv_ref, s_refs):
    real = lanes((1, 128)) < C - 128
    jobs = []
    count = len(windows)
    x = x_ref[...].reshape(count * 256, 256)
    n0, n1 = norm(x, gain_ref[0:1, :], real)
    n1 = jnp.where(real, n1, x[:, 128:])
    normed = jnp.concatenate([n0, n1], axis=1)
    kv = mm(normed.astype(BF), w1_ref[:, 256:]).astype(BF).reshape(count, 256, 512)
    ones = jnp.ones((count, 256, 128), BF)
    kv_ref[:, :, :384] = kv[:, :, :384]
    kv_ref[:, :, 384:512] = ones
    kv_ref[:, :, 512:640] = kv[:, :, 384:]
    kv_ref[:, :, 640:] = ones
    pixels_of = lambda all_rows, w: wanted(all_rows[256 * w[0] : 256 * w[0] + 256], w[1], w[2])
    q = mm(jnp.concatenate([pixels_of(normed, w) for w in windows], axis=0).astype(BF), w1_ref[:, :256])
    size = q.shape[0] // count
    q_ref[...] = (q * SCALE).astype(BF).reshape(count, size, 256)
    for slot, i, side in windows:
        jobs.append(
            (
                lambda half, slot=slot: q_ref[slot, :, half * 128 : half * 128 + 128],
                lambda half, slot=slot: kv_ref[slot, :, half * 128 : half * 128 + 128],
                lambda half, slot=slot: kv_ref[slot, :, 256 + half * 256 : 512 + half * 256],
                lambda h, i=i, side=side: wanted(b1_ref[h], i, side),
            )
        )
    mixed = jnp.concatenate(attend(jobs, s_refs), axis=0)
    x = x_ref[...].reshape(count * 256, 256)
    res = jnp.concatenate([pixels_of(x, w) for w in windows], axis=0) + mm(mixed, o1_ref[...])
    out = mlp(res, gain_ref[1:2, :], real, ww1_ref[...], wn1_ref[...]).astype(BF).astype(F32)
    return [spread(out[size * k : size * k + size], w[2]) for k, w in enumerate(windows)]


def put(x_ref, slot, y0, x0, piece, flag):
    lane1 = lanes((1, 128))
    ny, nx = piece.shape[0], piece.shape[1]
    x_ref[slot, y0 : y0 + ny, x0 : x0 + nx, 128:] = jnp.broadcast_to(
        jnp.where(lane1 == FLAG - 128, flag, jnp.where(lane1 == ONE - 128, 1.0, 0.0)), (ny, nx, 128)
    )
    x_ref[slot, y0 : y0 + ny, x0 : x0 + nx, :C] = piece.astype(F32)


def edges():
    row, col = lax.axis_index("rows"), lax.axis_index("cols")
    return row, col, lax.axis_size("rows") - 1, lax.axis_size("cols") - 1


def flag_of(condition):
    return jnp.where(condition, 1.0, 0.0)


def middle_kernel(
    cen_ref, ra_ref, rb_ref, gain_ref, b1_ref, w1_ref, o1_ref, ww1_ref, wn1_ref, ct_ref, cq_ref, ckv_ref, co_ref, cw_ref, cn_ref,
    out_ref, strip_ref, b2_ref, br_ref, w2_ref, o2_ref, ww2_ref, wn2_ref,
    x_ref, q_ref, kv_ref, s_ref, t2_ref, e2_ref,
):
    row, col, last_row, _ = edges()
    odd = lax.rem(row, 2) == 1
    top = jnp.where(odd, ra_ref[...], rb_ref[...])
    bot = jnp.where(odd, rb_ref[...], ra_ref[...])
    low = lax.rem(col, 2) == 1
    strip_ref[:8] = jnp.where(low, top[:, :8], top[:, 24:])
    strip_ref[8:24] = jnp.where(low, cen_ref[:, :8], cen_ref[:, 24:])
    strip_ref[24:] = jnp.where(low, bot[:, :8], bot[:, 24:])
    top, bot = top[:, 8:24], bot[:, 8:24]
    put(x_ref, 0, 0, 0, top, flag_of(row == 0))
    put(x_ref, 0, 8, 0, cen_ref[:8, 8:24], 0.0)
    put(x_ref, 1, 0, 0, cen_ref[8:, 8:24], 0.0)
    put(x_ref, 1, 8, 0, bot, flag_of(row == last_row))
    cross_tables(
        ct_ref, cq_ref, ckv_ref, co_ref, cw_ref, cn_ref, b2_ref, br_ref, w2_ref, o2_ref, ww2_ref, wn2_ref, t2_ref, e2_ref
    )
    outs = shifted_windows(
        [(0, 0, None), (1, 1, None)], x_ref, gain_ref, b1_ref, w1_ref, o1_ref, ww1_ref, wn1_ref, q_ref, kv_ref, s_ref
    )
    out_ref[:12] = outs[0]
    out_ref[12:] = outs[1]


def main_kernel(
    cen_ref, ra_ref, rb_ref, ca_ref, cb_ref, mid_ref, gain_ref,
    b1_ref, b2_ref, br_ref, w1_ref, o1_ref, ww1_ref, wn1_ref, w2_ref, o2_ref, ww2_ref, wn2_ref,
    out_ref,
    x_ref, q_ref, kv_ref, s_ref, bo_ref, a3_ref, kvs_ref, q2_ref, kv2_ref, kr_ref, vr_ref, s2_ref, sr_ref,
):
    row, col, last_row, last_col = edges()
    real = lanes((1, 128)) < C - 128
    one1 = jnp.where(lanes((1, 128)) == ONE - 128, 1.0, 0.0)
    row_odd = lax.rem(row, 2) == 1
    col_odd = lax.rem(col, 2) == 1
    out_top = flag_of(row == 0)
    out_bot = flag_of(row == last_row)
    out_lef = flag_of(col == 0)
    out_rig = flag_of(col == last_col)
    top = jnp.where(row_odd, ra_ref[...], rb_ref[...])
    bot = jnp.where(row_odd, rb_ref[...], ra_ref[...])
    lef = jnp.where(col_odd, ca_ref[...], cb_ref[...])
    rig = jnp.where(col_odd, cb_ref[...], ca_ref[...])
    both = jnp.maximum
    put(x_ref, 0, 0, 0, lef[:8], both(out_top, out_lef))
    put(x_ref, 0, 0, 8, top[:, :8], out_top)
    put(x_ref, 0, 8, 0, lef[8:16], out_lef)
    put(x_ref, 0, 8, 8, cen_ref[:8, :8], 0.0)
    put(x_ref, 1, 0, 0, lef[16:24], out_lef)
    put(x_ref, 1, 0, 8, cen_ref[8:, :8], 0.0)
    put(x_ref, 1, 8, 0, lef[24:], both(out_bot, out_lef))
    put(x_ref, 1, 8, 8, bot[:, :8], out_bot)
    put(x_ref, 2, 0, 0, top[:, 24:], out_top)
    put(x_ref, 2, 0, 8, rig[:8], both(out_top, out_rig))
    put(x_ref, 2, 8, 0, cen_ref[:8, 24:], 0.0)
    put(x_ref, 2, 8, 8, rig[8:16], out_rig)
    put(x_ref, 3, 0, 0, cen_ref[8:, 24:], 0.0)
    put(x_ref, 3, 0, 8, rig[16:24], out_rig)
    put(x_ref, 3, 8, 0, bot[:, 24:], out_bot)
    put(x_ref, 3, 8, 8, rig[24:], both(out_bot, out_rig))

    outs = shifted_windows(
        [(0, 0, 0), (1, 1, 0), (2, 0, 1), (3, 1, 1)],
        x_ref, gain_ref, b1_ref, w1_ref, o1_ref, ww1_ref, wn1_ref, q_ref, kv_ref, s_ref,
    )
    bo_ref[:12, :16] = outs[0]
    bo_ref[12:, :16] = outs[1]
    bo_ref[:, 16:32] = mid_ref[...]
    bo_ref[:12, 32:] = outs[2]
    bo_ref[12:, 32:] = outs[3]

    rows_in = jnp.concatenate(
        [jnp.full((4, 1, 1), 1.0 - out_top), jnp.ones((16, 1, 1), F32), jnp.full((4, 1, 1), 1.0 - out_bot)], axis=0
    )
    cols_in = jnp.concatenate(
        [jnp.full((1, 8, 1), 1.0 - out_lef), jnp.ones((1, 32, 1), F32), jnp.full((1, 8, 1), 1.0 - out_rig)], axis=1
    )
    inside = (rows_in * cols_in).reshape(24 * 48, 1)
    n0, n1 = norm(bo_ref[...].reshape(24 * 48, 256), gain_ref[2:3, :], real, inside)
    a3_ref[:, :, :128] = n0.reshape(24, 48, 128)
    a3_ref[:, :, 128:] = (n1 + one1).reshape(24, 48, 128)

    kvs_ref[...] = mm(a3_ref[:, 4:44, :].reshape(960, 256).astype(BF), w2_ref[:, 256:]).reshape(24, 40, 512)
    lane = lanes((1, 128))
    masks = [jnp.where((lane >= 30 * t) & (lane < 30 * t + 30), 1.0, 0.0).astype(BF) for t in range(3)]
    kr_ref[:, :, 3 * REST :, :] = jnp.zeros((2, 2, 256 - 3 * REST, 128), BF)
    vr_ref[:, :, 3 * REST :, :] = jnp.zeros((2, 2, 256 - 3 * REST, 256), BF)
    for j in range(2):
        q = a3_ref[4:20, 8 + 16 * j : 24 + 16 * j, :].reshape(256, 256).astype(BF)
        q2_ref[j] = (mm(q, w2_ref[:, :256]) * SCALE).astype(BF)
        kv = kvs_ref[:, 16 * j : 16 * j + 24, :].reshape(576, 512).astype(BF)
        kv2_ref[j, :, :384] = kv[:KEYS, :384]
        kv2_ref[j, :, 512:640] = kv[:KEYS, 384:]
        kv2_ref[j, :, 384:512] = jnp.ones((KEYS, 128), BF)
        kv2_ref[j, :, 640:] = jnp.ones((KEYS, 128), BF)
        for half in range(2):
            for t in range(3):
                rows = slice(t * REST, t * REST + REST)
                kr_ref[j, half, rows, :] = kv[KEYS:, 128 * half : 128 * half + 128] * masks[t]
                vr_ref[j, half, rows, :128] = kv[KEYS:, 256 + 128 * half : 384 + 128 * half] * masks[t]
                vr_ref[j, half, rows, 128:] = jnp.broadcast_to(masks[t], (REST, 128))
    mixed = jnp.concatenate(cross_attend(2, q2_ref, kv2_ref, kr_ref, vr_ref, b2_ref, br_ref, s2_ref, sr_ref), axis=0)
    own = [bo_ref[4:20, 8 + 16 * j : 24 + 16 * j, :].reshape(256, 256) for j in range(2)]
    res = jnp.concatenate(own, axis=0) + mm(mixed, o2_ref[...])
    out = mlp(res, gain_ref[3:4, :], real, ww2_ref[...], wn2_ref[...])
    for j in range(2):
        part = out[256 * j : 256 * j + 256].reshape(16, 16, 256)
        out_ref[:, 16 * j : 16 * j + 16, :] = part[:, :, :C].astype(BF)


def pairs(axis, first):
    found = []
    for i in range(first, lax.axis_size(axis) - 1, 2):
        found += [(i, i + 1), (i + 1, i)]
    return found


def per_device(
    pixels, shift_prenorm, shift_inputs, shift_table, shift_output, shift_postnorm, shift_widen, shift_narrow,
    cross_prenorm, cross_query, cross_keyval, cross_table, cross_output, cross_postnorm, cross_widen, cross_narrow,
):
    odd = lax.axis_index("rows") % 2 == 1
    ra = lax.ppermute(jnp.where(odd, pixels[:SHIFT], pixels[SHIFT:]), "rows", pairs("rows", 0))
    rb = lax.ppermute(jnp.where(odd, pixels[SHIFT:], pixels[:SHIFT]), "rows", pairs("rows", 1))
    top = jnp.where(odd, ra, rb)
    bot = jnp.where(odd, rb, ra)
    sds = jax.ShapeDtypeStruct
    vmem = pl.BlockSpec(memory_space=pltpu.VMEM)
    hbm = pl.BlockSpec(memory_space=pltpu.HBM)
    firsts = (
        pixels, shift_table,
        shift_prenorm.reshape(1, C), shift_postnorm.reshape(1, C), cross_prenorm.reshape(1, C), cross_postnorm.reshape(1, C),
        shift_inputs, shift_output, shift_widen, shift_narrow.T,
    )
    seconds = (cross_table, cross_query, cross_keyval, cross_output, cross_widen, cross_narrow.T)
    strip = (pixels.shape[0], SHIFT, C)
    like = lambda x: sds(x.shape, x.dtype)
    center, *rest = pl.pallas_call(
        tables_kernel,
        out_shape=(
            like(pixels), *map(like, seconds), sds(strip, BF), sds(strip, BF), sds((8, 256), F32), sds((HEADS, 256, 256), F32),
            sds((256, 768), BF), sds((256, 256), BF), sds((256, 384), BF), sds((256, 384), BF),
        ),
        in_specs=[hbm] * 16,
        out_specs=[vmem] * 15,
        scratch_shapes=[pltpu.VMEM(x.shape, x.dtype) for x in firsts[1:]]
        + [pltpu.SemaphoreType.DMA((16,)), pltpu.VMEM((192, 32), F32), pltpu.VMEM((144, 512), F32)],
        cost_estimate=pl.CostEstimate(flops=100_000_000, bytes_accessed=5_000_000, transcendentals=0),
        compiler_params=pltpu.CompilerParams(vmem_limit_bytes=16 * 2**20),
        name="tables",
    )(*[pltpu.with_memory_space_constraint(x, pltpu.HBM) for x in (*firsts, *seconds)])
    raw, (low, high, gains, b1, w1, o1, ww1, wn1) = rest[:6], rest[6:]

    column_odd = lax.axis_index("cols") % 2 == 1
    pick = lambda rows: jnp.where(column_odd, rows[:, 24:], rows[:, :SHIFT])
    strip = jnp.concatenate([pick(top), jnp.where(column_odd, high, low), pick(bot)], axis=0)
    cb = lax.ppermute(strip, "cols", pairs("cols", 1))
    middle, strip, b2, br, w2, o2, ww2, wn2 = pl.pallas_call(
        middle_kernel,
        out_shape=(
            sds((24, 16, 256), F32), like(strip), sds((HEADS, 256, KEYS), F32), sds((2, 256, 256), F32), sds((256, 768), BF),
            sds((256, 256), BF), sds((256, 384), BF), sds((256, 384), BF),
        ),
        in_specs=[vmem] * 15,
        out_specs=[vmem] * 8,
        scratch_shapes=[
            pltpu.VMEM((2, 16, 16, 256), F32), pltpu.VMEM((2, 192, 256), BF), pltpu.VMEM((2, 256, 768), BF),
            pltpu.VMEM((AHEAD + 1, 192, 256), F32), pltpu.VMEM((240, 40), F32), pltpu.VMEM((144, 1024), F32),
        ],
        cost_estimate=pl.CostEstimate(flops=2_000_000_000, bytes_accessed=8_000_000, transcendentals=1_000_000),
        compiler_params=pltpu.CompilerParams(vmem_limit_bytes=20 * 2**20),
        name="middle",
    )(center, ra, rb, gains, b1, w1, o1, ww1, wn1, *raw)
    ca = lax.ppermute(strip, "cols", pairs("cols", 0))
    return pl.pallas_call(
        main_kernel,
        out_shape=sds(pixels.shape, BF),
        in_specs=[vmem] * 18,
        out_specs=vmem,
        scratch_shapes=[
            pltpu.VMEM((4, 16, 16, 256), F32), pltpu.VMEM((4, 144, 256), BF), pltpu.VMEM((4, 256, 768), BF),
            pltpu.VMEM((AHEAD + 1, 144, 256), F32),
            pltpu.VMEM((24, 48, 256), F32), pltpu.VMEM((24, 48, 256), F32), pltpu.VMEM((24, 40, 512), F32),
            pltpu.VMEM((2, 256, 256), BF), pltpu.VMEM((2, KEYS, 768), BF),
            pltpu.VMEM((2, 2, 256, 128), BF), pltpu.VMEM((2, 2, 256, 256), BF),
            pltpu.VMEM((CROSS_AHEAD + 1, 256, KEYS), F32), pltpu.VMEM((2, 2, 256, 256), F32),
        ],
        cost_estimate=pl.CostEstimate(flops=10_000_000_000, bytes_accessed=8_000_000, transcendentals=4_000_000),
        compiler_params=pltpu.CompilerParams(vmem_limit_bytes=32 * 2**20),
        name="blocks",
    )(center, ra, rb, ca, cb, middle, gains, b1, b2, br, w1, o1, ww1, wn1, w2, o2, ww2, wn2)


def solution(mesh):
    return jax.shard_map(
        per_device,
        mesh=mesh,
        in_specs=(P("rows", "cols", None),) + (P(),) * 15,
        out_specs=P("rows", "cols", None),
        check_vma=False,
    )
```
